128 devices in a mesh: tiles: 32 (over x, y, z_lo), chan: 4 (over z_hi, core).
Axes of the slice: x: 4, y: 4, z: 4 (z_hi: 2, z_lo: 2; z = z_hi * 2 + z_lo), core: 2. Of those that a mesh axis runs over, the one named last changes fastest.
Arguments:
- latents: bfloat16 [2560, 64, 384], P('tiles', 'chan'), may hold values from -6 to 6
- owner: int32 [1024], replicated, may hold values from 0 to 31, as said below
- neighbours: int32 [2560, 8], P('tiles'), may hold values from 0 to 112, as said below
- rotations: int32 [2560, 8], P('tiles'), may hold values from 0 to 3, as said below
- cell_mask: int32 [2560, 64], P('tiles', 'chan'), may hold values 0 or 1
- gain_image: float32 [384], replicated, may hold values from 0.1 to 1.9
- conv_weight: bfloat16 [3456, 384], replicated, may hold values from -0.109375 to 0.109375
- gain_attn: float32 [384], replicated, may hold values from 0.1 to 1.9
- qkv_weight: bfloat16 [384, 1152], replicated
- out_weight: bfloat16 [384, 384], replicated, may hold values from -0.3125 to 0.3125
- gain_mlp: float32 [384], replicated, may hold values from 0.1 to 1.9
- up_weight: bfloat16 [384, 1536], replicated, may hold values from -0.3125 to 0.3125
- down_weight: bfloat16 [1536, 384], replicated, may hold values from -0.15625 to 0.15625
Outputs:
- encoded: bfloat16 [2560, 64, 384], P('tiles', 'chan')
The draws below stay inside these ranges and needn't reach their ends.
Inputs may be any that keep to these rules, and one draw needn't show every extreme that they name: `owner`: tile index = band column * 16 + band row over 64 band columns that close into a loop; band columns 32 and above are turned a quarter against the others. Each device of tiles owns a contiguous run of whole band columns, the runs following device order from column 0; a device owns 1 to 5 columns, each aligned group of four devices owns 4 * 2 columns, and in every draw some device owns 4 * 2 - 3 columns. `neighbours`: entries as in the reference program, in the slot's own frame. Every neighbour of a filled slot is a tile of the same device, of the last column of the previous device or of the first column of the next device (cyclically); the value 80 + 2 * 16 marks a neighbour beyond the band's upper or lower edge, and fills every row of an empty slot. `rotations`: zero for empty slots and missing neighbours.
All inputs are finite; a program needn't handle non-finite values. No bound on the sum of `cell_mask` on one device may be relied on, other than what follows from the above.
Results may differ from the reference program's by a relative error of at most 0.008.
Values may be sent and summed in bfloat16 or wider, within the bound.
A program may use at most 128 MiB of HBM per device.

```python
import math
import jax
import jax.numpy as jnp
from jax import lax

D = 384
HEADS = 6
HEAD_DIM = 64
FFN_UNITS = 1536
SIDE = 8
FACE = 16
COLS_MEAN = 2
SLOTS = 80
TILES_ALL = 1024
SLOT_ALL = 2560
CELLS = 64
N_TILES = 32


STEPS = ((-1, -1), (-1, 0), (-1, 1), (0, -1), (0, 1), (1, -1), (1, 0), (1, 1))


def column_counts(key):
    groups = N_TILES // 4
    per_group = 4 * COLS_MEAN
    group_keys = jax.random.split(jax.random.fold_in(key, 11), groups)

    def cut_points(group_key):
        shuffled = jax.random.permutation(group_key, per_group - 1)
        return jnp.sort(shuffled[:3] + 1).astype(jnp.int32)
    cut_marks = jax.vmap(cut_points)(group_keys)
    chosen = jax.random.randint(jax.random.fold_in(key, 12), (), 0, groups)
    flipped = jax.random.randint(jax.random.fold_in(key, 13), (), 0, 2)
    low_marks = jnp.array([1, 2, 3], jnp.int32)
    high_marks = per_group - jnp.array([3, 2, 1], jnp.int32)
    forced = jnp.where(flipped == 1, high_marks, low_marks)
    cut_marks = jnp.where((jnp.arange(groups) == chosen)[:, None], forced[None, :], cut_marks)
    bounds = jnp.concatenate([jnp.zeros((groups, 1), jnp.int32), cut_marks, jnp.full((groups, 1), per_group, jnp.int32)], axis=1)
    return (bounds[:, 1:] - bounds[:, :-1]).reshape(-1).astype(jnp.int32)


def layout(key):
    counts = column_counts(key)
    starts = (jnp.cumsum(counts) - counts).astype(jnp.int32)
    column_ids = jnp.arange(4 * FACE, dtype=jnp.int32)
    column_owner = jnp.sum((column_ids[:, None] >= starts[None, 1:]).astype(jnp.int32), axis=1)
    return (counts, starts, column_owner)


def slot_tables(key):
    counts, starts, column_owner = layout(jax.random.fold_in(key, 5))
    band_columns = 4 * FACE
    device = jnp.arange(N_TILES, dtype=jnp.int32)[:, None]
    slot_rank = jnp.arange(SLOTS, dtype=jnp.int32)[None, :]
    filled = slot_rank < counts[:, None] * FACE
    tile_index = starts[:, None] * FACE + slot_rank
    column = jnp.minimum(tile_index // FACE, band_columns - 1)
    band_row = tile_index % FACE
    turned = (column >= 2 * FACE).astype(jnp.int32)
    previous = (device - 1) % N_TILES
    entries = []
    turn_list = []
    for row_step, col_step in STEPS:
        geo_row = jnp.where(turned == 1, col_step, row_step)
        geo_col = jnp.where(turned == 1, -row_step, col_step)
        near_row = band_row + geo_row
        near_col = (column + geo_col) % band_columns
        inside = filled & (near_row >= 0) & (near_row < FACE)
        near_owner = column_owner[near_col]
        near_slot = (near_col - starts[near_owner]) * FACE + near_row
        local_entry = jnp.where(near_owner == device, near_slot, jnp.where(near_owner == previous, SLOTS + near_slot - (counts[near_owner] - 1) * FACE, SLOTS + FACE + near_slot))
        entries.append(jnp.where(inside, local_entry, SLOTS + 2 * FACE).astype(jnp.int32))
        near_turned = (near_col >= 2 * FACE).astype(jnp.int32)
        turn_list.append(jnp.where(inside, (turned - near_turned) % 4, 0).astype(jnp.int32))
    return (jnp.stack(entries, axis=-1).reshape(SLOT_ALL, 8), jnp.stack(turn_list, axis=-1).reshape(SLOT_ALL, 8))


def draw_owner(key, part):
    counts, starts, column_owner = layout(jax.random.fold_in(key, 5))
    return jnp.repeat(column_owner, FACE).astype(jnp.int32)


def draw_neighbours(key, part):
    return slot_tables(key)[0]


def draw_rotations(key, part):
    return slot_tables(key)[1]


def draw_qkv_weight(key, part):
    base = jax.random.normal(key, (D, 3 * D), jnp.float32) * D ** (-0.5)
    return base.astype(jnp.bfloat16)


def plant(values, rng, low, high):
    dims = values.shape
    index_at = [jax.random.randint(jax.random.fold_in(rng, axis), (), 0, dims[axis]) for axis in range(len(dims))]
    values = values.at[tuple(index_at)].set(low)
    longest = dims.index(max(dims))
    index_at[longest] = (index_at[longest] + 1) % dims[longest]
    return values.at[tuple(index_at)].set(high)


def shard_levels(own_key, extent, cuts, smallest, largest):
    level = 1.0
    for axis_at, blocks in cuts:
        draws = jax.random.uniform(jax.random.fold_in(jax.random.fold_in(own_key, 6), axis_at), (blocks,), jnp.float32, smallest / len(cuts), largest / len(cuts))
        level = level * jnp.repeat(jnp.exp(draws), extent[axis_at] // blocks).reshape((-1,) + (1,) * (len(extent) - 1 - axis_at))
    return level


def gaussian(stream_key, extent, spread, reach, cuts=(), kind=jnp.bfloat16):
    level = shard_levels(stream_key, extent, cuts, -0.22, 0.18) if cuts else 1.0
    values = jax.random.normal(stream_key, extent, jnp.float32) * spread * level
    return jnp.minimum(jnp.maximum(values, -reach), reach).astype(kind)


def setup_inputs(seed: int = 0) -> dict:
    key_of = jax.random.split(jax.random.key(seed), 14)
    return {
        "latents": gaussian(key_of[0], (SLOT_ALL, CELLS, D), 1.0, 6.0, ((0, 32), (1, 4))),
        "owner": draw_owner(jax.random.fold_in(key_of[13], 71), 0),
        "neighbours": draw_neighbours(jax.random.fold_in(key_of[13], 71), 0),
        "rotations": draw_rotations(jax.random.fold_in(key_of[13], 71), 0),
        "cell_mask": plant((jax.random.randint(key_of[4], (SLOT_ALL, CELLS), 0, 4) < 3).astype(jnp.int32), jax.random.fold_in(key_of[4], 1), 0, 1),
        "gain_image": jnp.clip(1.0 + 0.18 * jax.random.normal(key_of[5], (D,), jnp.float32), 0.1, 1.9),
        "conv_weight": gaussian(key_of[6], (9 * D, D), (9 * D) ** -0.5, 0.109375),
        "gain_attn": jnp.clip(1.0 + 0.18 * jax.random.normal(key_of[7], (D,), jnp.float32), 0.1, 1.9),
        "qkv_weight": draw_qkv_weight(jax.random.fold_in(key_of[13], 71), 0),
        "out_weight": gaussian(key_of[9], (D, D), D ** -0.5, 0.3125),
        "gain_mlp": jnp.clip(1.0 + 0.18 * jax.random.normal(key_of[10], (D,), jnp.float32), 0.1, 1.9),
        "up_weight": gaussian(key_of[11], (D, FFN_UNITS), D ** -0.5, 0.3125),
        "down_weight": gaussian(key_of[12], (FFN_UNITS, D), FFN_UNITS ** -0.5, 0.15625),
    }


epsilon = 1e-06
PICKS = ((2, 2), (2, 1), (2, 0), (1, 2), (1, 0), (0, 2), (0, 1), (0, 0))

def part_slice(which_part):
    if which_part == 0:
        return slice(0, 1)
    if which_part == 2:
        return slice(-1, None)
    return slice(None)

def rms_scaled(values, gain):
    wide = values.astype(jnp.float32)
    return wide * lax.rsqrt(lax.optimization_barrier(jnp.mean(wide * wide, axis=-1, keepdims=True)) + epsilon) * gain

def turned_part(tile_data, turn_code, row_part, col_part):
    picked = tile_data[:, row_part, col_part]
    for quarter in (1, 2, 3):
        rotated = jnp.rot90(tile_data, quarter, axes=(1, 2))[:, row_part, col_part]
        picked = jnp.where((turn_code == quarter)[:, None, None, None], rotated, picked)
    return picked

def framed(own_tiles, near_tiles, turn_codes):
    pieces = []
    for position in range(8):
        row_kind, col_kind = PICKS[position]
        pieces.append(turned_part(near_tiles[:, position], turn_codes[:, position], part_slice(row_kind), part_slice(col_kind)))
    upper = jnp.concatenate([pieces[0], pieces[1], pieces[2]], axis=2)
    middle = jnp.concatenate([pieces[3], own_tiles, pieces[4]], axis=2)
    lower = jnp.concatenate([pieces[5], pieces[6], pieces[7]], axis=2)
    return jnp.concatenate([upper, middle, lower], axis=1)

def stencil(padded, out_rows, conv_weight):
    tile_side = padded.shape[2] - 2
    windows = []
    for row_step in (-1, 0, 1):
        for col_step in (-1, 0, 1):
            windows.append(padded[:, 1 + row_step:1 + row_step + out_rows, 1 + col_step:1 + col_step + tile_side])
    patches = jnp.concatenate(windows, axis=-1)
    flat = patches.reshape(-1, patches.shape[-1])
    return jnp.dot(flat, conv_weight, preferred_element_type=jnp.float32)

def attend(queries, memory, heads):
    batch, rows_in, model_width = queries.shape
    head_size = model_width // heads
    keys = memory[..., :model_width].reshape(batch, -1, heads, head_size).astype(jnp.float32)
    values = memory[..., model_width:].reshape(batch, -1, heads, head_size).astype(jnp.float32)
    grouped = queries.reshape(batch, rows_in, heads, head_size).astype(jnp.float32)
    scores = jnp.einsum('bqhe,bkhe->bhqk', grouped, keys)
    highest = lax.optimization_barrier(jnp.max(scores, axis=-1, keepdims=True))
    weights = jnp.exp(scores - highest)
    probs = (weights / lax.optimization_barrier(jnp.sum(weights, axis=-1, keepdims=True))).astype(jnp.bfloat16)
    mixed = jnp.einsum('bhqk,bkhe->bqhe', probs.astype(jnp.float32), values)
    return mixed.astype(jnp.bfloat16).reshape(batch, rows_in, model_width)

def reference(latents, owner, neighbours, rotations, cell_mask, gain_image, conv_weight, gain_attn, qkv_weight, out_weight, gain_mlp, up_weight, down_weight):
    devices = jnp.arange(N_TILES, dtype=jnp.int32)
    counts = lax.optimization_barrier(jnp.sum((owner[None, :] == devices[:, None]).astype(jnp.int32), axis=1))
    starts = jnp.cumsum(counts) - counts
    tile_ids = jnp.arange(TILES_ALL, dtype=jnp.int32)
    slot_of_tile = (owner * SLOTS + tile_ids - starts[owner]).astype(jnp.int32)
    near_local = neighbours[slot_of_tile]
    near_turns = rotations[slot_of_tile]
    previous = (owner - 1) % N_TILES
    following = (owner + 1) % N_TILES
    own_start = starts[owner][:, None]
    prev_base = (starts[previous] + counts[previous] - FACE)[:, None]
    next_base = starts[following][:, None]
    near_tile = jnp.where(near_local < SLOTS, own_start + near_local, jnp.where(near_local < SLOTS + FACE, prev_base + near_local - SLOTS, jnp.where(near_local < SLOTS + 2 * FACE, next_base + near_local - SLOTS - FACE, TILES_ALL)))
    near_tile = near_tile.astype(jnp.int32)
    tile_latents = latents[slot_of_tile]
    tile_mask = cell_mask[slot_of_tile].astype(jnp.float32)[..., None]
    normed = (rms_scaled(tile_latents, gain_image) * tile_mask).astype(jnp.bfloat16)
    blank = jnp.zeros((1, CELLS, D), jnp.bfloat16)
    image_grid = jnp.concatenate([normed, blank], axis=0).reshape(TILES_ALL + 1, SIDE, SIDE, D)
    block_count = TILES_ALL // FACE

    def image_block(block_index):
        first_tile = (block_index * FACE).astype(jnp.int32)
        own_tiles = lax.dynamic_slice_in_dim(image_grid, first_tile, FACE, 0)
        near_index = lax.dynamic_slice_in_dim(near_tile, first_tile, FACE, 0)
        turn_block = lax.dynamic_slice_in_dim(near_turns, first_tile, FACE, 0)
        padded = framed(own_tiles, image_grid[near_index], turn_block)
        return stencil(padded, SIDE, conv_weight).reshape(FACE, CELLS, D)
    stencil_out = lax.map(image_block, jnp.arange(block_count, dtype=jnp.int32)).reshape(TILES_ALL, CELLS, D)
    after_image = (tile_latents.astype(jnp.float32) + stencil_out).astype(jnp.bfloat16)
    attn_input = (rms_scaled(after_image, gain_attn) * tile_mask).astype(jnp.bfloat16)
    projected = jnp.dot(attn_input.reshape(-1, D), qkv_weight, preferred_element_type=jnp.float32)
    score_scale = 1.0 / math.sqrt(HEAD_DIM)
    queries = (projected[:, :D] * score_scale).astype(jnp.bfloat16).reshape(TILES_ALL, CELLS, D)
    memory = projected[:, D:].astype(jnp.bfloat16).reshape(TILES_ALL, CELLS, 2 * D)
    memory_table = jnp.concatenate([memory, jnp.zeros((1, CELLS, 2 * D), jnp.bfloat16)], axis=0)
    gather_ids = jnp.concatenate([tile_ids[:, None], near_tile], axis=1)

    def attend_block(block_index):
        first_tile = (block_index * FACE).astype(jnp.int32)
        tile_index = lax.dynamic_slice_in_dim(gather_ids, first_tile, FACE, 0)
        block_memory = memory_table[tile_index].reshape(FACE, 9 * CELLS, 2 * D)
        block_queries = lax.dynamic_slice_in_dim(queries, first_tile, FACE, 0)
        return attend(block_queries, block_memory, HEADS)
    mixed = lax.map(attend_block, jnp.arange(block_count, dtype=jnp.int32)).reshape(TILES_ALL, CELLS, D)
    after_attn = (after_image.astype(jnp.float32) + jnp.dot(mixed, out_weight, preferred_element_type=jnp.float32)).astype(jnp.bfloat16)
    mlp_input = rms_scaled(after_attn, gain_mlp).astype(jnp.bfloat16)
    hidden = jax.nn.gelu(jnp.dot(mlp_input, up_weight, preferred_element_type=jnp.float32), approximate=False).astype(jnp.bfloat16)
    tile_out = (after_attn.astype(jnp.float32) + jnp.dot(hidden, down_weight, preferred_element_type=jnp.float32)).astype(jnp.bfloat16)
    slot_ids = jnp.arange(SLOT_ALL, dtype=jnp.int32)
    slot_device = slot_ids // SLOTS
    slot_rank = slot_ids % SLOTS
    slot_filled = slot_rank < counts[slot_device]
    slot_tile = jnp.minimum(starts[slot_device] + slot_rank, TILES_ALL - 1).astype(jnp.int32)
    encoded = jnp.where(slot_filled[:, None, None], tile_out[slot_tile], jnp.zeros_like(tile_out[slot_tile]))
    return encoded.astype(jnp.bfloat16)
```

```python
import functools
import math

import jax
import jax.numpy as jnp
import numpy as np
from jax import lax
from jax.experimental import pallas as pl
from jax.experimental.pallas import tpu as pltpu
from jax.sharding import PartitionSpec as P

MESH = pl.DeviceIdType.MESH
ANY = pl.BlockSpec(memory_space=pl.ANY)
VMEM = pl.BlockSpec(memory_space=pltpu.VMEM)
F32, BF16 = jnp.float32, jnp.bfloat16

D = 384
HEAD_DIM = 64
FACE = 16
SIDE = 8
CELLS = 64
SLOTS = 80
HELD = 5
GROUP = 4
CHAN = 4
COLS = 2
ROWS = 4
OWN = COLS * ROWS
GRID_R, GRID_C = ROWS + 2, COLS + 2
SPOTS = GRID_R * GRID_C
RIM = 32
PIECE = ROWS * 3 + 1
epsilon = 1e-06


def rim_recipe():
    rows = [(1, 7, i) for i in range(8)] + [(6, 0, i) for i in range(8)]
    rows += [(3, i, 7) for i in range(8)] + [(4, i, 0) for i in range(8)]
    rows += [(0, 7, 7), (2, 7, 0), (5, 0, 7), (7, 0, 0)]
    return rows


def rms(wide, gain):
    return wide * lax.rsqrt(jnp.mean(wide * wide, axis=-1, keepdims=True) + epsilon) * gain


def tables(owner, neighbours, rotations, cell_mask, device):
    count = jnp.sum((owner == device).astype(jnp.int32))
    start = jnp.sum((owner < device).astype(jnp.int32))
    slot = jnp.arange(SLOTS, dtype=jnp.int32)[:, None]
    entry = neighbours
    base = jnp.where(
        entry < SLOTS,
        start,
        jnp.where(entry < SLOTS + FACE, start - FACE - SLOTS, start + count - SLOTS - FACE),
    )
    tile = (base + entry + owner.shape[0]) % owner.shape[0]
    band = owner.shape[0] // FACE
    own_col = start // FACE + slot // FACE
    grid_row = tile % FACE - (slot % FACE) // ROWS * ROWS + 1
    grid_col = (tile // FACE - own_col // COLS * COLS + 1 + band) % band
    place = jnp.clip(grid_col, 0, GRID_C - 1) * GRID_R + jnp.clip(grid_row, 0, GRID_R - 1)
    place = jnp.where(entry < SLOTS + 2 * FACE, place, SPOTS)
    recipe = rim_recipe()
    fill = 48 - len(recipe)

    def spread(values, pad):
        parts = []
        for at in (1, 6, 3, 4):
            parts.append(jnp.broadcast_to(values[:, at : at + 1], (SLOTS, 8)))
        for at in (0, 2, 5, 7):
            parts.append(values[:, at : at + 1])
        parts.append(jnp.full((SLOTS, fill), pad, jnp.int32))
        return jnp.concatenate(parts, axis=1)

    turn = spread(rotations, 0)
    rim_place = spread(place, SPOTS)
    row = jnp.asarray([r[1] for r in recipe] + [0] * fill, jnp.int32)[None]
    col = jnp.asarray([r[2] for r in recipe] + [0] * fill, jnp.int32)[None]
    from_row = jnp.where(turn == 0, row, jnp.where(turn == 1, col, jnp.where(turn == 2, 7 - row, 7 - col)))
    from_col = jnp.where(turn == 0, col, jnp.where(turn == 1, 7 - row, jnp.where(turn == 2, 7 - col, row)))
    rim_row = jnp.where(
        from_row == 0,
        from_col,
        jnp.where(from_row == 7, 8 + from_col, jnp.where(from_col == 0, 16 + from_row, 24 + from_row)),
    )
    near = jnp.concatenate([place, jnp.zeros((SLOTS, 8), jnp.int32)], axis=1)
    fields = jnp.concatenate([cell_mask, rim_place, rim_row, near], axis=1).astype(BF16)
    fields = fields.reshape(HELD, CHAN, ROWS, 8, 16).transpose(0, 1, 4, 2, 3)
    fields = fields.reshape(HELD, CHAN, 16, ROWS * 8)
    fields = jnp.pad(fields, ((0, 0), (0, 0), (0, 0), (0, 128 - ROWS * 8)))
    return fields, start, count


def pack_kernel(shift, latents, fields, out):
    for c in range(CHAN):
        for r in range(ROWS):
            for part in range(3):
                out[0, c, r * 3 + part] = latents[0, c * ROWS + r, :, part * 128 : (part + 1) * 128]
        out[0, c, PIECE - 1] = fields[0, c]


def pack(shift, latents, fields):
    def place(i, shift):
        return lax.rem(i + HELD - shift[0], HELD)

    return pl.pallas_call(
        pack_kernel,
        out_shape=jax.ShapeDtypeStruct((HELD, CHAN, PIECE, 16, 128), BF16),
        grid_spec=pltpu.PrefetchScalarGridSpec(
            num_scalar_prefetch=1,
            grid=(HELD,),
            in_specs=[
                pl.BlockSpec((1, FACE, 16, D), lambda i, s: (place(i, s), 0, 0, 0)),
                pl.BlockSpec((1, CHAN, 16, 128), lambda i, s: (place(i, s), 0, 0, 0)),
            ],
            out_specs=pl.BlockSpec((1, CHAN, PIECE, 16, 128), lambda i, s: (i, 0, 0, 0, 0)),
        ),
        name="pack",
    )(shift, latents.reshape(HELD, FACE, 16, D), fields)


def greet(partners):
    barrier = pltpu.get_barrier_semaphore()
    for partner in partners:
        pl.semaphore_signal(barrier, inc=1, device_id=partner, device_id_type=MESH)
    pl.semaphore_wait(barrier, len(partners))


def group_partners(base, rank, chan):
    partners = []
    for step in range(1, GROUP * CHAN):
        other = lax.rem(rank * CHAN + chan + step, GROUP * CHAN)
        partners.append((base + other // CHAN, lax.rem(other, CHAN)))
    return partners


def remote(src, dst, send, recv, device):
    return pltpu.make_async_remote_copy(
        src_ref=src, dst_ref=dst, send_sem=send, recv_sem=recv, device_id=device, device_id_type=MESH
    )


def spread_kernel(payload, got, send, recv, local):
    device, chan = lax.axis_index("tiles"), lax.axis_index("chan")
    rank = lax.rem(device, GROUP)
    base = device - rank
    greet(group_partners(base, rank, chan))
    started = []
    for step in range(3):
        i = lax.rem(rank + 2 + step, HELD)
        col = rank + i
        for c in range(CHAN):
            at = lax.rem(chan + c, CHAN)
            copy = remote(
                payload.at[i, at],
                got.at[rank, chan, lax.rem(col, 2)],
                send.at[len(started)],
                recv.at[(rank * CHAN + chan) * COLS + lax.rem(col, 2)],
                (base + col // 2, at),
            )
            copy.start()
            started.append(copy)
    for col in range(COLS):
        i = rank + col
        for c in range(1, CHAN):
            at = lax.rem(chan + c, CHAN)
            copy = remote(
                payload.at[i, at],
                got.at[rank, chan, col],
                send.at[len(started)],
                recv.at[(rank * CHAN + chan) * COLS + col],
                (device, at),
            )
            copy.start()
            started.append(copy)
    stays = []
    for col in range(COLS):
        copy = pltpu.make_async_copy(payload.at[rank + col, chan], got.at[rank, chan, col], local.at[col])
        copy.start()
        stays.append(copy)
    for step in range(GROUP):
        source = lax.rem(rank + step, GROUP)
        for c in range(1 if step == 0 else 0, CHAN):
            at = lax.rem(chan + c, CHAN)
            for col in range(COLS):
                far = rank * COLS + col - source
                arrival = remote(
                    payload.at[0, 0],
                    got.at[source, at, col],
                    send.at[0],
                    recv.at[(source * CHAN + at) * COLS + col],
                    (device, at),
                )

                @pl.when((far >= 0) & (far < HELD))
                def _():
                    arrival.wait_recv()

    for copy in started:
        copy.wait_send()
    for copy in stays:
        copy.wait()


def spread_out(payload):
    return pl.pallas_call(
        spread_kernel,
        out_shape=jax.ShapeDtypeStruct((GROUP, CHAN, COLS, PIECE, 16, 128), BF16),
        in_specs=[ANY],
        out_specs=ANY,
        scratch_shapes=[
            pltpu.SemaphoreType.DMA((18,)),
            pltpu.SemaphoreType.DMA((GROUP * CHAN * COLS,)),
            pltpu.SemaphoreType.DMA((COLS,)),
        ],
        compiler_params=pltpu.CompilerParams(collective_id=0, has_side_effects=True),
        name="spread_out",
    )(payload)


def image_kernel(source, got, gain, latents, normed, rims, fields, held, sem):
    copies = []
    for col in range(COLS):
        for c in range(CHAN):
            copy = pltpu.make_async_copy(
                got.at[source[col], c, col], held.at[col, c], sem.at[col * CHAN + c]
            )
            copy.start()
            copies.append(copy)
    for copy in copies:
        copy.wait()
    row = lax.broadcasted_iota(jnp.int32, (RIM, CELLS), 0)
    cell = lax.broadcasted_iota(jnp.int32, (RIM, CELLS), 1)
    edge, along = row // 8, row % 8
    wanted = jnp.where(
        edge == 0, along, jnp.where(edge == 1, 56 + along, jnp.where(edge == 2, along * 8, along * 8 + 7))
    )
    chosen = jnp.where(cell == wanted, 1.0, 0.0).astype(BF16)
    for col in range(COLS):
        for c in range(CHAN):
            fields[col, c] = held[col, c, PIECE - 1]
        for r in range(ROWS):
            tile = col * ROWS + r
            pieces, masks = [], []
            for c in range(CHAN):
                pieces.append(jnp.concatenate([held[col, c, r * 3 + part] for part in range(3)], axis=1))
                masks.append(held[col, c, PIECE - 1][:, r * 8 : r * 8 + 1].astype(F32))
            values = jnp.concatenate(pieces, axis=0)
            mask = jnp.concatenate(masks, axis=0)
            latents[tile] = values
            norm = (rms(values.astype(F32), gain[...]) * mask).astype(BF16)
            normed[tile] = norm
            rims[tile] = jnp.dot(chosen, norm, preferred_element_type=F32).astype(BF16)


def image(source, got, gain):
    tiles = jax.ShapeDtypeStruct((OWN, CELLS, D), BF16)
    return pl.pallas_call(
        image_kernel,
        out_shape=(
            tiles,
            tiles,
            jax.ShapeDtypeStruct((OWN, RIM, D), BF16),
            jax.ShapeDtypeStruct((COLS, CHAN, 16, 128), BF16),
        ),
        grid_spec=pltpu.PrefetchScalarGridSpec(
            num_scalar_prefetch=1,
            grid=(),
            in_specs=[ANY, VMEM],
            out_specs=(VMEM, VMEM, VMEM, VMEM),
            scratch_shapes=[
                pltpu.VMEM((COLS, CHAN, PIECE, 16, 128), BF16),
                pltpu.SemaphoreType.DMA((COLS * CHAN,)),
            ],
        ),
        name="image_norm",
    )(source, got, gain)


def halo_kernel(tiles, out, send, recv, local):
    device, chan = lax.axis_index("tiles"), lax.axis_index("chan")
    total = lax.axis_size("tiles")
    left, right = lax.rem(device + total - 1, total), lax.rem(device + 1, total)
    above, below = lax.rem(chan + CHAN - 1, CHAN), lax.rem(chan + 1, CHAN)
    greet(
        [
            (left, chan),
            (right, chan),
            (device, above),
            (device, below),
            (left, above),
            (left, below),
            (right, above),
            (right, below),
        ]
    )
    last = ROWS - 1
    moves = [
        (0, 3 * GRID_R + 1, ROWS, (left, chan)),
        (ROWS, 1, ROWS, (right, chan)),
        (0, 3 * GRID_R + 5, 1, (left, above)),
        (last, 3 * GRID_R, 1, (left, below)),
        (ROWS, 5, 1, (right, above)),
        (ROWS + last, 0, 1, (right, below)),
    ]
    for col in range(COLS):
        moves.append((col * ROWS, (1 + col) * GRID_R + 5, 1, (device, above)))
        moves.append((col * ROWS + last, (1 + col) * GRID_R, 1, (device, below)))
    copies = []
    for at, (src, dst, many, where) in enumerate(moves):
        copy = remote(tiles.at[pl.ds(src, many)], out.at[pl.ds(dst, many)], send.at[at], recv.at[at], where)
        copy.start()
        copies.append(copy)
    stays = []
    for col in range(COLS):
        copy = pltpu.make_async_copy(
            tiles.at[pl.ds(col * ROWS, ROWS)],
            out.at[pl.ds((1 + col) * GRID_R + 1, ROWS)],
            local.at[col],
        )
        copy.start()
        stays.append(copy)
    for copy in copies:
        copy.wait()
    for copy in stays:
        copy.wait()


def halo(tiles, collective_id):
    moves = 6 + 2 * COLS
    return pl.pallas_call(
        halo_kernel,
        out_shape=jax.ShapeDtypeStruct((SPOTS,) + tiles.shape[1:], BF16),
        in_specs=[ANY],
        out_specs=ANY,
        scratch_shapes=[
            pltpu.SemaphoreType.DMA((moves,)),
            pltpu.SemaphoreType.DMA((moves,)),
            pltpu.SemaphoreType.DMA((COLS,)),
        ],
        compiler_params=pltpu.CompilerParams(collective_id=collective_id, has_side_effects=True),
        name="halo",
    )(tiles)


def stencil_kernel(around, latents, normed, fields, weight, gain, after, attn, frame, patches):
    lane = lax.broadcasted_iota(jnp.int32, (48, SPOTS * RIM), 1).astype(F32)
    rim_table = around[...]
    for tile in range(OWN):
        col, r = tile // ROWS, tile % ROWS
        marks = fields[col, 0].astype(F32)
        wanted = jnp.concatenate(
            [
                marks[:, r * 8 + 1 + k : r * 8 + 2 + k] * RIM + marks[:, r * 8 + 4 + k : r * 8 + 5 + k]
                for k in range(3)
            ],
            axis=0,
        )
        chosen = jnp.where(lane == wanted, 1.0, 0.0).astype(BF16)
        rim = jnp.dot(chosen, rim_table, preferred_element_type=F32)
        frame[tile, 1:9, 8:16, :] = normed[tile].astype(F32).reshape(SIDE, SIDE, D)
        frame[tile, 0, 8:16, :] = rim[0:8]
        frame[tile, 9, 8:16, :] = rim[8:16]
        for i in range(SIDE):
            frame[tile, 1 + i, 7:8, :] = rim[16 + i : 17 + i]
            frame[tile, 1 + i, 16:17, :] = rim[24 + i : 25 + i]
        frame[tile, 0, 7:8, :] = rim[32:33]
        frame[tile, 0, 16:17, :] = rim[33:34]
        frame[tile, 9, 7:8, :] = rim[34:35]
        frame[tile, 9, 16:17, :] = rim[35:36]
        for tap in range(9):
            dr, dc = tap // 3, tap % 3
            window = frame[tile, dr : dr + SIDE, 7 + dc : 7 + dc + SIDE, :]
            patches[tile * CELLS : (tile + 1) * CELLS, tap * D : (tap + 1) * D] = window.reshape(
                CELLS, D
            ).astype(BF16)

    def block(at, _):
        rows = pl.ds(pl.multiple_of(at * 256, 256), 256)
        total = jnp.dot(patches[rows, :], weight[...], preferred_element_type=F32)
        image = (latents[rows, :].astype(F32) + total).astype(BF16)
        after[rows, :] = image
        attn[rows, :] = rms(image.astype(F32), gain[...]).astype(BF16)
        return 0

    lax.fori_loop(0, OWN * CELLS // 256, block, 0)
    for tile in range(OWN):
        col, r = tile // ROWS, tile % ROWS
        mask = jnp.concatenate([fields[col, c][:, r * 8 : r * 8 + 1] for c in range(CHAN)], axis=0)
        rows = slice(tile * CELLS, (tile + 1) * CELLS)
        attn[rows, :] = (attn[rows, :].astype(F32) * mask.astype(F32)).astype(BF16)


def stencil(around, latents, normed, fields, weight, gain):
    flat = jax.ShapeDtypeStruct((OWN * CELLS, D), BF16)
    return pl.pallas_call(
        stencil_kernel,
        out_shape=(flat, flat),
        in_specs=[VMEM] * 6,
        out_specs=(VMEM, VMEM),
        scratch_shapes=[
            pltpu.VMEM((OWN, 10, 24, D), F32),
            pltpu.VMEM((OWN * CELLS, 9 * D), BF16),
        ],
        compiler_params=pltpu.CompilerParams(vmem_limit_bytes=40 << 20),
        name="stencil",
    )(around.reshape(SPOTS * RIM, D), latents.reshape(OWN * CELLS, D), normed, fields, weight, gain)


def attend_kernel(
    near, around, after, qkv, out_weight, gain, up, down, out, memory, queries, keys, mixed
):
    def project(at, _):
        rows = pl.ds(pl.multiple_of(at * 256, 256), 256)
        memory[rows, :] = jnp.dot(around[rows, :], qkv[:, D:], preferred_element_type=F32).astype(BF16)
        return 0

    lax.fori_loop(0, SPOTS * CELLS // 256, project, 0)
    memory[SPOTS * CELLS :, :] = jnp.zeros((CELLS, 2 * D), BF16)
    scale = 1.0 / math.sqrt(HEAD_DIM)
    for col in range(COLS):
        first = ((1 + col) * GRID_R + 1) * CELLS
        rows = slice(col * ROWS * CELLS, (col + 1) * ROWS * CELLS)
        projected = jnp.dot(around[first : first + ROWS * CELLS, :], qkv[:, :D], preferred_element_type=F32)
        queries[rows, :] = (projected * scale).astype(BF16)
    low = lax.broadcasted_iota(jnp.int32, (CELLS, 128), 1) < HEAD_DIM

    def tile_step(tile, _):
        own = (1 + tile // ROWS) * GRID_R + 1 + tile % ROWS
        for n in range(9):
            place = own if n == 8 else near[tile * 8 + n]
            keys[n * CELLS : (n + 1) * CELLS, :] = memory[pl.ds(pl.multiple_of(place * CELLS, CELLS), CELLS), :]
        rows = pl.ds(pl.multiple_of(tile * CELLS, CELLS), CELLS)
        for pair in range(3):
            lanes = slice(pair * 128, (pair + 1) * 128)
            query = queries[rows, lanes]
            nothing = jnp.zeros_like(query)
            both = jnp.concatenate([jnp.where(low, query, nothing), jnp.where(low, nothing, query)], axis=0)
            scores = lax.dot_general(
                both, keys[:, lanes], (((1,), (1,)), ((), ())), preferred_element_type=F32
            )
            weights = jnp.exp(scores - jnp.max(scores, axis=-1, keepdims=True))
            total = jnp.sum(weights, axis=-1, keepdims=True)
            value = jnp.dot(
                weights.astype(BF16), keys[:, D + pair * 128 : D + (pair + 1) * 128], preferred_element_type=F32
            )
            value = value / total
            mixed[rows, lanes] = jnp.where(low, value[:CELLS], value[CELLS:]).astype(BF16)
        return 0

    lax.fori_loop(0, OWN, tile_step, 0)

    def finish(at, _):
        rows = pl.ds(pl.multiple_of(at * 256, 256), 256)
        attended = jnp.dot(mixed[rows, :], out_weight[...], preferred_element_type=F32)
        attended = (after[rows, :].astype(F32) + attended).astype(BF16)
        wide = attended.astype(F32)
        hidden = jnp.dot(rms(wide, gain[...]).astype(BF16), up[...], preferred_element_type=F32)
        hidden = (0.5 * hidden * (1.0 + lax.erf(hidden * (0.5**0.5)))).astype(BF16)
        encoded = wide + jnp.dot(hidden, down[...], preferred_element_type=F32)
        encoded = encoded.astype(BF16).reshape(ROWS, CHAN, 16, D)
        for r in range(ROWS):
            for c in range(CHAN):
                out[at, c, r] = encoded[r, c]
        return 0

    lax.fori_loop(0, COLS, finish, 0)


def attend(near, around, after, qkv, out_weight, gain, up, down):
    return pl.pallas_call(
        attend_kernel,
        out_shape=jax.ShapeDtypeStruct((COLS, CHAN, ROWS, 16, D), BF16),
        grid_spec=pltpu.PrefetchScalarGridSpec(
            num_scalar_prefetch=1,
            grid=(),
            in_specs=[VMEM] * 7,
            out_specs=VMEM,
            scratch_shapes=[
                pltpu.VMEM(((SPOTS + 1) * CELLS, 2 * D), BF16),
                pltpu.VMEM((OWN * CELLS, D), BF16),
                pltpu.VMEM((9 * CELLS, 2 * D), BF16),
                pltpu.VMEM((OWN * CELLS, D), BF16),
            ],
        ),
        compiler_params=pltpu.CompilerParams(vmem_limit_bytes=40 << 20),
        name="attend",
    )(near, around.reshape(SPOTS * CELLS, D), after, qkv, out_weight, gain, up, down)


def return_kernel(tiles, out, send, recv, local):
    device, chan = lax.axis_index("tiles"), lax.axis_index("chan")
    rank = lax.rem(device, GROUP)
    base = device - rank
    greet(group_partners(base, rank, chan))
    started = []
    for step in range(GROUP):
        target = lax.rem(rank + step, GROUP)
        for col in range(COLS):
            i = rank * COLS + col - target
            for c in range(1 if step == 0 else 0, CHAN):
                at = lax.rem(chan + c, CHAN)
                copy = remote(
                    tiles.at[col, at],
                    out.at[i, chan],
                    send.at[len(started)],
                    recv.at[i * CHAN + chan],
                    (base + target, at),
                )
                valid = (i >= 0) & (i < HELD)
                started.append((copy, valid))

                @pl.when(valid)
                def _():
                    copy.start()

    stays = []
    for col in range(COLS):
        copy = pltpu.make_async_copy(tiles.at[col, chan], out.at[rank + col, chan], local.at[col])
        copy.start()
        stays.append(copy)
    for step in range(HELD):
        i = lax.rem(rank + step, HELD)
        for c in range(1 if step < COLS else 0, CHAN):
            at = lax.rem(chan + c, CHAN)
            remote(
                tiles.at[0, 0], out.at[i, at], send.at[0], recv.at[i * CHAN + at], (device, at)
            ).wait_recv()
    for copy, valid in started:

        @pl.when(valid)
        def _():
            copy.wait_send()

    for copy in stays:
        copy.wait()


def return_home(tiles):
    return pl.pallas_call(
        return_kernel,
        out_shape=jax.ShapeDtypeStruct((HELD, CHAN, ROWS, 16, D), BF16),
        in_specs=[ANY],
        out_specs=ANY,
        scratch_shapes=[
            pltpu.SemaphoreType.DMA((GROUP * CHAN * COLS,)),
            pltpu.SemaphoreType.DMA((HELD * CHAN,)),
            pltpu.SemaphoreType.DMA((COLS,)),
        ],
        compiler_params=pltpu.CompilerParams(collective_id=3, has_side_effects=True),
        name="return_home",
    )(tiles)


def unpack_kernel(where, tiles, out):
    filled = pl.program_id(0) < where[1]

    @pl.when(filled)
    def _():
        for c in range(CHAN):
            for r in range(ROWS):
                out[0, c * ROWS + r] = tiles[0, c, r]

    @pl.when(jnp.logical_not(filled))
    def _():
        out[...] = jnp.zeros_like(out)


def unpack(where, tiles):
    return pl.pallas_call(
        unpack_kernel,
        out_shape=jax.ShapeDtypeStruct((HELD, FACE, 16, D), BF16),
        grid_spec=pltpu.PrefetchScalarGridSpec(
            num_scalar_prefetch=1,
            grid=(HELD,),
            in_specs=[
                pl.BlockSpec(
                    (1, CHAN, ROWS, 16, D), lambda i, w: (jnp.minimum(i + w[0], HELD - 1), 0, 0, 0, 0)
                )
            ],
            out_specs=pl.BlockSpec((1, FACE, 16, D), lambda i, w: (i, 0, 0, 0)),
        ),
        name="unpack",
    )(where, tiles)


def per_device(
    latents,
    owner,
    neighbours,
    rotations,
    cell_mask,
    gain_image,
    conv_weight,
    gain_attn,
    qkv_weight,
    out_weight,
    gain_mlp,
    up_weight,
    down_weight,
):
    device = lax.axis_index("tiles").astype(jnp.int32)
    rank = device % GROUP
    base = device - rank
    fields, start, count = tables(owner, neighbours, rotations, cell_mask, device)
    shift = jnp.clip(start // FACE - base * COLS - rank, 0, HELD - 1)
    held = count // FACE
    firsts = lax.dynamic_slice_in_dim(owner, device * (COLS * FACE), COLS * FACE)
    source = jnp.clip(firsts.reshape(COLS, FACE)[:, 0] - base, 0, GROUP - 1)

    payload = pack(shift[None], latents, fields)
    got = spread_out(payload)
    own, normed, rims, marks = image(source, got, gain_image[None])
    around = halo(rims, 1)
    after, attn = stencil(around, own, normed, marks, conv_weight, gain_attn[None])
    near = marks[:, 0, :8, 7 : ROWS * 8 : 8].transpose(0, 2, 1).astype(jnp.int32).reshape(-1)
    around = halo(attn.reshape(OWN, CELLS, D), 2)
    tiles = attend(near, around, after, qkv_weight, out_weight, gain_mlp[None], up_weight, down_weight)
    home = return_home(tiles)
    out = unpack(jnp.stack([shift, held]), home)
    return out.reshape(SLOTS, 16, D)


def solution(mesh):
    in_specs = (
        P("tiles", "chan", None),
        P(),
        P("tiles", None),
        P("tiles", None),
        P("tiles", "chan"),
        P(),
        P(),
        P(),
        P(),
        P(),
        P(),
        P(),
        P(),
    )
    return jax.shard_map(
        per_device,
        mesh=mesh,
        in_specs=in_specs,
        out_specs=P("tiles", "chan", None),
        check_vma=False,
    )
```

```python
import math

import jax
import jax.numpy as jnp
from jax import lax
from jax.experimental import pallas as pl
from jax.experimental.pallas import tpu as pltpu
from jax.sharding import PartitionSpec as P

MESH = pl.DeviceIdType.MESH
VMEM = pl.BlockSpec(memory_space=pltpu.VMEM)
HBM = pl.BlockSpec(memory_space=pltpu.HBM)
F32, BF16 = jnp.float32, jnp.bfloat16

D = 384
FFN_UNITS = 1536
HEAD_DIM = 64
FACE = 16
BAND = 64
SIDE = 8
CELLS = 64
SLOTS = 80
HELD = 5
GROUP = 4
CHAN = 4
COLS = 2
ROWS = 4
OWN = COLS * ROWS
GRID_R, GRID_C = ROWS + 2, COLS + 2
SPOTS = GRID_R * GRID_C
HALF = ROWS * CELLS
RIM = 32
PIECE = ROWS * 3 + 1
epsilon = 1e-06


def rms(wide, gain):
    return wide * lax.rsqrt(jnp.mean(wide * wide, axis=-1, keepdims=True) + epsilon) * gain


def snake(q):
    return q // 2 * 2 + lax.rem(q + q // 2, 2)


def device_of(worker):
    base = worker // GROUP * GROUP
    return base + snake(worker - base)


def remote(src, dst, send, recv, device):
    return pltpu.make_async_remote_copy(
        src_ref=src, dst_ref=dst, send_sem=send, recv_sem=recv, device_id=device, device_id_type=MESH
    )


def neighbour_places(near, start, count):
    slot = lax.broadcasted_iota(jnp.int32, near.shape, 1)
    base = jnp.where(
        near < SLOTS,
        start,
        jnp.where(near < SLOTS + FACE, start - FACE - SLOTS, start + count - SLOTS - FACE),
    )
    tile = (near + base) & (FACE * BAND - 1)
    own_col = (start + slot) >> 4
    grid_row = (tile & 15) - (slot & 12) + 1
    grid_col = ((tile >> 4) - (own_col - (own_col & 1)) + 1) & (BAND - 1)
    grid_row = jnp.minimum(jnp.maximum(grid_row, 0), GRID_R - 1)
    grid_col = jnp.minimum(jnp.maximum(grid_col, 0), GRID_C - 1)
    return jnp.where(near < SLOTS + 2 * FACE, grid_col * GRID_R + grid_row, SPOTS)


def rim_wanted(near, turns):
    q = lax.broadcasted_iota(jnp.int32, (48, 128), 0)

    def pick(*values):
        found = values[7]
        for at, top in ((6, 35), (5, 34), (4, 33), (3, 32), (2, 24), (1, 16), (0, 8)):
            found = jnp.where(q < top, values[at], found)
        return found

    along = q & 7
    order = (1, 6, 3, 4, 0, 2, 5, 7)
    place = pick(*[near[n : n + 1] for n in order])
    turn = pick(*[turns[n : n + 1] for n in order])
    i = pick(7, 0, along, along, 7, 7, 0, 0)
    j = pick(along, along, 7, 0, 7, 0, 7, 0)

    def turned(a, b, c, d):
        return jnp.where(turn < 0.5, a, jnp.where(turn < 1.5, b, jnp.where(turn < 2.5, c, d)))

    from_row = turned(i, j, 7 - i, 7 - j)
    from_col = turned(j, 7 - i, 7 - j, i)
    rim = jnp.where(
        from_row == 0,
        from_col,
        jnp.where(from_row == 7, 8 + from_col, jnp.where(from_col == 0, 16 + from_row, 24 + from_row)),
    )
    return jnp.where(q < 36, place * RIM + rim.astype(F32), float(SPOTS * RIM))


def halo_moves(device, chan, base, rank):
    worker = base + snake(rank)
    total = lax.axis_size("tiles")
    left = device_of(lax.rem(worker + total - 1, total))
    right = device_of(lax.rem(worker + 1, total))
    up, down = chan > 0, chan < CHAN - 1
    above, below = lax.rem(chan + CHAN - 1, CHAN), lax.rem(chan + 1, CHAN)
    first, second, third = GRID_R, 2 * GRID_R, 3 * GRID_R
    moves = [
        (first + 1, third + 1, ROWS, 0, (left, chan), None, None),
        (second + 1, 1, ROWS, 1, (right, chan), None, None),
        (first + 1, third + ROWS + 1, 1, 0, (left, above), up, down),
        (first + ROWS, third, 1, 0, (left, below), down, up),
        (first + 1, first + ROWS + 1, 1, 0, (device, above), up, down),
        (first + ROWS, first, 1, 0, (device, below), down, up),
        (second + 1, ROWS + 1, 1, 1, (right, above), up, down),
        (second + ROWS, 0, 1, 1, (right, below), down, up),
        (second + 1, second + ROWS + 1, 1, 1, (device, above), up, down),
        (second + ROWS, second, 1, 1, (device, below), down, up),
    ]
    return moves, (left, right, above, below)


def when(condition, action):
    if condition is None:
        action()
    else:
        pl.when(condition)(action)


def block_kernel(
    owner_hbm,
    mask_in,
    near_in,
    turn_in,
    latents,
    gain_image,
    gain_attn,
    gain_mlp,
    conv_hbm,
    qkv_hbm,
    proj_hbm,
    up_hbm,
    down_hbm,
    out,
    owner,
    raw,
    held,
    payload,
    got,
    own,
    normed,
    marks,
    rims,
    frame,
    patches,
    after,
    table,
    memory,
    queries,
    keys,
    mixed,
    tiles,
    home,
    conv,
    qkv,
    proj,
    up,
    down,
    load_sem,
    spread_send,
    spread_recv,
    rim_send,
    rim_recv,
    halo_send,
    halo_recv,
    home_send,
    home_recv,
    local,
):
    device, chan = lax.axis_index("tiles"), lax.axis_index("chan")
    rank = lax.rem(device, GROUP)
    base = device - rank
    place = snake(rank)
    moves, (left, right, above, below) = halo_moves(device, chan, base, rank)

    owner_load = pltpu.make_async_copy(owner_hbm, owner, load_sem.at[6])
    owner_load.start()
    first_load = pltpu.make_async_copy(latents, held, load_sem.at[0])
    first_load.start()
    loads = []
    for at, (src, dst) in enumerate(
        [(conv_hbm, conv), (qkv_hbm, qkv), (proj_hbm, proj), (up_hbm, up), (down_hbm, down)]
    ):
        loads.append(pltpu.make_async_copy(src, dst, load_sem.at[1 + at]))

    barrier = pltpu.get_barrier_semaphore()
    partners = []
    for step in range(1, GROUP * CHAN):
        other = lax.rem(rank * CHAN + chan + step, GROUP * CHAN)
        partners.append((base + other // CHAN, lax.rem(other, CHAN)))
    for side in (left, right):
        partners += [(side, chan), (side, above), (side, below)]
    for partner in partners:
        pl.semaphore_signal(barrier, inc=1, device_id=partner, device_id_type=MESH)

    def count_columns(col, carry):
        start, count = carry
        holder = owner[col * FACE]
        return (
            start + jnp.where(holder < device, 1, 0),
            count + jnp.where(holder == device, 1, 0),
        )

    owner_load.wait()
    start, count = lax.fori_loop(0, BAND, count_columns, (jnp.int32(0), jnp.int32(0)))
    limit = lambda value, top: jnp.minimum(jnp.maximum(value, 0), top)
    shift = limit(start - base * COLS - rank, HELD - 1)
    sources = [
        limit(owner[((base + place) * COLS + col) * FACE] - base, GROUP - 1) for col in range(COLS)
    ]

    raw[...] = jnp.zeros_like(raw)
    raw[0:16, 0:SLOTS] = mask_in[...]
    raw[16:24, 0:SLOTS] = near_in[...]
    raw[24:32, 0:SLOTS] = turn_in[...]
    lane = lax.broadcasted_iota(jnp.int32, (16, 128), 1)
    mask_rows = raw[0:16].astype(F32)
    near_rows = neighbour_places(raw[16:24], start * FACE, count * FACE).astype(F32)
    near_rows = jnp.concatenate([near_rows, raw[24:32].astype(F32)], axis=0)
    for i in range(HELD):
        cells = pltpu.roll(mask_rows, (128 - i * FACE) % 128, axis=1)
        near = pltpu.roll(near_rows, (128 + FACE - i * FACE) % 128, axis=1)
        marks[i] = jnp.where(lane < FACE, cells, near).astype(BF16)
    first_load.wait()

    def fill(i, _):
        col = lax.rem(i + HELD - shift, HELD)
        field = marks[col]
        for c in range(CHAN):
            for r in range(ROWS):
                for part in range(3):
                    payload[i, c, r * 3 + part] = held[col, c * ROWS + r, :, part * 128 : (part + 1) * 128]
            payload[i, c, PIECE - 1] = field
        return 0

    lax.fori_loop(0, HELD, fill, 0)
    pl.semaphore_wait(barrier, len(partners))

    sent = []
    for c in (2, 3, 1, 0):
        to = lax.rem(chan + c, CHAN)
        for i in range(HELD):
            target = snake((rank + i) // COLS)
            col = lax.rem(rank + i, COLS)
            copy = remote(
                payload.at[i, to],
                got.at[rank, chan, col],
                spread_send.at[len(sent)],
                spread_recv.at[(rank * CHAN + chan) * COLS + col],
                (base + target, to),
            )
            needed = None if c else target != rank
            when(needed, copy.start)
            sent.append((copy, needed))
    stays = []
    for col in range(COLS):
        i = place * COLS + col - rank
        copy = pltpu.make_async_copy(
            payload.at[limit(i, HELD - 1), chan], got.at[rank, chan, col], local.at[col]
        )
        inside = (i >= 0) & (i < HELD)
        when(inside, copy.start)
        stays.append((copy, inside))
    for load in loads:
        load.start()
    beyond = jnp.zeros((RIM, D), BF16)
    for col in range(GRID_C):

        @pl.when(chan == 0)
        def _():
            rims[col * GRID_R] = beyond
            for part in range(2):
                table[col * GRID_R, part * RIM : (part + 1) * RIM] = beyond

        @pl.when(chan == CHAN - 1)
        def _():
            rims[(col + 1) * GRID_R - 1] = beyond
            for part in range(2):
                table[(col + 1) * GRID_R - 1, part * RIM : (part + 1) * RIM] = beyond

    def exchange(buffer, send, recv, col):
        for at, (src, dst, many, ready, to, needed, _) in enumerate(moves):
            if ready == col:
                copy = remote(
                    buffer.at[pl.ds(src, many)], buffer.at[pl.ds(dst, many)], send.at[at], recv.at[at], to
                )
                when(needed, copy.start)

    def arrived(buffer, send, recv):
        for at, (src, dst, many, _, to, needed, coming) in enumerate(moves):
            copy = remote(
                buffer.at[pl.ds(src, many)], buffer.at[pl.ds(dst, many)], send.at[at], recv.at[at], to
            )
            when(coming, copy.wait_recv)

    def departed(buffer, send, recv):
        for at, (src, dst, many, _, to, needed, _) in enumerate(moves):
            copy = remote(
                buffer.at[pl.ds(src, many)], buffer.at[pl.ds(dst, many)], send.at[at], recv.at[at], to
            )
            when(needed, copy.wait_send)

    for step in range(GROUP):
        source = lax.rem(rank + step, GROUP)
        for c in range(CHAN):
            at = lax.rem(chan + c, CHAN)
            for col in range(COLS):
                far = place * COLS + col - source
                if step == 0 and c == 0:
                    when(stays[col][1], stays[col][0].wait)
                else:
                    arrival = remote(
                        payload.at[0, 0],
                        got.at[source, at, col],
                        spread_send.at[0],
                        spread_recv.at[(source * CHAN + at) * COLS + col],
                        (device, at),
                    )
                    when((far >= 0) & (far < HELD), arrival.wait_recv)

    row = lax.broadcasted_iota(jnp.int32, (RIM, CELLS), 0)
    cell = lax.broadcasted_iota(jnp.int32, (RIM, CELLS), 1)
    edge, along = row >> 3, row & 7
    at_rim = jnp.where(
        edge == 0, along, jnp.where(edge == 1, 56 + along, jnp.where(edge == 2, along * 8, along * 8 + 7))
    )
    at_rim = jnp.where(cell == at_rim, 1.0, 0.0).astype(BF16)
    gain_of = lambda gain: gain[...].reshape(1, D)
    wide_lane = lax.broadcasted_iota(jnp.int32, (48, 128), 1)
    masks = []
    wanted = []
    for col in range(COLS):
        blocks = [got[sources[col], c, col, PIECE - 1].astype(F32) for c in range(CHAN)]
        all_wanted = rim_wanted(blocks[0][0:8], blocks[0][8:16])
        for r in range(ROWS):
            slot = chan * ROWS + r
            wanted.append(
                jnp.sum(jnp.where(wide_lane == slot + FACE, all_wanted, 0.0), axis=1, keepdims=True)
            )
            pieces, column = [], []
            for c in range(CHAN):
                pieces.append(
                    jnp.concatenate([got[sources[col], c, col, r * 3 + part] for part in range(3)], axis=1)
                )
                column.append(jnp.sum(jnp.where(lane == slot, blocks[c], 0.0), axis=1, keepdims=True))
            values = jnp.concatenate(pieces, axis=0)
            mask = jnp.concatenate(column, axis=0)
            masks.append(mask)
            tile = col * ROWS + r
            own[tile * CELLS : (tile + 1) * CELLS] = values
            norm = (rms(values.astype(F32), gain_of(gain_image)) * mask).astype(BF16)
            normed[tile] = norm
            rims[(1 + col) * GRID_R + 1 + r] = jnp.dot(at_rim, norm, preferred_element_type=F32).astype(BF16)
        exchange(rims, rim_send, rim_recv, col)

    for tile in range(OWN):
        frame[tile, 1:9, 8:16, :] = normed[tile].astype(F32).reshape(SIDE, SIDE, D)
    loads[0].wait()
    arrived(rims, rim_send, rim_recv)

    rim_lane = lax.broadcasted_iota(jnp.int32, (48, SPOTS * RIM), 1).astype(F32)
    for col in range(COLS):
        for r in range(ROWS):
            tile = col * ROWS + r
            chosen = jnp.where(rim_lane == wanted[tile], 1.0, 0.0).astype(BF16)
            rim = jnp.dot(chosen, rims[...].reshape(SPOTS * RIM, D), preferred_element_type=F32)
            frame[tile, 0, 8:16, :] = rim[0:8]
            frame[tile, 9, 8:16, :] = rim[8:16]
            for i in range(SIDE):
                frame[tile, 1 + i, 7:8, :] = rim[16 + i : 17 + i]
                frame[tile, 1 + i, 16:17, :] = rim[24 + i : 25 + i]
            frame[tile, 0, 7:8, :] = rim[32:33]
            frame[tile, 0, 16:17, :] = rim[33:34]
            frame[tile, 9, 7:8, :] = rim[34:35]
            frame[tile, 9, 16:17, :] = rim[35:36]
            for tap in range(9):
                dr, dc = tap // 3, tap % 3
                window = frame[tile, dr : dr + SIDE, 7 + dc : 7 + dc + SIDE, :]
                patches[tile * CELLS : (tile + 1) * CELLS, tap * D : (tap + 1) * D] = window.reshape(
                    CELLS, D
                ).astype(BF16)
        rows = slice(col * HALF, (col + 1) * HALF)
        total = jnp.dot(patches[rows, :], conv[...], preferred_element_type=F32)
        image = (own[rows, :].astype(F32) + total).astype(BF16)
        after[rows, :] = image
        mask = jnp.concatenate(masks[col * ROWS : (col + 1) * ROWS], axis=0)
        attn = (rms(image.astype(F32), gain_of(gain_attn)) * mask).astype(BF16)
        spot = (1 + col) * GRID_R + 1
        table[spot : spot + ROWS] = attn.reshape(ROWS, CELLS, D)
        exchange(table, halo_send, halo_recv, col)

    def project(spot, many):
        rows = table[spot : spot + many].reshape(many * CELLS, D)
        found = jnp.dot(rows, qkv[:, D:], preferred_element_type=F32)
        memory[spot * CELLS : (spot + many) * CELLS, :] = found.astype(BF16)

    loads[1].wait()
    scale = 1.0 / math.sqrt(HEAD_DIM)
    for col in range(COLS):
        spot = (1 + col) * GRID_R + 1
        found = jnp.dot(
            table[spot : spot + ROWS].reshape(HALF, D), qkv[:, :D], preferred_element_type=F32
        )
        queries[col * HALF : (col + 1) * HALF, :] = (found * scale).astype(BF16)
        project(spot, ROWS)
    for load in loads[2:]:
        load.wait()
    arrived(table, halo_send, halo_recv)
    project(0, GRID_R + 1)
    project(GRID_R + ROWS + 1, 2)
    project(2 * GRID_R + ROWS + 1, GRID_R + 1)

    low = lax.broadcasted_iota(jnp.int32, (CELLS, 128), 1) < HEAD_DIM
    returned = []
    for col in range(COLS):

        def tile_step(r, _):
            for n in range(3):
                spot = (col + n) * GRID_R + r
                keys[n * 3 * CELLS : (n + 1) * 3 * CELLS, :] = memory[
                    pl.ds(pl.multiple_of(spot * CELLS, CELLS), 3 * CELLS), :
                ]
            rows = pl.ds(pl.multiple_of(col * HALF + r * CELLS, CELLS), CELLS)
            for pair in range(3):
                lanes = slice(pair * 128, (pair + 1) * 128)
                query = queries[rows, lanes]
                nothing = jnp.zeros_like(query)
                both = jnp.concatenate(
                    [jnp.where(low, query, nothing), jnp.where(low, nothing, query)], axis=0
                )
                scores = lax.dot_general(
                    both, keys[:, lanes], (((1,), (1,)), ((), ())), preferred_element_type=F32
                )
                weights = jnp.exp(scores - jnp.max(scores, axis=-1, keepdims=True))
                total = jnp.sum(weights, axis=-1, keepdims=True)
                value = jnp.dot(
                    weights.astype(BF16),
                    keys[:, D + pair * 128 : D + (pair + 1) * 128],
                    preferred_element_type=F32,
                )
                value = value / total
                mixed[rows, lanes] = jnp.where(low, value[:CELLS], value[CELLS:]).astype(BF16)
            return 0

        lax.fori_loop(0, ROWS, tile_step, 0)
        rows = slice(col * HALF, (col + 1) * HALF)
        attended = jnp.dot(mixed[rows, :], proj[...], preferred_element_type=F32)
        attended = (after[rows, :].astype(F32) + attended).astype(BF16)
        wide = attended.astype(F32)
        hidden = jnp.dot(rms(wide, gain_of(gain_mlp)).astype(BF16), up[...], preferred_element_type=F32)
        hidden = (0.5 * hidden * (1.0 + lax.erf(hidden * (0.5**0.5)))).astype(BF16)
        encoded = wide + jnp.dot(hidden, down[...], preferred_element_type=F32)
        encoded = encoded.astype(BF16).reshape(ROWS, CHAN, 16, D)
        for r in range(ROWS):
            for c in range(CHAN):
                tiles[col, c, r] = encoded[r, c]
        for c in (2, 3, 1, 0):
            to = lax.rem(chan + c, CHAN)
            for step in range(GROUP):
                target = lax.rem(rank + step, GROUP)
                i = place * COLS + col - target
                slot = limit(i, HELD - 1)
                inside = (i >= 0) & (i < HELD)
                if c == 0 and step == 0:
                    copy = pltpu.make_async_copy(tiles.at[col, chan], home.at[slot, chan], local.at[COLS + col])
                    when(inside, copy.start)
                    returned.append((copy, inside, True))
                else:
                    copy = remote(
                        tiles.at[col, to],
                        home.at[slot, chan],
                        home_send.at[len(returned)],
                        home_recv.at[slot * CHAN + chan],
                        (base + target, to),
                    )
                    when(inside, copy.start)
                    returned.append((copy, inside, False))

    departed(rims, rim_send, rim_recv)
    departed(table, halo_send, halo_recv)
    for copy, needed in sent:
        when(needed, copy.wait_send)
    for copy, inside, stays_here in returned:
        if stays_here:
            when(inside, copy.wait)
    for i in range(HELD):
        worker = snake((rank + i) // COLS)
        for c in range(CHAN):
            at = lax.rem(chan + c, CHAN)
            arrival = remote(
                tiles.at[0, 0], home.at[i, at], home_send.at[0], home_recv.at[i * CHAN + at], (device, at)
            )
            when(None if c else worker != rank, arrival.wait_recv)

    for i in range(HELD):
        from_col = limit(i + shift, HELD - 1)
        for c in range(CHAN):
            for r in range(ROWS):
                values = home[from_col, c, r]
                out[i, c * ROWS + r] = lax.select(i < count, values, jnp.zeros_like(values))
    for copy, inside, stays_here in returned:
        if not stays_here:
            when(inside, copy.wait_send)


def per_device(
    latents,
    owner,
    neighbours,
    rotations,
    cell_mask,
    gain_image,
    conv_weight,
    gain_attn,
    qkv_weight,
    out_weight,
    gain_mlp,
    up_weight,
    down_weight,
):
    weights = [conv_weight, qkv_weight, out_weight, up_weight, down_weight]
    vmem = pltpu.VMEM
    dma = pltpu.SemaphoreType.DMA
    moves = 6 + 2 * COLS
    out = pl.pallas_call(
        block_kernel,
        out_shape=jax.ShapeDtypeStruct((HELD, FACE, 16, D), BF16),
        in_specs=[HBM] + [VMEM] * 3 + [HBM] + [VMEM] * 3 + [HBM] * 5,
        out_specs=VMEM,
        scratch_shapes=[
            pltpu.SMEM((FACE * BAND,), jnp.int32),
            vmem((32, 128), jnp.int32),
            vmem((HELD, FACE, 16, D), BF16),
            vmem((HELD, CHAN, PIECE, 16, 128), BF16),
            vmem((GROUP, CHAN, COLS, PIECE, 16, 128), BF16),
            vmem((OWN * CELLS, D), BF16),
            vmem((OWN, CELLS, D), BF16),
            vmem((HELD, FACE, 128), BF16),
            vmem((SPOTS, RIM, D), BF16),
            vmem((OWN, 10, 24, D), F32),
            vmem((OWN * CELLS, 9 * D), BF16),
            vmem((OWN * CELLS, D), BF16),
            vmem((SPOTS, CELLS, D), BF16),
            vmem((SPOTS * CELLS, 2 * D), BF16),
            vmem((OWN * CELLS, D), BF16),
            vmem((9 * CELLS, 2 * D), BF16),
            vmem((OWN * CELLS, D), BF16),
            vmem((COLS, CHAN, ROWS, 16, D), BF16),
            vmem((HELD, CHAN, ROWS, 16, D), BF16),
            *[vmem(w.shape, BF16) for w in weights],
            dma((7,)),
            dma((HELD * CHAN,)),
            dma((GROUP * CHAN * COLS,)),
            dma((moves,)),
            dma((moves,)),
            dma((moves,)),
            dma((moves,)),
            dma((GROUP * CHAN * COLS,)),
            dma((HELD * CHAN,)),
            dma((2 * COLS,)),
        ],
        compiler_params=pltpu.CompilerParams(
            collective_id=0, has_side_effects=True, vmem_limit_bytes=60 << 20
        ),
        name="encoder_block",
    )(
        owner,
        cell_mask.T,
        neighbours.T,
        rotations.T,
        latents.reshape(HELD, FACE, 16, D),
        gain_image,
        gain_attn,
        gain_mlp,
        *weights,
    )
    return out.reshape(SLOTS, 16, D)


def solution(mesh):
    in_specs = (
        P("tiles", "chan", None),
        P(),
        P("tiles", None),
        P("tiles", None),
        P("tiles", "chan"),
        P(),
        P(),
        P(),
        P(),
        P(),
        P(),
        P(),
        P(),
    )
    return jax.shard_map(
        per_device,
        mesh=mesh,
        in_specs=in_specs,
        out_specs=P("tiles", "chan", None),
        check_vma=False,
    )
```

```python
import math

import jax
import jax.numpy as jnp
from jax import lax
from jax.experimental import pallas as pl
from jax.experimental.pallas import tpu as pltpu
from jax.sharding import PartitionSpec as P

MESH = pl.DeviceIdType.MESH
VMEM = pl.BlockSpec(memory_space=pltpu.VMEM)
SMEM = pl.BlockSpec(memory_space=pltpu.SMEM)
HBM = pl.BlockSpec(memory_space=pltpu.HBM)
F32, BF16 = jnp.float32, jnp.bfloat16

D = 384
FFN_UNITS = 1536
HEAD_DIM = 64
FACE = 16
BAND = 64
SIDE = 8
CELLS = 64
SLOTS = 80
HELD = 5
GROUP = 4
CHAN = 4
COLS = 2
ROWS = 4
OWN = COLS * ROWS
GRID_R, GRID_C = ROWS + 2, COLS + 2
SPOTS = GRID_R * GRID_C
HALF = ROWS * CELLS
PART = 2
RIM = 32
PIECE = ROWS * 3 + 1
epsilon = 1e-06


def rms(wide, gain):
    return wide * lax.rsqrt(jnp.mean(wide * wide, axis=-1, keepdims=True) + epsilon) * gain


def snake(q):
    return q // 2 * 2 + lax.rem(q + q // 2, 2)


def device_of(worker):
    base = worker // GROUP * GROUP
    return base + snake(worker - base)


def remote(src, dst, send, recv, device):
    return pltpu.make_async_remote_copy(
        src_ref=src, dst_ref=dst, send_sem=send, recv_sem=recv, device_id=device, device_id_type=MESH
    )


def neighbour_places(near, start, count):
    slot = lax.broadcasted_iota(jnp.int32, near.shape, 1)
    base = jnp.where(
        near < SLOTS,
        start,
        jnp.where(near < SLOTS + FACE, start - FACE - SLOTS, start + count - SLOTS - FACE),
    )
    tile = (near + base) & (FACE * BAND - 1)
    own_col = (start + slot) >> 4
    grid_row = (tile & 15) - (slot & 12) + 1
    grid_col = ((tile >> 4) - (own_col - (own_col & 1)) + 1) & (BAND - 1)
    grid_row = jnp.minimum(jnp.maximum(grid_row, 0), GRID_R - 1)
    grid_col = jnp.minimum(jnp.maximum(grid_col, 0), GRID_C - 1)
    return jnp.where(near < SLOTS + 2 * FACE, grid_col * GRID_R + grid_row, SPOTS)


def rim_wanted(near, turns):
    q = lax.broadcasted_iota(jnp.int32, (48, 128), 0)

    def pick(*values):
        found = values[7]
        for at, top in ((6, 35), (5, 34), (4, 33), (3, 32), (2, 24), (1, 16), (0, 8)):
            found = jnp.where(q < top, values[at], found)
        return found

    along = q & 7
    order = (1, 6, 3, 4, 0, 2, 5, 7)
    place = pick(*[near[n : n + 1] for n in order])
    turn = pick(*[turns[n : n + 1] for n in order])
    i = pick(7, 0, along, along, 7, 7, 0, 0)
    j = pick(along, along, 7, 0, 7, 0, 7, 0)

    def turned(a, b, c, d):
        return jnp.where(turn < 0.5, a, jnp.where(turn < 1.5, b, jnp.where(turn < 2.5, c, d)))

    from_row = turned(i, j, 7 - i, 7 - j)
    from_col = turned(j, 7 - i, 7 - j, i)
    rim = jnp.where(
        from_row == 0,
        from_col,
        jnp.where(from_row == 7, 8 + from_col, jnp.where(from_col == 0, 16 + from_row, 24 + from_row)),
    )
    return jnp.where(q < 36, place * RIM + rim.astype(F32), float(SPOTS * RIM))


def halo_moves(device, chan, base, rank):
    worker = base + snake(rank)
    total = lax.axis_size("tiles")
    left = device_of(lax.rem(worker + total - 1, total))
    right = device_of(lax.rem(worker + 1, total))
    up, down = chan > 0, chan < CHAN - 1
    above, below = lax.rem(chan + CHAN - 1, CHAN), lax.rem(chan + 1, CHAN)
    first, second, third = GRID_R, 2 * GRID_R, 3 * GRID_R
    last = ROWS - PART
    moves = [
        (first + 1, third + 1, PART, (0, 0), (left, chan), None, None),
        (second + 1, 1, PART, (1, 0), (right, chan), None, None),
        (first + 1 + last, third + 1 + last, PART, (0, last), (left, chan), None, None),
        (second + 1 + last, 1 + last, PART, (1, last), (right, chan), None, None),
        (first + 1, third + ROWS + 1, 1, (0, 0), (left, above), up, down),
        (first + ROWS, third, 1, (0, last), (left, below), down, up),
        (first + 1, first + ROWS + 1, 1, (0, 0), (device, above), up, down),
        (first + ROWS, first, 1, (0, last), (device, below), down, up),
        (second + 1, ROWS + 1, 1, (1, 0), (right, above), up, down),
        (second + ROWS, 0, 1, (1, last), (right, below), down, up),
        (second + 1, second + ROWS + 1, 1, (1, 0), (device, above), up, down),
        (second + ROWS, second, 1, (1, last), (device, below), down, up),
    ]
    return moves, (left, right, above, below)


def when(condition, action):
    if condition is None:
        action()
    else:
        pl.when(condition)(action)


def block_kernel(
    owner_hbm,
    mask_in,
    near_in,
    turn_in,
    latents,
    gain_image,
    gain_attn,
    gain_mlp,
    conv_hbm,
    qkv_hbm,
    proj_hbm,
    up_hbm,
    down_hbm,
    home,
    where,
    owner,
    raw,
    held,
    payload,
    got_first,
    got_second,
    own,
    normed,
    marks,
    rims,
    frame,
    patches,
    after,
    table,
    memory,
    queries,
    keys,
    mixed,
    tiles,
    conv,
    qkv,
    proj,
    up,
    down,
    load_sem,
    spread_send,
    spread_recv,
    rim_send,
    rim_recv,
    halo_send,
    halo_recv,
    home_send,
    home_recv,
    local,
):
    device, chan = lax.axis_index("tiles"), lax.axis_index("chan")
    rank = lax.rem(device, GROUP)
    base = device - rank
    place = snake(rank)
    moves, (left, right, above, below) = halo_moves(device, chan, base, rank)

    got = (got_first, got_second)
    owner_load = pltpu.make_async_copy(owner_hbm, owner, load_sem.at[6])
    owner_load.start()
    first_load = pltpu.make_async_copy(latents, held, load_sem.at[0])
    first_load.start()
    loads = []
    for at, (src, dst) in enumerate(
        [(conv_hbm, conv), (qkv_hbm, qkv), (proj_hbm, proj), (up_hbm, up), (down_hbm, down)]
    ):
        loads.append(pltpu.make_async_copy(src, dst, load_sem.at[1 + at]))

    barrier = pltpu.get_barrier_semaphore()
    partners = []
    for step in range(1, GROUP * CHAN):
        other = lax.rem(rank * CHAN + chan + step, GROUP * CHAN)
        partners.append((base + other // CHAN, lax.rem(other, CHAN)))
    for side in (left, right):
        partners += [(side, chan), (side, above), (side, below)]
    for partner in partners:
        pl.semaphore_signal(barrier, inc=1, device_id=partner, device_id_type=MESH)

    def count_columns(col, carry):
        start, count = carry
        holder = owner[col * FACE]
        return (
            start + jnp.where(holder < device, 1, 0),
            count + jnp.where(holder == device, 1, 0),
        )

    owner_load.wait()
    start, count = lax.fori_loop(0, BAND, count_columns, (jnp.int32(0), jnp.int32(0)))
    limit = lambda value, top: jnp.minimum(jnp.maximum(value, 0), top)
    shift = limit(start - base * COLS - rank, HELD - 1)
    where[0], where[1] = shift, count
    sources = [
        limit(owner[((base + place) * COLS + col) * FACE] - base, GROUP - 1) for col in range(COLS)
    ]

    raw[...] = jnp.zeros_like(raw)
    raw[0:16, 0:SLOTS] = mask_in[...]
    raw[16:24, 0:SLOTS] = near_in[...]
    raw[24:32, 0:SLOTS] = turn_in[...]
    lane = lax.broadcasted_iota(jnp.int32, (16, 128), 1)
    mask_rows = raw[0:16].astype(F32)
    near_rows = neighbour_places(raw[16:24], start * FACE, count * FACE).astype(F32)
    near_rows = jnp.concatenate([near_rows, raw[24:32].astype(F32)], axis=0)
    for i in range(HELD):
        cells = pltpu.roll(mask_rows, (128 - i * FACE) % 128, axis=1)
        near = pltpu.roll(near_rows, (128 + FACE - i * FACE) % 128, axis=1)
        marks[i] = jnp.where(lane < FACE, cells, near).astype(BF16)
    first_load.wait()

    def fill(i):
        col = lax.rem(i + HELD - shift, HELD)
        for c in range(CHAN):
            for r in range(ROWS):
                for part in range(3):
                    payload[i, c, r * 3 + part] = held[col, c * ROWS + r, :, part * 128 : (part + 1) * 128]
            payload[i, c, PIECE - 1] = marks[col]

    sent = []
    for step in range(HELD):
        i = lax.rem(2 * step + lax.rem(rank, 2), HELD)
        fill(i)
        if step == 0:
            pl.semaphore_wait(barrier, len(partners))
        target = snake((rank + i) // COLS)
        odd = lax.rem(rank, 2) == 1
        for c in (2, 3, 1, 0):
            to = lax.rem(chan + c, CHAN)
            away = None if c else target != rank
            for col in range(COLS):
                if step == 2:
                    needed = odd if col else jnp.logical_not(odd)
                    needed = needed if away is None else needed & away
                elif (step > 2) == (col == 1):
                    needed = away
                else:
                    continue
                copy = remote(
                    payload.at[i, to],
                    got[col].at[rank, chan],
                    spread_send.at[step * CHAN + c],
                    spread_recv.at[(rank * CHAN + chan) * COLS + col],
                    (base + target, to),
                )
                when(needed, copy.start)
                sent.append((copy, needed))
    stays = []
    for col in range(COLS):
        i = place * COLS + col - rank
        copy = pltpu.make_async_copy(
            payload.at[limit(i, HELD - 1), chan], got[col].at[rank, chan], local.at[col]
        )
        inside = (i >= 0) & (i < HELD)
        when(inside, copy.start)
        stays.append((copy, inside))
    for load in loads:
        load.start()
    beyond = jnp.zeros((RIM, D), BF16)
    for col in range(GRID_C):

        @pl.when(chan == 0)
        def _():
            rims[col * GRID_R] = beyond
            for part in range(2):
                table[col * GRID_R, part * RIM : (part + 1) * RIM] = beyond

        @pl.when(chan == CHAN - 1)
        def _():
            rims[(col + 1) * GRID_R - 1] = beyond
            for part in range(2):
                table[(col + 1) * GRID_R - 1, part * RIM : (part + 1) * RIM] = beyond

    def exchange(buffer, send, recv, kind, which):
        for at, (src, dst, many, ready, to, needed, _) in enumerate(moves):
            if ready[kind] == which:
                copy = remote(
                    buffer.at[pl.ds(src, many)], buffer.at[pl.ds(dst, many)], send.at[at], recv.at[at], to
                )
                when(needed, copy.start)

    def arrived(buffer, send, recv):
        for at, (src, dst, many, _, to, needed, coming) in enumerate(moves):
            copy = remote(
                buffer.at[pl.ds(src, many)], buffer.at[pl.ds(dst, many)], send.at[at], recv.at[at], to
            )
            when(coming, copy.wait_recv)

    def departed(buffer, send, recv):
        for at, (src, dst, many, _, to, needed, _) in enumerate(moves):
            copy = remote(
                buffer.at[pl.ds(src, many)], buffer.at[pl.ds(dst, many)], send.at[at], recv.at[at], to
            )
            when(needed, copy.wait_send)

    def pieces_in(col):
        for step in range(GROUP):
            source = lax.rem(rank + step, GROUP)
            far = place * COLS + col - source
            for c in range(CHAN):
                at = lax.rem(chan + c, CHAN)
                if step == 0 and c == 0:
                    when(stays[col][1], stays[col][0].wait)
                else:
                    arrival = remote(
                        payload.at[0, 0],
                        got[col].at[source, at],
                        spread_send.at[0],
                        spread_recv.at[(source * CHAN + at) * COLS + col],
                        (device, at),
                    )
                    when((far >= 0) & (far < HELD), arrival.wait_recv)

    row = lax.broadcasted_iota(jnp.int32, (RIM, CELLS), 0)
    cell = lax.broadcasted_iota(jnp.int32, (RIM, CELLS), 1)
    edge, along = row >> 3, row & 7
    at_rim = jnp.where(
        edge == 0, along, jnp.where(edge == 1, 56 + along, jnp.where(edge == 2, along * 8, along * 8 + 7))
    )
    at_rim = jnp.where(cell == at_rim, 1.0, 0.0).astype(BF16)
    gain_of = lambda gain: gain[...].reshape(1, D)
    wide_lane = lax.broadcasted_iota(jnp.int32, (48, 128), 1)
    masks = []
    wanted = []
    for col in range(COLS):
        pieces_in(col)
        blocks = [got[col][sources[col], c, PIECE - 1].astype(F32) for c in range(CHAN)]
        all_wanted = rim_wanted(blocks[0][0:8], blocks[0][8:16])
        for r in range(ROWS):
            slot = chan * ROWS + r
            wanted.append(
                jnp.sum(jnp.where(wide_lane == slot + FACE, all_wanted, 0.0), axis=1, keepdims=True)
            )
            pieces, column = [], []
            for c in range(CHAN):
                pieces.append(
                    jnp.concatenate([got[col][sources[col], c, r * 3 + part] for part in range(3)], axis=1)
                )
                column.append(jnp.sum(jnp.where(lane == slot, blocks[c], 0.0), axis=1, keepdims=True))
            values = jnp.concatenate(pieces, axis=0)
            mask = jnp.concatenate(column, axis=0)
            masks.append(mask)
            tile = col * ROWS + r
            own[tile * CELLS : (tile + 1) * CELLS] = values
            norm = (rms(values.astype(F32), gain_of(gain_image)) * mask).astype(BF16)
            normed[tile] = norm
            rims[(1 + col) * GRID_R + 1 + r] = jnp.dot(at_rim, norm, preferred_element_type=F32).astype(BF16)
        exchange(rims, rim_send, rim_recv, 0, col)
        for tile in range(col * ROWS, (col + 1) * ROWS):
            frame[tile, 1:9, 8:16, :] = normed[tile].astype(F32).reshape(SIDE, SIDE, D)

    loads[0].wait()
    arrived(rims, rim_send, rim_recv)

    rim_lane = lax.broadcasted_iota(jnp.int32, (48, SPOTS * RIM), 1).astype(F32)
    for part in range(0, ROWS, PART):
        for col in range(COLS):
            for r in range(part, part + PART):
                tile = col * ROWS + r
                at = part * COLS + col * PART + r - part
                chosen = jnp.where(rim_lane == wanted[tile], 1.0, 0.0).astype(BF16)
                rim = jnp.dot(chosen, rims[...].reshape(SPOTS * RIM, D), preferred_element_type=F32)
                frame[tile, 0, 8:16, :] = rim[0:8]
                frame[tile, 9, 8:16, :] = rim[8:16]
                for i in range(SIDE):
                    frame[tile, 1 + i, 7:8, :] = rim[16 + i : 17 + i]
                    frame[tile, 1 + i, 16:17, :] = rim[24 + i : 25 + i]
                frame[tile, 0, 7:8, :] = rim[32:33]
                frame[tile, 0, 16:17, :] = rim[33:34]
                frame[tile, 9, 7:8, :] = rim[34:35]
                frame[tile, 9, 16:17, :] = rim[35:36]
                for tap in range(9):
                    dr, dc = tap // 3, tap % 3
                    window = frame[tile, dr : dr + SIDE, 7 + dc : 7 + dc + SIDE, :]
                    patches[at * CELLS : (at + 1) * CELLS, tap * D : (tap + 1) * D] = window.reshape(
                        CELLS, D
                    ).astype(BF16)
        total = jnp.dot(
            patches[part * COLS * CELLS : (part + PART) * COLS * CELLS, :], conv[...], preferred_element_type=F32
        )
        for col in range(COLS):
            tile = col * ROWS + part
            rows = slice(tile * CELLS, (tile + PART) * CELLS)
            mine = total[col * PART * CELLS : (col + 1) * PART * CELLS]
            image = (own[rows, :].astype(F32) + mine).astype(BF16)
            after[rows, :] = image
            mask = jnp.concatenate(masks[tile : tile + PART], axis=0)
            attn = (rms(image.astype(F32), gain_of(gain_attn)) * mask).astype(BF16)
            spot = (1 + col) * GRID_R + 1 + part
            table[spot : spot + PART] = attn.reshape(PART, CELLS, D)
        exchange(table, halo_send, halo_recv, 1, part)

    def project(spot, many):
        rows = table[spot : spot + many].reshape(many * CELLS, D)
        found = jnp.dot(rows, qkv[:, D:], preferred_element_type=F32)
        memory[spot * CELLS : (spot + many) * CELLS, :] = found.astype(BF16)

    loads[1].wait()
    scale = 1.0 / math.sqrt(HEAD_DIM)
    for col in range(COLS):
        spot = (1 + col) * GRID_R + 1
        found = jnp.dot(
            table[spot : spot + ROWS].reshape(HALF, D), qkv[:, :D], preferred_element_type=F32
        )
        queries[col * HALF : (col + 1) * HALF, :] = (found * scale).astype(BF16)
        project(spot, ROWS)
    for load in loads[2:]:
        load.wait()
    arrived(table, halo_send, halo_recv)
    project(0, GRID_R + 1)
    project(GRID_R + ROWS + 1, 2)
    project(2 * GRID_R + ROWS + 1, GRID_R + 1)

    def heads_step(rows, first, lanes, base):
        heads = lanes // HEAD_DIM
        head = lax.broadcasted_iota(jnp.int32, (CELLS, lanes), 1) >> 6
        query = queries[rows, first : first + lanes]
        nothing = jnp.zeros_like(query)
        blocks = jnp.concatenate([jnp.where(head == h, query, nothing) for h in range(heads)], axis=0)
        spots = slice(base, base + 9 * CELLS)
        scores = lax.dot_general(
            blocks, keys[spots, first : first + lanes], (((1,), (1,)), ((), ())), preferred_element_type=F32
        )
        weights = jnp.exp(scores - jnp.max(scores, axis=-1, keepdims=True))
        total = jnp.sum(weights, axis=-1, keepdims=True)
        value = jnp.dot(
            weights.astype(BF16), keys[spots, D + first : D + first + lanes], preferred_element_type=F32
        )
        value = value / total
        found = value[:CELLS]
        for h in range(1, heads):
            found = jnp.where(head == h, value[h * CELLS : (h + 1) * CELLS], found)
        mixed[rows, first : first + lanes] = found.astype(BF16)

    returned = []
    for col in range(COLS):

        def attend(r):
            base_key = r % PART * 9 * CELLS
            for n in range(3):
                spot = (col + n) * GRID_R + r
                keys[base_key + n * 3 * CELLS : base_key + (n + 1) * 3 * CELLS, :] = memory[
                    spot * CELLS : (spot + 3) * CELLS, :
                ]
            rows = slice((col * ROWS + r) * CELLS, (col * ROWS + r + 1) * CELLS)
            heads_step(rows, 0, 4 * HEAD_DIM, base_key)
            heads_step(rows, 4 * HEAD_DIM, 2 * HEAD_DIM, base_key)

        for part in range(0, ROWS, PART):
            for r in range(part, part + PART):
                attend(r)
            rows = slice(col * HALF + part * CELLS, col * HALF + (part + PART) * CELLS)
            attended = jnp.dot(mixed[rows, :], proj[...], preferred_element_type=F32)
            attended = (after[rows, :].astype(F32) + attended).astype(BF16)
            wide = attended.astype(F32)
            hidden = jnp.dot(rms(wide, gain_of(gain_mlp)).astype(BF16), up[...], preferred_element_type=F32)
            hidden = (0.5 * hidden * (1.0 + lax.erf(hidden * (0.5**0.5)))).astype(BF16)
            encoded = wide + jnp.dot(hidden, down[...], preferred_element_type=F32)
            encoded = encoded.astype(BF16).reshape(PART, CHAN, 16, D)
            for r in range(PART):
                for c in range(CHAN):
                    tiles[col, c, part + r] = encoded[r, c]
            span = pl.ds(part, PART)
            for c in (2, 3, 1, 0):
                to = lax.rem(chan + c, CHAN)
                for step in range(GROUP):
                    target = lax.rem(rank + step, GROUP)
                    i = place * COLS + col - target
                    slot = limit(i, HELD - 1)
                    inside = (i >= 0) & (i < HELD)
                    if c == 0 and step == 0:
                        copy = pltpu.make_async_copy(
                            tiles.at[col, chan, span],
                            home.at[slot, chan, span],
                            local.at[COLS + (col * ROWS + part) // PART],
                        )
                    else:
                        copy = remote(
                            tiles.at[col, to, span],
                            home.at[slot, chan, span],
                            home_send.at[len(returned)],
                            home_recv.at[(slot * CHAN + chan) * (ROWS // PART) + part // PART],
                            (base + target, to),
                        )
                    when(inside, copy.start)
                    returned.append((copy, inside, c == 0 and step == 0))

    departed(rims, rim_send, rim_recv)
    departed(table, halo_send, halo_recv)
    for copy, needed in sent:
        when(needed, copy.wait_send)
    for copy, inside, stays_here in returned:
        when(inside, copy.wait if stays_here else copy.wait_send)
    for i in range(HELD):
        worker = snake((rank + i) // COLS)
        for c in range(CHAN):
            at = lax.rem(chan + c, CHAN)
            for part in range(0, ROWS, PART):
                span = pl.ds(part, PART)
                arrival = remote(
                    tiles.at[0, 0, span],
                    home.at[i, at, span],
                    home_send.at[0],
                    home_recv.at[(i * CHAN + at) * (ROWS // PART) + part // PART],
                    (device, at),
                )
                when(None if c else worker != rank, arrival.wait_recv)


def settle_kernel(where, home, out, columns, blank, come, go):
    shift, count = where[0], where[1]

    def fetch(i):
        return pltpu.make_async_copy(home.at[jnp.minimum(i + shift, HELD - 1)], columns.at[i], come.at[i])

    for i in range(HELD):
        pl.when(i < count)(fetch(i).start)
    blank[...] = jnp.zeros_like(blank)
    for i in range(HELD):

        @pl.when(i < count)
        def _():
            fetch(i).wait()
            pltpu.make_async_copy(columns.at[i], out.at[i], go.at[i]).start()

        @pl.when(i >= count)
        def _():
            pltpu.make_async_copy(blank, out.at[i], go.at[i]).start()

    for i in range(HELD):
        pltpu.make_async_copy(blank, out.at[i], go.at[i]).wait()


def per_device(
    latents,
    owner,
    neighbours,
    rotations,
    cell_mask,
    gain_image,
    conv_weight,
    gain_attn,
    qkv_weight,
    out_weight,
    gain_mlp,
    up_weight,
    down_weight,
):
    weights = [conv_weight, qkv_weight, out_weight, up_weight, down_weight]
    vmem = pltpu.VMEM
    dma = pltpu.SemaphoreType.DMA
    moves = 8 + 2 * COLS
    home, where = pl.pallas_call(
        block_kernel,
        out_shape=(
            jax.ShapeDtypeStruct((HELD, CHAN, ROWS, 16, D), BF16),
            jax.ShapeDtypeStruct((2,), jnp.int32),
        ),
        in_specs=[HBM] + [VMEM] * 3 + [HBM] + [VMEM] * 3 + [HBM] * 5,
        out_specs=(HBM, SMEM),
        scratch_shapes=[
            pltpu.SMEM((FACE * BAND,), jnp.int32),
            vmem((32, 128), jnp.int32),
            vmem((HELD, FACE, 16, D), BF16),
            vmem((HELD, CHAN, PIECE, 16, 128), BF16),
            vmem((GROUP, CHAN, PIECE, 16, 128), BF16),
            vmem((GROUP, CHAN, PIECE, 16, 128), BF16),
            vmem((OWN * CELLS, D), BF16),
            vmem((OWN, CELLS, D), BF16),
            vmem((HELD, FACE, 128), BF16),
            vmem((SPOTS, RIM, D), BF16),
            vmem((OWN, 10, 24, D), F32),
            vmem((OWN * CELLS, 9 * D), BF16),
            vmem((OWN * CELLS, D), BF16),
            vmem((SPOTS, CELLS, D), BF16),
            vmem((SPOTS * CELLS, 2 * D), BF16),
            vmem((OWN * CELLS, D), BF16),
            vmem((PART * 9 * CELLS, 2 * D), BF16),
            vmem((OWN * CELLS, D), BF16),
            vmem((COLS, CHAN, ROWS, 16, D), BF16),
            *[vmem(w.shape, BF16) for w in weights],
            dma((7,)),
            dma((HELD * CHAN,)),
            dma((GROUP * CHAN * COLS,)),
            dma((moves,)),
            dma((moves,)),
            dma((moves,)),
            dma((moves,)),
            dma((GROUP * CHAN * OWN // PART,)),
            dma((HELD * CHAN * ROWS // PART,)),
            dma((COLS + OWN // PART,)),
        ],
        compiler_params=pltpu.CompilerParams(
            collective_id=0, has_side_effects=True, vmem_limit_bytes=60 << 20
        ),
        name="encoder_block",
    )(
        owner,
        cell_mask.T,
        neighbours.T,
        rotations.T,
        latents.reshape(HELD, FACE, 16, D),
        gain_image,
        gain_attn,
        gain_mlp,
        *weights,
    )
    out = pl.pallas_call(
        settle_kernel,
        out_shape=jax.ShapeDtypeStruct((HELD, FACE, 16, D), BF16),
        in_specs=[SMEM, HBM],
        out_specs=HBM,
        scratch_shapes=[
            vmem((HELD, FACE, 16, D), BF16),
            vmem((FACE, 16, D), BF16),
            dma((HELD,)),
            dma((HELD,)),
        ],
        name="settle",
    )(where, home.reshape(HELD, FACE, 16, D))
    return out.reshape(SLOTS, 16, D)


def solution(mesh):
    in_specs = (
        P("tiles", "chan", None),
        P(),
        P("tiles", None),
        P("tiles", None),
        P("tiles", "chan"),
        P(),
        P(),
        P(),
        P(),
        P(),
        P(),
        P(),
        P(),
    )
    return jax.shard_map(
        per_device,
        mesh=mesh,
        in_specs=in_specs,
        out_specs=P("tiles", "chan", None),
        check_vma=False,
    )
```

```python
import math

import jax
import jax.numpy as jnp
from jax import lax
from jax.experimental import pallas as pl
from jax.experimental.pallas import tpu as pltpu
from jax.sharding import PartitionSpec as P

MESH = pl.DeviceIdType.MESH
VMEM = pl.BlockSpec(memory_space=pltpu.VMEM)
HBM = pl.BlockSpec(memory_space=pltpu.HBM)
F32, BF16 = jnp.float32, jnp.bfloat16

D = 384
FFN_UNITS = 1536
HEAD_DIM = 64
FACE = 16
BAND = 64
SIDE = 8
CELLS = 64
SLOTS = 80
HELD = 5
GROUP = 4
CHAN = 4
COLS = 2
ROWS = 4
OWN = COLS * ROWS
GRID_R, GRID_C = ROWS + 2, COLS + 2
SPOTS = GRID_R * GRID_C
HALF = ROWS * CELLS
PART = 2
RIM = 32
PIECE = ROWS * 3 + 1
epsilon = 1e-06


def rms(wide, gain):
    return wide * lax.rsqrt(jnp.mean(wide * wide, axis=-1, keepdims=True) + epsilon) * gain


def snake(q):
    return q // 2 * 2 + lax.rem(q + q // 2, 2)


def device_of(worker):
    base = worker // GROUP * GROUP
    return base + snake(worker - base)


def remote(src, dst, send, recv, device):
    return pltpu.make_async_remote_copy(
        src_ref=src, dst_ref=dst, send_sem=send, recv_sem=recv, device_id=device, device_id_type=MESH
    )


def neighbour_places(near, start, count):
    slot = lax.broadcasted_iota(jnp.int32, near.shape, 1)
    base = jnp.where(
        near < SLOTS,
        start,
        jnp.where(near < SLOTS + FACE, start - FACE - SLOTS, start + count - SLOTS - FACE),
    )
    tile = (near + base) & (FACE * BAND - 1)
    own_col = (start + slot) >> 4
    grid_row = (tile & 15) - (slot & 12) + 1
    grid_col = ((tile >> 4) - (own_col - (own_col & 1)) + 1) & (BAND - 1)
    grid_row = jnp.minimum(jnp.maximum(grid_row, 0), GRID_R - 1)
    grid_col = jnp.minimum(jnp.maximum(grid_col, 0), GRID_C - 1)
    return jnp.where(near < SLOTS + 2 * FACE, grid_col * GRID_R + grid_row, SPOTS)


def rim_wanted(near, turns):
    q = lax.broadcasted_iota(jnp.int32, (48, 128), 0)

    def pick(*values):
        found = values[7]
        for at, top in ((6, 35), (5, 34), (4, 33), (3, 32), (2, 24), (1, 16), (0, 8)):
            found = jnp.where(q < top, values[at], found)
        return found

    along = q & 7
    order = (1, 6, 3, 4, 0, 2, 5, 7)
    place = pick(*[near[n : n + 1] for n in order])
    turn = pick(*[turns[n : n + 1] for n in order])
    i = pick(7, 0, along, along, 7, 7, 0, 0)
    j = pick(along, along, 7, 0, 7, 0, 7, 0)

    def turned(a, b, c, d):
        return jnp.where(turn < 0.5, a, jnp.where(turn < 1.5, b, jnp.where(turn < 2.5, c, d)))

    from_row = turned(i, j, 7 - i, 7 - j)
    from_col = turned(j, 7 - i, 7 - j, i)
    rim = jnp.where(
        from_row == 0,
        from_col,
        jnp.where(from_row == 7, 8 + from_col, jnp.where(from_col == 0, 16 + from_row, 24 + from_row)),
    )
    return jnp.where(q < 36, place * RIM + rim.astype(F32), float(SPOTS * RIM))


def halo_moves(device, chan, base, rank):
    worker = base + snake(rank)
    total = lax.axis_size("tiles")
    left = device_of(lax.rem(worker + total - 1, total))
    right = device_of(lax.rem(worker + 1, total))
    up, down = chan > 0, chan < CHAN - 1
    above, below = lax.rem(chan + CHAN - 1, CHAN), lax.rem(chan + 1, CHAN)
    first, second, third = GRID_R, 2 * GRID_R, 3 * GRID_R
    last = ROWS - PART
    moves = [
        (first + 1, third + 1, PART, (0, 0), (left, chan), None, None),
        (second + 1, 1, PART, (1, 0), (right, chan), None, None),
        (first + 1 + last, third + 1 + last, PART, (0, last), (left, chan), None, None),
        (second + 1 + last, 1 + last, PART, (1, last), (right, chan), None, None),
        (first + 1, third + ROWS + 1, 1, (0, 0), (left, above), up, down),
        (first + ROWS, third, 1, (0, last), (left, below), down, up),
        (first + 1, first + ROWS + 1, 1, (0, 0), (device, above), up, down),
        (first + ROWS, first, 1, (0, last), (device, below), down, up),
        (second + 1, ROWS + 1, 1, (1, 0), (right, above), up, down),
        (second + ROWS, 0, 1, (1, last), (right, below), down, up),
        (second + 1, second + ROWS + 1, 1, (1, 0), (device, above), up, down),
        (second + ROWS, second, 1, (1, last), (device, below), down, up),
    ]
    return moves, (left, right, above, below)


def when(condition, action):
    if condition is None:
        action()
    else:
        pl.when(condition)(action)


def block_kernel(
    owner_hbm,
    mask_hbm,
    near_hbm,
    turn_hbm,
    latents,
    image_hbm,
    attn_hbm,
    mlp_hbm,
    conv_hbm,
    qkv_hbm,
    proj_hbm,
    up_hbm,
    down_hbm,
    out,
    owner,
    mask_in,
    near_in,
    turn_in,
    gain_image,
    gain_attn,
    gain_mlp,
    home,
    raw,
    held,
    payload,
    got_first,
    got_second,
    own,
    normed,
    marks,
    rims,
    frame,
    patches,
    after,
    table,
    memory,
    queries,
    keys,
    mixed,
    tiles,
    conv,
    qkv,
    proj,
    up,
    down,
    load_sem,
    spread_send,
    spread_recv,
    rim_send,
    rim_recv,
    halo_send,
    halo_recv,
    home_send,
    home_recv,
    local,
):
    device, chan = lax.axis_index("tiles"), lax.axis_index("chan")
    rank = lax.rem(device, GROUP)
    base = device - rank
    place = snake(rank)
    moves, (left, right, above, below) = halo_moves(device, chan, base, rank)

    got = (got_first, got_second)
    owner_load = pltpu.make_async_copy(owner_hbm, owner, load_sem.at[6])
    owner_load.start()
    small_loads = []
    for at, (src, dst) in enumerate(
        [
            (mask_hbm, mask_in),
            (near_hbm, near_in),
            (turn_hbm, turn_in),
            (image_hbm, gain_image),
            (attn_hbm, gain_attn),
            (mlp_hbm, gain_mlp),
        ]
    ):
        small_loads.append(pltpu.make_async_copy(src, dst, load_sem.at[7 + at]))
        small_loads[-1].start()
    first_load = pltpu.make_async_copy(latents, held, load_sem.at[0])
    first_load.start()
    loads = []
    for at, (src, dst) in enumerate(
        [(conv_hbm, conv), (qkv_hbm, qkv), (proj_hbm, proj), (up_hbm, up), (down_hbm, down)]
    ):
        loads.append(pltpu.make_async_copy(src, dst, load_sem.at[1 + at]))

    barrier = pltpu.get_barrier_semaphore()
    partners = []
    for step in range(1, GROUP * CHAN):
        other = lax.rem(rank * CHAN + chan + step, GROUP * CHAN)
        partners.append((base + other // CHAN, lax.rem(other, CHAN)))
    for side in (left, right):
        partners += [(side, chan), (side, above), (side, below)]
    for partner in partners:
        pl.semaphore_signal(barrier, inc=1, device_id=partner, device_id_type=MESH)

    def count_columns(col, carry):
        start, count = carry
        holder = owner[col * FACE]
        return (
            start + jnp.where(holder < device, 1, 0),
            count + jnp.where(holder == device, 1, 0),
        )

    owner_load.wait()
    start, count = lax.fori_loop(0, BAND, count_columns, (jnp.int32(0), jnp.int32(0)))
    limit = lambda value, top: jnp.minimum(jnp.maximum(value, 0), top)
    shift = limit(start - base * COLS - rank, HELD - 1)
    sources = [
        limit(owner[((base + place) * COLS + col) * FACE] - base, GROUP - 1) for col in range(COLS)
    ]

    for load in small_loads:
        load.wait()
    raw[...] = jnp.zeros_like(raw)
    raw[0:16, 0:SLOTS] = mask_in[...]
    raw[16:24, 0:SLOTS] = near_in[...]
    raw[24:32, 0:SLOTS] = turn_in[...]
    lane = lax.broadcasted_iota(jnp.int32, (16, 128), 1)
    mask_rows = raw[0:16].astype(F32)
    near_rows = neighbour_places(raw[16:24], start * FACE, count * FACE).astype(F32)
    near_rows = jnp.concatenate([near_rows, raw[24:32].astype(F32)], axis=0)
    for i in range(HELD):
        cells = pltpu.roll(mask_rows, (128 - i * FACE) % 128, axis=1)
        near = pltpu.roll(near_rows, (128 + FACE - i * FACE) % 128, axis=1)
        marks[i] = jnp.where(lane < FACE, cells, near).astype(BF16)
    first_load.wait()

    def fill(i):
        col = lax.rem(i + HELD - shift, HELD)
        for c in range(CHAN):
            for r in range(ROWS):
                for part in range(3):
                    payload[i, c, r * 3 + part] = held[col, c * ROWS + r, :, part * 128 : (part + 1) * 128]
            payload[i, c, PIECE - 1] = marks[col]

    sent = []
    for step in range(HELD):
        i = lax.rem(2 * step + lax.rem(rank, 2), HELD)
        fill(i)
        if step == 0:
            pl.semaphore_wait(barrier, len(partners))
        target = snake((rank + i) // COLS)
        odd = lax.rem(rank, 2) == 1
        for c in (2, 3, 1, 0):
            to = lax.rem(chan + c, CHAN)
            away = None if c else target != rank
            for col in range(COLS):
                if step == 2:
                    needed = odd if col else jnp.logical_not(odd)
                    needed = needed if away is None else needed & away
                elif (step > 2) == (col == 1):
                    needed = away
                else:
                    continue
                copy = remote(
                    payload.at[i, to],
                    got[col].at[rank, chan],
                    spread_send.at[step * CHAN + c],
                    spread_recv.at[(rank * CHAN + chan) * COLS + col],
                    (base + target, to),
                )
                when(needed, copy.start)
                sent.append((copy, needed))
    stays = []
    for col in range(COLS):
        i = place * COLS + col - rank
        copy = pltpu.make_async_copy(
            payload.at[limit(i, HELD - 1), chan], got[col].at[rank, chan], local.at[col]
        )
        inside = (i >= 0) & (i < HELD)
        when(inside, copy.start)
        stays.append((copy, inside))
    for load in loads:
        load.start()
    beyond = jnp.zeros((RIM, D), BF16)
    for col in range(GRID_C):

        @pl.when(chan == 0)
        def _():
            rims[col * GRID_R] = beyond
            for part in range(2):
                table[col * GRID_R, part * RIM : (part + 1) * RIM] = beyond

        @pl.when(chan == CHAN - 1)
        def _():
            rims[(col + 1) * GRID_R - 1] = beyond
            for part in range(2):
                table[(col + 1) * GRID_R - 1, part * RIM : (part + 1) * RIM] = beyond

    def exchange(buffer, send, recv, kind, which):
        for at, (src, dst, many, ready, to, needed, _) in enumerate(moves):
            if ready[kind] == which:
                copy = remote(
                    buffer.at[pl.ds(src, many)], buffer.at[pl.ds(dst, many)], send.at[at], recv.at[at], to
                )
                when(needed, copy.start)

    def arrived(buffer, send, recv):
        for at, (src, dst, many, _, to, needed, coming) in enumerate(moves):
            copy = remote(
                buffer.at[pl.ds(src, many)], buffer.at[pl.ds(dst, many)], send.at[at], recv.at[at], to
            )
            when(coming, copy.wait_recv)

    def departed(buffer, send, recv):
        for at, (src, dst, many, _, to, needed, _) in enumerate(moves):
            copy = remote(
                buffer.at[pl.ds(src, many)], buffer.at[pl.ds(dst, many)], send.at[at], recv.at[at], to
            )
            when(needed, copy.wait_send)

    def pieces_in(col):
        for step in range(GROUP):
            source = lax.rem(rank + step, GROUP)
            far = place * COLS + col - source
            for c in range(CHAN):
                at = lax.rem(chan + c, CHAN)
                if step == 0 and c == 0:
                    when(stays[col][1], stays[col][0].wait)
                else:
                    arrival = remote(
                        payload.at[0, 0],
                        got[col].at[source, at],
                        spread_send.at[0],
                        spread_recv.at[(source * CHAN + at) * COLS + col],
                        (device, at),
                    )
                    when((far >= 0) & (far < HELD), arrival.wait_recv)

    row = lax.broadcasted_iota(jnp.int32, (RIM, CELLS), 0)
    cell = lax.broadcasted_iota(jnp.int32, (RIM, CELLS), 1)
    edge, along = row >> 3, row & 7
    at_rim = jnp.where(
        edge == 0, along, jnp.where(edge == 1, 56 + along, jnp.where(edge == 2, along * 8, along * 8 + 7))
    )
    at_rim = jnp.where(cell == at_rim, 1.0, 0.0).astype(BF16)
    gain_of = lambda gain: gain[...].reshape(1, D)
    wide_lane = lax.broadcasted_iota(jnp.int32, (48, 128), 1)
    masks = []
    wanted = []
    for col in range(COLS):
        pieces_in(col)
        blocks = [got[col][sources[col], c, PIECE - 1].astype(F32) for c in range(CHAN)]
        for r in range(ROWS):
            slot = chan * ROWS + r
            pieces, column = [], []
            for c in range(CHAN):
                pieces.append(
                    jnp.concatenate([got[col][sources[col], c, r * 3 + part] for part in range(3)], axis=1)
                )
                column.append(jnp.sum(jnp.where(lane == slot, blocks[c], 0.0), axis=1, keepdims=True))
            values = jnp.concatenate(pieces, axis=0)
            mask = jnp.concatenate(column, axis=0)
            masks.append(mask)
            tile = col * ROWS + r
            own[tile * CELLS : (tile + 1) * CELLS] = values
            norm = (rms(values.astype(F32), gain_of(gain_image)) * mask).astype(BF16)
            normed[tile] = norm
            rims[(1 + col) * GRID_R + 1 + r] = jnp.dot(at_rim, norm, preferred_element_type=F32).astype(BF16)
        exchange(rims, rim_send, rim_recv, 0, col)
        all_wanted = rim_wanted(blocks[0][0:8], blocks[0][8:16])
        for r in range(ROWS):
            slot = chan * ROWS + r + FACE
            wanted.append(jnp.sum(jnp.where(wide_lane == slot, all_wanted, 0.0), axis=1, keepdims=True))
        for tile in range(col * ROWS, (col + 1) * ROWS):
            frame[tile, 1:9, 8:16, :] = normed[tile].astype(F32).reshape(SIDE, SIDE, D)

    loads[0].wait()
    arrived(rims, rim_send, rim_recv)

    rim_lane = lax.broadcasted_iota(jnp.int32, (48, SPOTS * RIM), 1).astype(F32)
    for part in range(0, ROWS, PART):
        for col in range(COLS):
            for r in range(part, part + PART):
                tile = col * ROWS + r
                at = part * COLS + col * PART + r - part
                chosen = jnp.where(rim_lane == wanted[tile], 1.0, 0.0).astype(BF16)
                rim = jnp.dot(chosen, rims[...].reshape(SPOTS * RIM, D), preferred_element_type=F32)
                frame[tile, 0, 8:16, :] = rim[0:8]
                frame[tile, 9, 8:16, :] = rim[8:16]
                for i in range(SIDE):
                    frame[tile, 1 + i, 7:8, :] = rim[16 + i : 17 + i]
                    frame[tile, 1 + i, 16:17, :] = rim[24 + i : 25 + i]
                frame[tile, 0, 7:8, :] = rim[32:33]
                frame[tile, 0, 16:17, :] = rim[33:34]
                frame[tile, 9, 7:8, :] = rim[34:35]
                frame[tile, 9, 16:17, :] = rim[35:36]
                for tap in range(9):
                    dr, dc = tap // 3, tap % 3
                    window = frame[tile, dr : dr + SIDE, 7 + dc : 7 + dc + SIDE, :]
                    patches[at * CELLS : (at + 1) * CELLS, tap * D : (tap + 1) * D] = window.reshape(
                        CELLS, D
                    ).astype(BF16)
        total = jnp.dot(
            patches[part * COLS * CELLS : (part + PART) * COLS * CELLS, :], conv[...], preferred_element_type=F32
        )
        for col in range(COLS):
            tile = col * ROWS + part
            rows = slice(tile * CELLS, (tile + PART) * CELLS)
            mine = total[col * PART * CELLS : (col + 1) * PART * CELLS]
            image = (own[rows, :].astype(F32) + mine).astype(BF16)
            after[rows, :] = image
            mask = jnp.concatenate(masks[tile : tile + PART], axis=0)
            attn = (rms(image.astype(F32), gain_of(gain_attn)) * mask).astype(BF16)
            spot = (1 + col) * GRID_R + 1 + part
            table[spot : spot + PART] = attn.reshape(PART, CELLS, D)
        exchange(table, halo_send, halo_recv, 1, part)

    def project(spot, many):
        rows = table[spot : spot + many].reshape(many * CELLS, D)
        found = jnp.dot(rows, qkv[:, D:], preferred_element_type=F32)
        memory[spot * CELLS : (spot + many) * CELLS, :] = found.astype(BF16)

    loads[1].wait()
    scale = 1.0 / math.sqrt(HEAD_DIM)
    for col in range(COLS):
        spot = (1 + col) * GRID_R + 1
        found = jnp.dot(
            table[spot : spot + ROWS].reshape(HALF, D), qkv[:, :D], preferred_element_type=F32
        )
        queries[col * HALF : (col + 1) * HALF, :] = (found * scale).astype(BF16)
        project(spot, ROWS)
    for load in loads[2:]:
        load.wait()
    arrived(table, halo_send, halo_recv)
    project(0, GRID_R + 1)
    project(GRID_R + ROWS + 1, 2)
    project(2 * GRID_R + ROWS + 1, GRID_R + 1)

    def heads_step(rows, first, lanes, base):
        heads = lanes // HEAD_DIM
        head = lax.broadcasted_iota(jnp.int32, (CELLS, lanes), 1) >> 6
        query = queries[rows, first : first + lanes]
        nothing = jnp.zeros_like(query)
        blocks = jnp.concatenate([jnp.where(head == h, query, nothing) for h in range(heads)], axis=0)
        spots = slice(base, base + 9 * CELLS)
        scores = lax.dot_general(
            blocks, keys[spots, first : first + lanes], (((1,), (1,)), ((), ())), preferred_element_type=F32
        )
        weights = jnp.exp(scores - jnp.max(scores, axis=-1, keepdims=True))
        total = jnp.sum(weights, axis=-1, keepdims=True)
        value = jnp.dot(
            weights.astype(BF16), keys[spots, D + first : D + first + lanes], preferred_element_type=F32
        )
        value = value / total
        found = value[:CELLS]
        for h in range(1, heads):
            found = jnp.where(head == h, value[h * CELLS : (h + 1) * CELLS], found)
        mixed[rows, first : first + lanes] = found.astype(BF16)

    returned = []
    for col in range(COLS):

        def attend(r):
            base_key = r % PART * 9 * CELLS
            for n in range(3):
                spot = (col + n) * GRID_R + r
                keys[base_key + n * 3 * CELLS : base_key + (n + 1) * 3 * CELLS, :] = memory[
                    spot * CELLS : (spot + 3) * CELLS, :
                ]
            rows = slice((col * ROWS + r) * CELLS, (col * ROWS + r + 1) * CELLS)
            heads_step(rows, 0, 4 * HEAD_DIM, base_key)
            heads_step(rows, 4 * HEAD_DIM, 2 * HEAD_DIM, base_key)

        for part in range(0, ROWS, PART):
            for r in range(part, part + PART):
                attend(r)
            rows = slice(col * HALF + part * CELLS, col * HALF + (part + PART) * CELLS)
            attended = jnp.dot(mixed[rows, :], proj[...], preferred_element_type=F32)
            attended = (after[rows, :].astype(F32) + attended).astype(BF16)
            wide = attended.astype(F32)
            hidden = jnp.dot(rms(wide, gain_of(gain_mlp)).astype(BF16), up[...], preferred_element_type=F32)
            hidden = (0.5 * hidden * (1.0 + lax.erf(hidden * (0.5**0.5)))).astype(BF16)
            encoded = wide + jnp.dot(hidden, down[...], preferred_element_type=F32)
            encoded = encoded.astype(BF16).reshape(PART, CHAN, 16, D)
            for r in range(PART):
                for c in range(CHAN):
                    tiles[col, c, part + r] = encoded[r, c]
            span = pl.ds(part, PART)
            for c in (2, 3, 1, 0):
                to = lax.rem(chan + c, CHAN)
                for step in range(GROUP):
                    target = lax.rem(rank + step, GROUP)
                    i = place * COLS + col - target
                    slot = limit(i, HELD - 1)
                    inside = (i >= 0) & (i < HELD)
                    if c == 0 and step == 0:
                        copy = pltpu.make_async_copy(
                            tiles.at[col, chan, span],
                            home.at[slot, chan, span],
                            local.at[COLS + (col * ROWS + part) // PART],
                        )
                    else:
                        copy = remote(
                            tiles.at[col, to, span],
                            home.at[slot, chan, span],
                            home_send.at[len(returned)],
                            home_recv.at[(slot * CHAN + chan) * (ROWS // PART) + part // PART],
                            (base + target, to),
                        )
                    when(inside, copy.start)
                    returned.append((copy, inside, c == 0 and step == 0))

    for i in range(HELD):
        worker = snake((rank + i) // COLS)
        for c in range(CHAN):
            at = lax.rem(chan + c, CHAN)
            for part in range(0, ROWS, PART):
                span = pl.ds(part, PART)
                arrival = remote(
                    tiles.at[0, 0, span],
                    home.at[i, at, span],
                    home_send.at[0],
                    home_recv.at[(i * CHAN + at) * (ROWS // PART) + part // PART],
                    (device, at),
                )
                when(None if c else worker != rank, arrival.wait_recv)

    departed(rims, rim_send, rim_recv)
    departed(table, halo_send, halo_recv)
    for copy, needed in sent:
        when(needed, copy.wait_send)
    for copy, inside, stays_here in returned:
        when(inside, copy.wait if stays_here else copy.wait_send)
    for i in range(HELD):
        column = limit(i + shift, HELD - 1)
        for c in range(CHAN):
            for r in range(ROWS):
                values = home[column, c, r]
                out[i, c * ROWS + r] = lax.select(i < count, values, jnp.zeros_like(values))


def per_device(
    latents,
    owner,
    neighbours,
    rotations,
    cell_mask,
    gain_image,
    conv_weight,
    gain_attn,
    qkv_weight,
    out_weight,
    gain_mlp,
    up_weight,
    down_weight,
):
    weights = [conv_weight, qkv_weight, out_weight, up_weight, down_weight]
    vmem = pltpu.VMEM
    dma = pltpu.SemaphoreType.DMA
    moves = 8 + 2 * COLS
    out = pl.pallas_call(
        block_kernel,
        out_shape=jax.ShapeDtypeStruct((HELD, FACE, 16, D), BF16),
        in_specs=[HBM] * 13,
        out_specs=VMEM,
        scratch_shapes=[
            pltpu.SMEM((FACE * BAND,), jnp.int32),
            vmem((16, SLOTS), jnp.int32),
            vmem((8, SLOTS), jnp.int32),
            vmem((8, SLOTS), jnp.int32),
            vmem((D,), F32),
            vmem((D,), F32),
            vmem((D,), F32),
            vmem((HELD, CHAN, ROWS, 16, D), BF16),
            vmem((32, 128), jnp.int32),
            vmem((HELD, FACE, 16, D), BF16),
            vmem((HELD, CHAN, PIECE, 16, 128), BF16),
            vmem((GROUP, CHAN, PIECE, 16, 128), BF16),
            vmem((GROUP, CHAN, PIECE, 16, 128), BF16),
            vmem((OWN * CELLS, D), BF16),
            vmem((OWN, CELLS, D), BF16),
            vmem((HELD, FACE, 128), BF16),
            vmem((SPOTS, RIM, D), BF16),
            vmem((OWN, 10, 24, D), F32),
            vmem((OWN * CELLS, 9 * D), BF16),
            vmem((OWN * CELLS, D), BF16),
            vmem((SPOTS, CELLS, D), BF16),
            vmem((SPOTS * CELLS, 2 * D), BF16),
            vmem((OWN * CELLS, D), BF16),
            vmem((PART * 9 * CELLS, 2 * D), BF16),
            vmem((OWN * CELLS, D), BF16),
            vmem((COLS, CHAN, ROWS, 16, D), BF16),
            *[vmem(w.shape, BF16) for w in weights],
            dma((13,)),
            dma((HELD * CHAN,)),
            dma((GROUP * CHAN * COLS,)),
            dma((moves,)),
            dma((moves,)),
            dma((moves,)),
            dma((moves,)),
            dma((GROUP * CHAN * OWN // PART,)),
            dma((HELD * CHAN * ROWS // PART,)),
            dma((COLS + OWN // PART,)),
        ],
        compiler_params=pltpu.CompilerParams(
            collective_id=0, has_side_effects=True, vmem_limit_bytes=60 << 20
        ),
        name="encoder_block",
    )(
        owner,
        cell_mask.T,
        neighbours.T,
        rotations.T,
        latents.reshape(HELD, FACE, 16, D),
        gain_image,
        gain_attn,
        gain_mlp,
        *weights,
    )
    return out.reshape(SLOTS, 16, D)


def solution(mesh):
    in_specs = (
        P("tiles", "chan", None),
        P(),
        P("tiles", None),
        P("tiles", None),
        P("tiles", "chan"),
        P(),
        P(),
        P(),
        P(),
        P(),
        P(),
        P(),
        P(),
    )
    return jax.shard_map(
        per_device,
        mesh=mesh,
        in_specs=in_specs,
        out_specs=P("tiles", "chan", None),
        check_vma=False,
    )
```

```python
import math

import jax
import jax.numpy as jnp
from jax import lax
from jax.experimental import pallas as pl
from jax.experimental.pallas import tpu as pltpu
from jax.sharding import PartitionSpec as P

MESH = pl.DeviceIdType.MESH
VMEM = pl.BlockSpec(memory_space=pltpu.VMEM)
HBM = pl.BlockSpec(memory_space=pltpu.HBM)
F32, BF16 = jnp.float32, jnp.bfloat16

D = 384
FFN_UNITS = 1536
HEAD_DIM = 64
FACE = 16
BAND = 64
SIDE = 8
CELLS = 64
SLOTS = 80
HELD = 5
GROUP = 4
CHAN = 4
COLS = 2
ROWS = 4
OWN = COLS * ROWS
GRID_R, GRID_C = ROWS + 2, COLS + 2
SPOTS = GRID_R * GRID_C
HALF = ROWS * CELLS
PART = 2
RIM = 32
PIECE = ROWS * 3 + 1
epsilon = 1e-06


def rms(wide, gain):
    return wide * lax.rsqrt(jnp.mean(wide * wide, axis=-1, keepdims=True) + epsilon) * gain


def snake(q):
    return q // 2 * 2 + lax.rem(q + q // 2, 2)


def device_of(worker):
    base = worker // GROUP * GROUP
    return base + snake(worker - base)


def remote(src, dst, send, recv, device):
    return pltpu.make_async_remote_copy(
        src_ref=src, dst_ref=dst, send_sem=send, recv_sem=recv, device_id=device, device_id_type=MESH
    )


def neighbour_places(near, start, count):
    slot = lax.broadcasted_iota(jnp.int32, near.shape, 1)
    base = jnp.where(
        near < SLOTS,
        start,
        jnp.where(near < SLOTS + FACE, start - FACE - SLOTS, start + count - SLOTS - FACE),
    )
    tile = (near + base) & (FACE * BAND - 1)
    own_col = (start + slot) >> 4
    grid_row = (tile & 15) - (slot & 12) + 1
    grid_col = ((tile >> 4) - (own_col - (own_col & 1)) + 1) & (BAND - 1)
    grid_row = jnp.minimum(jnp.maximum(grid_row, 0), GRID_R - 1)
    grid_col = jnp.minimum(jnp.maximum(grid_col, 0), GRID_C - 1)
    return jnp.where(near < SLOTS + 2 * FACE, grid_col * GRID_R + grid_row, SPOTS)


def rim_wanted(near, turns):
    q = lax.broadcasted_iota(jnp.int32, (48, 128), 0)

    def pick(*values):
        found = values[7]
        for at, top in ((6, 35), (5, 34), (4, 33), (3, 32), (2, 24), (1, 16), (0, 8)):
            found = jnp.where(q < top, values[at], found)
        return found

    along = q & 7
    order = (1, 6, 3, 4, 0, 2, 5, 7)
    place = pick(*[near[n : n + 1] for n in order])
    turn = pick(*[turns[n : n + 1] for n in order])
    i = pick(7, 0, along, along, 7, 7, 0, 0)
    j = pick(along, along, 7, 0, 7, 0, 7, 0)

    def turned(a, b, c, d):
        return jnp.where(turn < 0.5, a, jnp.where(turn < 1.5, b, jnp.where(turn < 2.5, c, d)))

    from_row = turned(i, j, 7 - i, 7 - j)
    from_col = turned(j, 7 - i, 7 - j, i)
    rim = jnp.where(
        from_row == 0,
        from_col,
        jnp.where(from_row == 7, 8 + from_col, jnp.where(from_col == 0, 16 + from_row, 24 + from_row)),
    )
    return jnp.where(q < 36, place * RIM + rim.astype(F32), float(SPOTS * RIM))


def halo_moves(device, chan, base, rank):
    worker = base + snake(rank)
    total = lax.axis_size("tiles")
    left = device_of(lax.rem(worker + total - 1, total))
    right = device_of(lax.rem(worker + 1, total))
    up, down = chan > 0, chan < CHAN - 1
    above, below = lax.rem(chan + CHAN - 1, CHAN), lax.rem(chan + 1, CHAN)
    first, second, third = GRID_R, 2 * GRID_R, 3 * GRID_R
    last = ROWS - PART
    moves = [
        (first + 1, third + 1, PART, (0, 0), (left, chan), None, None),
        (second + 1, 1, PART, (1, 0), (right, chan), None, None),
        (first + 1 + last, third + 1 + last, PART, (0, last), (left, chan), None, None),
        (second + 1 + last, 1 + last, PART, (1, last), (right, chan), None, None),
        (first + 1, third + ROWS + 1, 1, (0, 0), (left, above), up, down),
        (first + ROWS, third, 1, (0, last), (left, below), down, up),
        (first + 1, first + ROWS + 1, 1, (0, 0), (device, above), up, down),
        (first + ROWS, first, 1, (0, last), (device, below), down, up),
        (second + 1, ROWS + 1, 1, (1, 0), (right, above), up, down),
        (second + ROWS, 0, 1, (1, last), (right, below), down, up),
        (second + 1, second + ROWS + 1, 1, (1, 0), (device, above), up, down),
        (second + ROWS, second, 1, (1, last), (device, below), down, up),
    ]
    return moves, (left, right, above, below)


def when(condition, action):
    if condition is None:
        action()
    else:
        pl.when(condition)(action)


def block_kernel(
    owner_hbm,
    mask_hbm,
    near_hbm,
    turn_hbm,
    latents,
    image_hbm,
    attn_hbm,
    mlp_hbm,
    conv_hbm,
    qkv_hbm,
    proj_hbm,
    up_hbm,
    down_hbm,
    out,
    filled,
    owner,
    mask_in,
    near_in,
    turn_in,
    gain_image,
    gain_attn,
    gain_mlp,
    home,
    raw,
    held,
    payload,
    got_first,
    got_second,
    own,
    normed,
    marks,
    rims,
    frame,
    patches,
    after,
    table,
    memory,
    queries,
    keys,
    mixed,
    tiles,
    conv,
    qkv,
    proj,
    up,
    down,
    load_sem,
    spread_send,
    spread_recv,
    rim_send,
    rim_recv,
    halo_send,
    halo_recv,
    home_send,
    home_recv,
    local,
):
    device, chan = lax.axis_index("tiles"), lax.axis_index("chan")
    rank = lax.rem(device, GROUP)
    base = device - rank
    place = snake(rank)
    moves, (left, right, above, below) = halo_moves(device, chan, base, rank)

    got = (got_first, got_second)
    owner_load = pltpu.make_async_copy(owner_hbm, owner, load_sem.at[6])
    owner_load.start()
    small_loads = []
    for at, (src, dst) in enumerate(
        [
            (mask_hbm, mask_in),
            (near_hbm, near_in),
            (turn_hbm, turn_in),
            (image_hbm, gain_image),
            (attn_hbm, gain_attn),
            (mlp_hbm, gain_mlp),
        ]
    ):
        small_loads.append(pltpu.make_async_copy(src, dst, load_sem.at[7 + at]))
        small_loads[-1].start()
    first_load = pltpu.make_async_copy(latents, held, load_sem.at[0])
    first_load.start()
    loads = []
    for at, (src, dst) in enumerate(
        [(conv_hbm, conv), (qkv_hbm, qkv), (proj_hbm, proj), (up_hbm, up), (down_hbm, down)]
    ):
        loads.append(pltpu.make_async_copy(src, dst, load_sem.at[1 + at]))

    barrier = pltpu.get_barrier_semaphore()
    partners = []
    for step in range(1, GROUP * CHAN):
        other = lax.rem(rank * CHAN + chan + step, GROUP * CHAN)
        partners.append((base + other // CHAN, lax.rem(other, CHAN)))
    for side in (left, right):
        partners += [(side, chan), (side, above), (side, below)]
    for partner in partners:
        pl.semaphore_signal(barrier, inc=1, device_id=partner, device_id_type=MESH)

    def count_columns(col, carry):
        start, count = carry
        holder = owner[col * FACE]
        return (
            start + jnp.where(holder < device, 1, 0),
            count + jnp.where(holder == device, 1, 0),
        )

    owner_load.wait()
    start, count = lax.fori_loop(0, BAND, count_columns, (jnp.int32(0), jnp.int32(0)))
    limit = lambda value, top: jnp.minimum(jnp.maximum(value, 0), top)
    shift = limit(start - base * COLS - rank, HELD - 1)
    filled[0] = count * FACE
    sources = [
        limit(owner[((base + place) * COLS + col) * FACE] - base, GROUP - 1) for col in range(COLS)
    ]

    for load in small_loads:
        load.wait()
    raw[...] = jnp.zeros_like(raw)
    raw[0:16, 0:SLOTS] = mask_in[...]
    raw[16:24, 0:SLOTS] = near_in[...]
    raw[24:32, 0:SLOTS] = turn_in[...]
    lane = lax.broadcasted_iota(jnp.int32, (16, 128), 1)
    mask_rows = raw[0:16].astype(F32)
    near_rows = neighbour_places(raw[16:24], start * FACE, count * FACE).astype(F32)
    near_rows = jnp.concatenate([near_rows, raw[24:32].astype(F32)], axis=0)
    for i in range(HELD):
        cells = pltpu.roll(mask_rows, (128 - i * FACE) % 128, axis=1)
        near = pltpu.roll(near_rows, (128 + FACE - i * FACE) % 128, axis=1)
        marks[i] = jnp.where(lane < FACE, cells, near).astype(BF16)
    first_load.wait()

    def fill(i):
        col = lax.rem(i + HELD - shift, HELD)
        for c in range(CHAN):
            for r in range(ROWS):
                for part in range(3):
                    payload[i, c, r * 3 + part] = held[col, c * ROWS + r, :, part * 128 : (part + 1) * 128]
            payload[i, c, PIECE - 1] = marks[col]

    sent = []
    for step in range(HELD):
        i = lax.rem(2 * step + lax.rem(rank, 2), HELD)
        fill(i)
        if step == 0:
            pl.semaphore_wait(barrier, len(partners))
        target = snake((rank + i) // COLS)
        odd = lax.rem(rank, 2) == 1
        for c in (2, 3, 1, 0):
            to = lax.rem(chan + c, CHAN)
            away = None if c else target != rank
            for col in range(COLS):
                if step == 2:
                    needed = odd if col else jnp.logical_not(odd)
                    needed = needed if away is None else needed & away
                elif (step > 2) == (col == 1):
                    needed = away
                else:
                    continue
                copy = remote(
                    payload.at[i, to],
                    got[col].at[rank, chan],
                    spread_send.at[step * CHAN + c],
                    spread_recv.at[(rank * CHAN + chan) * COLS + col],
                    (base + target, to),
                )
                when(needed, copy.start)
                sent.append((copy, needed))
    stays = []
    for col in range(COLS):
        i = place * COLS + col - rank
        copy = pltpu.make_async_copy(
            payload.at[limit(i, HELD - 1), chan], got[col].at[rank, chan], local.at[col]
        )
        inside = (i >= 0) & (i < HELD)
        when(inside, copy.start)
        stays.append((copy, inside))
    for load in loads:
        load.start()
    beyond = jnp.zeros((RIM, D), BF16)
    for col in range(GRID_C):

        @pl.when(chan == 0)
        def _():
            rims[col * GRID_R] = beyond
            for part in range(2):
                table[col * GRID_R, part * RIM : (part + 1) * RIM] = beyond

        @pl.when(chan == CHAN - 1)
        def _():
            rims[(col + 1) * GRID_R - 1] = beyond
            for part in range(2):
                table[(col + 1) * GRID_R - 1, part * RIM : (part + 1) * RIM] = beyond

    def exchange(buffer, send, recv, cols, part):
        for at, (src, dst, many, ready, to, needed, _) in enumerate(moves):
            if ready[0] in cols and ready[1] == part:
                copy = remote(
                    buffer.at[pl.ds(src, many)], buffer.at[pl.ds(dst, many)], send.at[at], recv.at[at], to
                )
                when(needed, copy.start)

    def arrived(buffer, send, recv):
        for at, (src, dst, many, _, to, needed, coming) in enumerate(moves):
            copy = remote(
                buffer.at[pl.ds(src, many)], buffer.at[pl.ds(dst, many)], send.at[at], recv.at[at], to
            )
            when(coming, copy.wait_recv)

    def departed(buffer, send, recv):
        for at, (src, dst, many, _, to, needed, _) in enumerate(moves):
            copy = remote(
                buffer.at[pl.ds(src, many)], buffer.at[pl.ds(dst, many)], send.at[at], recv.at[at], to
            )
            when(needed, copy.wait_send)

    def pieces_in(col):
        for step in range(GROUP):
            source = lax.rem(rank + step, GROUP)
            far = place * COLS + col - source
            for c in range(CHAN):
                at = lax.rem(chan + c, CHAN)
                if step == 0 and c == 0:
                    when(stays[col][1], stays[col][0].wait)
                else:
                    arrival = remote(
                        payload.at[0, 0],
                        got[col].at[source, at],
                        spread_send.at[0],
                        spread_recv.at[(source * CHAN + at) * COLS + col],
                        (device, at),
                    )
                    when((far >= 0) & (far < HELD), arrival.wait_recv)

    row = lax.broadcasted_iota(jnp.int32, (RIM, CELLS), 0)
    cell = lax.broadcasted_iota(jnp.int32, (RIM, CELLS), 1)
    edge, along = row >> 3, row & 7
    at_rim = jnp.where(
        edge == 0, along, jnp.where(edge == 1, 56 + along, jnp.where(edge == 2, along * 8, along * 8 + 7))
    )
    at_rim = jnp.where(cell == at_rim, 1.0, 0.0).astype(BF16)
    gain_of = lambda gain: gain[...].reshape(1, D)
    wide_lane = lax.broadcasted_iota(jnp.int32, (48, 128), 1)
    masks = []
    wanted = []
    for col in range(COLS):
        pieces_in(col)
        blocks = [got[col][sources[col], c, PIECE - 1].astype(F32) for c in range(CHAN)]
        for r in range(ROWS):
            slot = chan * ROWS + r
            pieces, column = [], []
            for c in range(CHAN):
                pieces.append(
                    jnp.concatenate([got[col][sources[col], c, r * 3 + part] for part in range(3)], axis=1)
                )
                column.append(jnp.sum(jnp.where(lane == slot, blocks[c], 0.0), axis=1, keepdims=True))
            values = jnp.concatenate(pieces, axis=0)
            mask = jnp.concatenate(column, axis=0)
            masks.append(mask)
            tile = col * ROWS + r
            own[tile * CELLS : (tile + 1) * CELLS] = values
            norm = (rms(values.astype(F32), gain_of(gain_image)) * mask).astype(BF16)
            normed[tile] = norm
            rims[(1 + col) * GRID_R + 1 + r] = jnp.dot(at_rim, norm, preferred_element_type=F32).astype(BF16)
            if r % PART == PART - 1:
                exchange(rims, rim_send, rim_recv, (col,), r - PART + 1)
        all_wanted = rim_wanted(blocks[0][0:8], blocks[0][8:16])
        for r in range(ROWS):
            slot = chan * ROWS + r + FACE
            wanted.append(jnp.sum(jnp.where(wide_lane == slot, all_wanted, 0.0), axis=1, keepdims=True))
        for tile in range(col * ROWS, (col + 1) * ROWS):
            frame[tile, 1:9, 8:16, :] = normed[tile].astype(F32).reshape(SIDE, SIDE, D)

    loads[0].wait()
    arrived(rims, rim_send, rim_recv)

    rim_lane = lax.broadcasted_iota(jnp.int32, (48, SPOTS * RIM), 1).astype(F32)
    for part in range(0, ROWS, PART):
        for col in range(COLS):
            for r in range(part, part + PART):
                tile = col * ROWS + r
                at = part * COLS + col * PART + r - part
                chosen = jnp.where(rim_lane == wanted[tile], 1.0, 0.0).astype(BF16)
                rim = jnp.dot(chosen, rims[...].reshape(SPOTS * RIM, D), preferred_element_type=F32)
                frame[tile, 0, 8:16, :] = rim[0:8]
                frame[tile, 9, 8:16, :] = rim[8:16]
                for i in range(SIDE):
                    frame[tile, 1 + i, 7:8, :] = rim[16 + i : 17 + i]
                    frame[tile, 1 + i, 16:17, :] = rim[24 + i : 25 + i]
                frame[tile, 0, 7:8, :] = rim[32:33]
                frame[tile, 0, 16:17, :] = rim[33:34]
                frame[tile, 9, 7:8, :] = rim[34:35]
                frame[tile, 9, 16:17, :] = rim[35:36]
                for tap in range(9):
                    dr, dc = tap // 3, tap % 3
                    window = frame[tile, dr : dr + SIDE, 7 + dc : 7 + dc + SIDE, :]
                    patches[at * CELLS : (at + 1) * CELLS, tap * D : (tap + 1) * D] = window.reshape(
                        CELLS, D
                    ).astype(BF16)
        total = jnp.dot(
            patches[part * COLS * CELLS : (part + PART) * COLS * CELLS, :], conv[...], preferred_element_type=F32
        )
        for col in range(COLS):
            tile = col * ROWS + part
            rows = slice(tile * CELLS, (tile + PART) * CELLS)
            mine = total[col * PART * CELLS : (col + 1) * PART * CELLS]
            image = (own[rows, :].astype(F32) + mine).astype(BF16)
            after[rows, :] = image
            mask = jnp.concatenate(masks[tile : tile + PART], axis=0)
            attn = (rms(image.astype(F32), gain_of(gain_attn)) * mask).astype(BF16)
            spot = (1 + col) * GRID_R + 1 + part
            table[spot : spot + PART] = attn.reshape(PART, CELLS, D)
        exchange(table, halo_send, halo_recv, (0, 1), part)

    def project(spot, many):
        rows = table[spot : spot + many].reshape(many * CELLS, D)
        found = jnp.dot(rows, qkv[:, D:], preferred_element_type=F32)
        memory[spot * CELLS : (spot + many) * CELLS, :] = found.astype(BF16)

    loads[1].wait()
    scale = 1.0 / math.sqrt(HEAD_DIM)
    for col in range(COLS):
        spot = (1 + col) * GRID_R + 1
        found = jnp.dot(
            table[spot : spot + ROWS].reshape(HALF, D), qkv[:, :D], preferred_element_type=F32
        )
        queries[col * HALF : (col + 1) * HALF, :] = (found * scale).astype(BF16)
        project(spot, ROWS)
    for load in loads[2:]:
        load.wait()
    arrived(table, halo_send, halo_recv)
    project(0, GRID_R + 1)
    project(GRID_R + ROWS + 1, 2)
    project(2 * GRID_R + ROWS + 1, GRID_R + 1)

    def heads_step(rows, first, lanes, base):
        heads = lanes // HEAD_DIM
        head = lax.broadcasted_iota(jnp.int32, (CELLS, lanes), 1) >> 6
        query = queries[rows, first : first + lanes]
        nothing = jnp.zeros_like(query)
        blocks = jnp.concatenate([jnp.where(head == h, query, nothing) for h in range(heads)], axis=0)
        spots = slice(base, base + 9 * CELLS)
        scores = lax.dot_general(
            blocks, keys[spots, first : first + lanes], (((1,), (1,)), ((), ())), preferred_element_type=F32
        )
        weights = jnp.exp(scores - jnp.max(scores, axis=-1, keepdims=True))
        total = jnp.sum(weights, axis=-1, keepdims=True)
        value = jnp.dot(
            weights.astype(BF16), keys[spots, D + first : D + first + lanes], preferred_element_type=F32
        )
        value = value / total
        found = value[:CELLS]
        for h in range(1, heads):
            found = jnp.where(head == h, value[h * CELLS : (h + 1) * CELLS], found)
        mixed[rows, first : first + lanes] = found.astype(BF16)

    returned = []
    for col in range(COLS):

        def attend(r):
            base_key = r % PART * 9 * CELLS
            for n in range(3):
                spot = (col + n) * GRID_R + r
                keys[base_key + n * 3 * CELLS : base_key + (n + 1) * 3 * CELLS, :] = memory[
                    spot * CELLS : (spot + 3) * CELLS, :
                ]
            rows = slice((col * ROWS + r) * CELLS, (col * ROWS + r + 1) * CELLS)
            heads_step(rows, 0, 4 * HEAD_DIM, base_key)
            heads_step(rows, 4 * HEAD_DIM, 2 * HEAD_DIM, base_key)

        for part in range(0, ROWS, PART):
            for r in range(part, part + PART):
                attend(r)
            rows = slice(col * HALF + part * CELLS, col * HALF + (part + PART) * CELLS)
            attended = jnp.dot(mixed[rows, :], proj[...], preferred_element_type=F32)
            attended = (after[rows, :].astype(F32) + attended).astype(BF16)
            wide = attended.astype(F32)
            hidden = jnp.dot(rms(wide, gain_of(gain_mlp)).astype(BF16), up[...], preferred_element_type=F32)
            hidden = (0.5 * hidden * (1.0 + lax.erf(hidden * (0.5**0.5)))).astype(BF16)
            encoded = wide + jnp.dot(hidden, down[...], preferred_element_type=F32)
            encoded = encoded.astype(BF16).reshape(PART, CHAN, 16, D)
            for r in range(PART):
                for c in range(CHAN):
                    tiles[col, c, part + r] = encoded[r, c]
            span = pl.ds(part, PART)
            for c in (2, 3, 1, 0):
                to = lax.rem(chan + c, CHAN)
                for step in range(GROUP):
                    target = lax.rem(rank + step, GROUP)
                    i = place * COLS + col - target
                    slot = limit(i, HELD - 1)
                    inside = (i >= 0) & (i < HELD)
                    if c == 0 and step == 0:
                        copy = pltpu.make_async_copy(
                            tiles.at[col, chan, span],
                            home.at[slot, chan, span],
                            local.at[COLS + (col * ROWS + part) // PART],
                        )
                    else:
                        copy = remote(
                            tiles.at[col, to, span],
                            home.at[slot, chan, span],
                            home_send.at[len(returned)],
                            home_recv.at[(slot * CHAN + chan) * (ROWS // PART) + part // PART],
                            (base + target, to),
                        )
                    when(inside, copy.start)
                    returned.append((copy, inside, c == 0 and step == 0))

    for i in range(HELD):
        worker = snake((rank + i) // COLS)
        for c in range(CHAN):
            at = lax.rem(chan + c, CHAN)
            for part in range(0, ROWS, PART):
                span = pl.ds(part, PART)
                arrival = remote(
                    tiles.at[0, 0, span],
                    home.at[i, at, span],
                    home_send.at[0],
                    home_recv.at[(i * CHAN + at) * (ROWS // PART) + part // PART],
                    (device, at),
                )
                when(None if c else worker != rank, arrival.wait_recv)

    departed(rims, rim_send, rim_recv)
    departed(table, halo_send, halo_recv)
    for copy, needed in sent:
        when(needed, copy.wait_send)
    for copy, inside, stays_here in returned:
        when(inside, copy.wait if stays_here else copy.wait_send)
    for i in range(HELD):
        column = limit(i + shift, HELD - 1)
        for c in range(CHAN):
            for r in range(ROWS):
                out[i, c * ROWS + r] = home[column, c, r]


def per_device(
    latents,
    owner,
    neighbours,
    rotations,
    cell_mask,
    gain_image,
    conv_weight,
    gain_attn,
    qkv_weight,
    out_weight,
    gain_mlp,
    up_weight,
    down_weight,
):
    weights = [conv_weight, qkv_weight, out_weight, up_weight, down_weight]
    vmem = pltpu.VMEM
    dma = pltpu.SemaphoreType.DMA
    moves = 8 + 2 * COLS
    out, filled = pl.pallas_call(
        block_kernel,
        out_shape=(
            jax.ShapeDtypeStruct((HELD, FACE, 16, D), BF16),
            jax.ShapeDtypeStruct((1,), jnp.int32),
        ),
        in_specs=[HBM] * 13,
        out_specs=(VMEM, pl.BlockSpec(memory_space=pltpu.SMEM)),
        scratch_shapes=[
            pltpu.SMEM((FACE * BAND,), jnp.int32),
            vmem((16, SLOTS), jnp.int32),
            vmem((8, SLOTS), jnp.int32),
            vmem((8, SLOTS), jnp.int32),
            vmem((D,), F32),
            vmem((D,), F32),
            vmem((D,), F32),
            vmem((HELD, CHAN, ROWS, 16, D), BF16),
            vmem((32, 128), jnp.int32),
            vmem((HELD, FACE, 16, D), BF16),
            vmem((HELD, CHAN, PIECE, 16, 128), BF16),
            vmem((GROUP, CHAN, PIECE, 16, 128), BF16),
            vmem((GROUP, CHAN, PIECE, 16, 128), BF16),
            vmem((OWN * CELLS, D), BF16),
            vmem((OWN, CELLS, D), BF16),
            vmem((HELD, FACE, 128), BF16),
            vmem((SPOTS, RIM, D), BF16),
            vmem((OWN, 10, 24, D), F32),
            vmem((OWN * CELLS, 9 * D), BF16),
            vmem((OWN * CELLS, D), BF16),
            vmem((SPOTS, CELLS, D), BF16),
            vmem((SPOTS * CELLS, 2 * D), BF16),
            vmem((OWN * CELLS, D), BF16),
            vmem((PART * 9 * CELLS, 2 * D), BF16),
            vmem((OWN * CELLS, D), BF16),
            vmem((COLS, CHAN, ROWS, 16, D), BF16),
            *[vmem(w.shape, BF16) for w in weights],
            dma((13,)),
            dma((HELD * CHAN,)),
            dma((GROUP * CHAN * COLS,)),
            dma((moves,)),
            dma((moves,)),
            dma((moves,)),
            dma((moves,)),
            dma((GROUP * CHAN * OWN // PART,)),
            dma((HELD * CHAN * ROWS // PART,)),
            dma((COLS + OWN // PART,)),
        ],
        compiler_params=pltpu.CompilerParams(
            collective_id=0, has_side_effects=True, vmem_limit_bytes=60 << 20
        ),
        name="encoder_block",
    )(
        owner,
        cell_mask.T,
        neighbours.T,
        rotations.T,
        latents.reshape(HELD, FACE, 16, D),
        gain_image,
        gain_attn,
        gain_mlp,
        *weights,
    )
    out = out.reshape(SLOTS, 16, D)
    slot = lax.broadcasted_iota(jnp.int32, out.shape, 0)
    return jnp.where(slot < filled[0], out, jnp.zeros_like(out))


def solution(mesh):
    in_specs = (
        P("tiles", "chan", None),
        P(),
        P("tiles", None),
        P("tiles", None),
        P("tiles", "chan"),
        P(),
        P(),
        P(),
        P(),
        P(),
        P(),
        P(),
        P(),
    )
    return jax.shard_map(
        per_device,
        mesh=mesh,
        in_specs=in_specs,
        out_specs=P("tiles", "chan", None),
        check_vma=False,
    )
```

```python
import math

import jax
import jax.numpy as jnp
from jax import lax
from jax.experimental import pallas as pl
from jax.experimental.pallas import tpu as pltpu
from jax.sharding import PartitionSpec as P

MESH = pl.DeviceIdType.MESH
VMEM = pl.BlockSpec(memory_space=pltpu.VMEM)
SMEM = pl.BlockSpec(memory_space=pltpu.SMEM)
HBM = pl.BlockSpec(memory_space=pltpu.HBM)
F32, BF16 = jnp.float32, jnp.bfloat16

D = 384
FFN_UNITS = 1536
HEAD_DIM = 64
FACE = 16
BAND = 64
SIDE = 8
CELLS = 64
SLOTS = 80
HELD = 5
GROUP = 4
CHAN = 4
COLS = 2
ROWS = 4
OWN = COLS * ROWS
GRID_R, GRID_C = ROWS + 2, COLS + 2
SPOTS = GRID_R * GRID_C
HALF = ROWS * CELLS
PART = 2
RIM = 32
PIECE = ROWS * 3 + 1
epsilon = 1e-06


def rms(wide, gain):
    return wide * lax.rsqrt(jnp.mean(wide * wide, axis=-1, keepdims=True) + epsilon) * gain


def snake(q):
    return q // 2 * 2 + lax.rem(q + q // 2, 2)


def device_of(worker):
    base = worker // GROUP * GROUP
    return base + snake(worker - base)


def remote(src, dst, send, recv, device):
    return pltpu.make_async_remote_copy(
        src_ref=src, dst_ref=dst, send_sem=send, recv_sem=recv, device_id=device, device_id_type=MESH
    )


def neighbour_places(near, start, count):
    slot = lax.broadcasted_iota(jnp.int32, near.shape, 1)
    base = jnp.where(
        near < SLOTS,
        start,
        jnp.where(near < SLOTS + FACE, start - FACE - SLOTS, start + count - SLOTS - FACE),
    )
    tile = (near + base) & (FACE * BAND - 1)
    own_col = (start + slot) >> 4
    grid_row = (tile & 15) - (slot & 12) + 1
    grid_col = ((tile >> 4) - (own_col - (own_col & 1)) + 1) & (BAND - 1)
    grid_row = jnp.minimum(jnp.maximum(grid_row, 0), GRID_R - 1)
    grid_col = jnp.minimum(jnp.maximum(grid_col, 0), GRID_C - 1)
    return jnp.where(near < SLOTS + 2 * FACE, grid_col * GRID_R + grid_row, SPOTS)


def rim_wanted(near, turns):
    q = lax.broadcasted_iota(jnp.int32, (48, 128), 0)

    def pick(*values):
        found = values[7]
        for at, top in ((6, 35), (5, 34), (4, 33), (3, 32), (2, 24), (1, 16), (0, 8)):
            found = jnp.where(q < top, values[at], found)
        return found

    along = q & 7
    order = (1, 6, 3, 4, 0, 2, 5, 7)
    place = pick(*[near[n : n + 1] for n in order])
    turn = pick(*[turns[n : n + 1] for n in order])
    i = pick(7, 0, along, along, 7, 7, 0, 0)
    j = pick(along, along, 7, 0, 7, 0, 7, 0)

    def turned(a, b, c, d):
        return jnp.where(turn < 0.5, a, jnp.where(turn < 1.5, b, jnp.where(turn < 2.5, c, d)))

    from_row = turned(i, j, 7 - i, 7 - j)
    from_col = turned(j, 7 - i, 7 - j, i)
    rim = jnp.where(
        from_row == 0,
        from_col,
        jnp.where(from_row == 7, 8 + from_col, jnp.where(from_col == 0, 16 + from_row, 24 + from_row)),
    )
    return jnp.where(q < 36, place * RIM + rim.astype(F32), float(SPOTS * RIM))


def halo_moves(device, chan, base, rank):
    worker = base + snake(rank)
    total = lax.axis_size("tiles")
    left = device_of(lax.rem(worker + total - 1, total))
    right = device_of(lax.rem(worker + 1, total))
    up, down = chan > 0, chan < CHAN - 1
    above, below = lax.rem(chan + CHAN - 1, CHAN), lax.rem(chan + 1, CHAN)
    first, second, third = GRID_R, 2 * GRID_R, 3 * GRID_R
    last = ROWS - PART
    moves = [
        (first + 1, third + 1, PART, (0, 0), (left, chan), None, None),
        (second + 1, 1, PART, (1, 0), (right, chan), None, None),
        (first + 1 + last, third + 1 + last, PART, (0, last), (left, chan), None, None),
        (second + 1 + last, 1 + last, PART, (1, last), (right, chan), None, None),
        (first + 1, third + ROWS + 1, 1, (0, 0), (left, above), up, down),
        (first + ROWS, third, 1, (0, last), (left, below), down, up),
        (first + 1, first + ROWS + 1, 1, (0, 0), (device, above), up, down),
        (first + ROWS, first, 1, (0, last), (device, below), down, up),
        (second + 1, ROWS + 1, 1, (1, 0), (right, above), up, down),
        (second + ROWS, 0, 1, (1, last), (right, below), down, up),
        (second + 1, second + ROWS + 1, 1, (1, 0), (device, above), up, down),
        (second + ROWS, second, 1, (1, last), (device, below), down, up),
    ]
    return moves, (left, right, above, below)


def when(condition, action):
    if condition is None:
        action()
    else:
        pl.when(condition)(action)


def block_kernel(
    owner_hbm,
    mask_in,
    near_in,
    turn_in,
    latents,
    gain_image,
    gain_attn,
    gain_mlp,
    conv_hbm,
    qkv_hbm,
    proj_hbm,
    up_hbm,
    down_hbm,
    home,
    where,
    owner,
    raw,
    held,
    payload,
    got_first,
    got_second,
    own,
    normed,
    marks,
    rims,
    frame,
    patches,
    after,
    table,
    memory,
    queries,
    keys,
    mixed,
    tiles,
    conv,
    qkv,
    proj,
    up,
    down,
    load_sem,
    spread_send,
    spread_recv,
    rim_send,
    rim_recv,
    halo_send,
    halo_recv,
    home_send,
    home_recv,
    local,
):
    device, chan = lax.axis_index("tiles"), lax.axis_index("chan")
    rank = lax.rem(device, GROUP)
    base = device - rank
    place = snake(rank)
    moves, (left, right, above, below) = halo_moves(device, chan, base, rank)

    got = (got_first, got_second)
    owner_load = pltpu.make_async_copy(owner_hbm, owner, load_sem.at[6])
    owner_load.start()
    first_load = pltpu.make_async_copy(latents, held, load_sem.at[0])
    first_load.start()
    loads = []
    for at, (src, dst) in enumerate(
        [(conv_hbm, conv), (qkv_hbm, qkv), (proj_hbm, proj), (up_hbm, up), (down_hbm, down)]
    ):
        loads.append(pltpu.make_async_copy(src, dst, load_sem.at[1 + at]))

    barrier = pltpu.get_barrier_semaphore()
    partners = []
    for step in range(1, GROUP * CHAN):
        other = lax.rem(rank * CHAN + chan + step, GROUP * CHAN)
        partners.append((base + other // CHAN, lax.rem(other, CHAN)))
    for side in (left, right):
        partners += [(side, chan), (side, above), (side, below)]
    for partner in partners:
        pl.semaphore_signal(barrier, inc=1, device_id=partner, device_id_type=MESH)

    def count_columns(col, carry):
        start, count = carry
        holder = owner[col * FACE]
        return (
            start + jnp.where(holder < device, 1, 0),
            count + jnp.where(holder == device, 1, 0),
        )

    owner_load.wait()
    start, count = lax.fori_loop(0, BAND, count_columns, (jnp.int32(0), jnp.int32(0)))
    limit = lambda value, top: jnp.minimum(jnp.maximum(value, 0), top)
    shift = limit(start - base * COLS - rank, HELD - 1)
    where[0], where[1] = shift, count
    sources = [
        limit(owner[((base + place) * COLS + col) * FACE] - base, GROUP - 1) for col in range(COLS)
    ]

    raw[...] = jnp.zeros_like(raw)
    raw[0:16, 0:SLOTS] = mask_in[...]
    raw[16:24, 0:SLOTS] = near_in[...]
    raw[24:32, 0:SLOTS] = turn_in[...]
    lane = lax.broadcasted_iota(jnp.int32, (16, 128), 1)
    mask_rows = raw[0:16].astype(F32)
    near_rows = neighbour_places(raw[16:24], start * FACE, count * FACE).astype(F32)
    near_rows = jnp.concatenate([near_rows, raw[24:32].astype(F32)], axis=0)
    for i in range(HELD):
        cells = pltpu.roll(mask_rows, (128 - i * FACE) % 128, axis=1)
        near = pltpu.roll(near_rows, (128 + FACE - i * FACE) % 128, axis=1)
        marks[i] = jnp.where(lane < FACE, cells, near).astype(BF16)
    first_load.wait()

    def fill(i):
        col = lax.rem(i + HELD - shift, HELD)
        for c in range(CHAN):
            for r in range(ROWS):
                for part in range(3):
                    payload[i, c, r * 3 + part] = held[col, c * ROWS + r, :, part * 128 : (part + 1) * 128]
            payload[i, c, PIECE - 1] = marks[col]

    sent = []
    for step in range(HELD):
        i = lax.rem(2 * step + lax.rem(rank, 2), HELD)
        fill(i)
        if step == 0:
            pl.semaphore_wait(barrier, len(partners))
        target = snake((rank + i) // COLS)
        odd = lax.rem(rank, 2) == 1
        for c in (2, 3, 1, 0):
            to = lax.rem(chan + c, CHAN)
            away = None if c else target != rank
            for col in range(COLS):
                if step == 2:
                    needed = odd if col else jnp.logical_not(odd)
                    needed = needed if away is None else needed & away
                elif (step > 2) == (col == 1):
                    needed = away
                else:
                    continue
                copy = remote(
                    payload.at[i, to],
                    got[col].at[rank, chan],
                    spread_send.at[step * CHAN + c],
                    spread_recv.at[(rank * CHAN + chan) * COLS + col],
                    (base + target, to),
                )
                when(needed, copy.start)
                sent.append((copy, needed))
    stays = []
    for col in range(COLS):
        i = place * COLS + col - rank
        copy = pltpu.make_async_copy(
            payload.at[limit(i, HELD - 1), chan], got[col].at[rank, chan], local.at[col]
        )
        inside = (i >= 0) & (i < HELD)
        when(inside, copy.start)
        stays.append((copy, inside))
    for load in loads:
        load.start()
    beyond = jnp.zeros((RIM, D), BF16)
    for col in range(GRID_C):

        @pl.when(chan == 0)
        def _():
            rims[col * GRID_R] = beyond
            for part in range(2):
                table[col * GRID_R, part * RIM : (part + 1) * RIM] = beyond

        @pl.when(chan == CHAN - 1)
        def _():
            rims[(col + 1) * GRID_R - 1] = beyond
            for part in range(2):
                table[(col + 1) * GRID_R - 1, part * RIM : (part + 1) * RIM] = beyond

    def exchange(buffer, send, recv, kind, which):
        for at, (src, dst, many, ready, to, needed, _) in enumerate(moves):
            if ready[kind] == which:
                copy = remote(
                    buffer.at[pl.ds(src, many)], buffer.at[pl.ds(dst, many)], send.at[at], recv.at[at], to
                )
                when(needed, copy.start)

    def arrived(buffer, send, recv):
        for at, (src, dst, many, _, to, needed, coming) in enumerate(moves):
            copy = remote(
                buffer.at[pl.ds(src, many)], buffer.at[pl.ds(dst, many)], send.at[at], recv.at[at], to
            )
            when(coming, copy.wait_recv)

    def departed(buffer, send, recv):
        for at, (src, dst, many, _, to, needed, _) in enumerate(moves):
            copy = remote(
                buffer.at[pl.ds(src, many)], buffer.at[pl.ds(dst, many)], send.at[at], recv.at[at], to
            )
            when(needed, copy.wait_send)

    def pieces_in(col):
        for step in range(GROUP):
            source = lax.rem(rank + step, GROUP)
            far = place * COLS + col - source
            for c in range(CHAN):
                at = lax.rem(chan + c, CHAN)
                if step == 0 and c == 0:
                    when(stays[col][1], stays[col][0].wait)
                else:
                    arrival = remote(
                        payload.at[0, 0],
                        got[col].at[source, at],
                        spread_send.at[0],
                        spread_recv.at[(source * CHAN + at) * COLS + col],
                        (device, at),
                    )
                    when((far >= 0) & (far < HELD), arrival.wait_recv)

    row = lax.broadcasted_iota(jnp.int32, (RIM, CELLS), 0)
    cell = lax.broadcasted_iota(jnp.int32, (RIM, CELLS), 1)
    edge, along = row >> 3, row & 7
    at_rim = jnp.where(
        edge == 0, along, jnp.where(edge == 1, 56 + along, jnp.where(edge == 2, along * 8, along * 8 + 7))
    )
    at_rim = jnp.where(cell == at_rim, 1.0, 0.0).astype(BF16)
    gain_of = lambda gain: gain[...].reshape(1, D)
    wide_lane = lax.broadcasted_iota(jnp.int32, (48, 128), 1)
    masks = []
    wanted = []
    for col in range(COLS):
        pieces_in(col)
        blocks = [got[col][sources[col], c, PIECE - 1].astype(F32) for c in range(CHAN)]
        all_wanted = rim_wanted(blocks[0][0:8], blocks[0][8:16])
        for r in range(ROWS):
            slot = chan * ROWS + r
            wanted.append(
                jnp.sum(jnp.where(wide_lane == slot + FACE, all_wanted, 0.0), axis=1, keepdims=True)
            )
            pieces, column = [], []
            for c in range(CHAN):
                pieces.append(
                    jnp.concatenate([got[col][sources[col], c, r * 3 + part] for part in range(3)], axis=1)
                )
                column.append(jnp.sum(jnp.where(lane == slot, blocks[c], 0.0), axis=1, keepdims=True))
            values = jnp.concatenate(pieces, axis=0)
            mask = jnp.concatenate(column, axis=0)
            masks.append(mask)
            tile = col * ROWS + r
            own[tile * CELLS : (tile + 1) * CELLS] = values
            norm = (rms(values.astype(F32), gain_of(gain_image)) * mask).astype(BF16)
            normed[tile] = norm
            rims[(1 + col) * GRID_R + 1 + r] = jnp.dot(at_rim, norm, preferred_element_type=F32).astype(BF16)
        exchange(rims, rim_send, rim_recv, 0, col)
        for tile in range(col * ROWS, (col + 1) * ROWS):
            frame[tile, 1:9, 8:16, :] = normed[tile].astype(F32).reshape(SIDE, SIDE, D)

    loads[0].wait()
    arrived(rims, rim_send, rim_recv)

    rim_lane = lax.broadcasted_iota(jnp.int32, (48, SPOTS * RIM), 1).astype(F32)
    for part in range(0, ROWS, PART):
        chosen = [
            jnp.where(rim_lane == wanted[col * ROWS + r], 1.0, 0.0).astype(BF16)
            for col in range(COLS)
            for r in range(part, part + PART)
        ]
        strips = jnp.dot(
            jnp.concatenate(chosen, axis=0), rims[...].reshape(SPOTS * RIM, D), preferred_element_type=F32
        )
        for col in range(COLS):
            for r in range(part, part + PART):
                tile = col * ROWS + r
                at = part * COLS + col * PART + r - part
                rim = strips[(at - part * COLS) * 48 : (at - part * COLS + 1) * 48]
                frame[tile, 0, 8:16, :] = rim[0:8]
                frame[tile, 9, 8:16, :] = rim[8:16]
                for i in range(SIDE):
                    frame[tile, 1 + i, 7:8, :] = rim[16 + i : 17 + i]
                    frame[tile, 1 + i, 16:17, :] = rim[24 + i : 25 + i]
                frame[tile, 0, 7:8, :] = rim[32:33]
                frame[tile, 0, 16:17, :] = rim[33:34]
                frame[tile, 9, 7:8, :] = rim[34:35]
                frame[tile, 9, 16:17, :] = rim[35:36]
                for tap in range(9):
                    dr, dc = tap // 3, tap % 3
                    window = frame[tile, dr : dr + SIDE, 7 + dc : 7 + dc + SIDE, :]
                    patches[at * CELLS : (at + 1) * CELLS, tap * D : (tap + 1) * D] = window.reshape(
                        CELLS, D
                    ).astype(BF16)
        total = jnp.dot(
            patches[part * COLS * CELLS : (part + PART) * COLS * CELLS, :], conv[...], preferred_element_type=F32
        )
        for col in range(COLS):
            tile = col * ROWS + part
            rows = slice(tile * CELLS, (tile + PART) * CELLS)
            mine = total[col * PART * CELLS : (col + 1) * PART * CELLS]
            image = (own[rows, :].astype(F32) + mine).astype(BF16)
            after[rows, :] = image
            mask = jnp.concatenate(masks[tile : tile + PART], axis=0)
            attn = (rms(image.astype(F32), gain_of(gain_attn)) * mask).astype(BF16)
            spot = (1 + col) * GRID_R + 1 + part
            table[spot : spot + PART] = attn.reshape(PART, CELLS, D)
        exchange(table, halo_send, halo_recv, 1, part)

    def project(spot, many):
        rows = table[spot : spot + many].reshape(many * CELLS, D)
        found = jnp.dot(rows, qkv[:, D:], preferred_element_type=F32)
        memory[spot * CELLS : (spot + many) * CELLS, :] = found.astype(BF16)

    loads[1].wait()
    scale = 1.0 / math.sqrt(HEAD_DIM)
    for col in range(COLS):
        spot = (1 + col) * GRID_R + 1
        found = jnp.dot(
            table[spot : spot + ROWS].reshape(HALF, D), qkv[:, :D], preferred_element_type=F32
        )
        queries[col * HALF : (col + 1) * HALF, :] = (found * scale).astype(BF16)
        project(spot, ROWS)
    for load in loads[2:]:
        load.wait()
    arrived(table, halo_send, halo_recv)
    project(0, GRID_R + 1)
    project(GRID_R + ROWS + 1, 2)
    project(2 * GRID_R + ROWS + 1, GRID_R + 1)

    def heads_step(rows, first, lanes, base):
        heads = lanes // HEAD_DIM
        head = lax.broadcasted_iota(jnp.int32, (CELLS, lanes), 1) >> 6
        query = queries[rows, first : first + lanes]
        nothing = jnp.zeros_like(query)
        blocks = jnp.concatenate([jnp.where(head == h, query, nothing) for h in range(heads)], axis=0)
        spots = slice(base, base + 9 * CELLS)
        scores = lax.dot_general(
            blocks, keys[spots, first : first + lanes], (((1,), (1,)), ((), ())), preferred_element_type=F32
        )
        weights = jnp.exp(scores - jnp.max(scores, axis=-1, keepdims=True))
        total = jnp.sum(weights, axis=-1, keepdims=True)
        value = jnp.dot(
            weights.astype(BF16), keys[spots, D + first : D + first + lanes], preferred_element_type=F32
        )
        value = value / total
        found = value[:CELLS]
        for h in range(1, heads):
            found = jnp.where(head == h, value[h * CELLS : (h + 1) * CELLS], found)
        mixed[rows, first : first + lanes] = found.astype(BF16)

    returned = []
    for col in range(COLS):

        def attend(r):
            base_key = r % PART * 9 * CELLS
            for n in range(3):
                spot = (col + n) * GRID_R + r
                keys[base_key + n * 3 * CELLS : base_key + (n + 1) * 3 * CELLS, :] = memory[
                    spot * CELLS : (spot + 3) * CELLS, :
                ]
            rows = slice((col * ROWS + r) * CELLS, (col * ROWS + r + 1) * CELLS)
            heads_step(rows, 0, 4 * HEAD_DIM, base_key)
            heads_step(rows, 4 * HEAD_DIM, 2 * HEAD_DIM, base_key)

        for part in range(0, ROWS, PART):
            for r in range(part, part + PART):
                attend(r)
            rows = slice(col * HALF + part * CELLS, col * HALF + (part + PART) * CELLS)
            attended = jnp.dot(mixed[rows, :], proj[...], preferred_element_type=F32)
            attended = (after[rows, :].astype(F32) + attended).astype(BF16)
            wide = attended.astype(F32)
            hidden = jnp.dot(rms(wide, gain_of(gain_mlp)).astype(BF16), up[...], preferred_element_type=F32)
            hidden = (0.5 * hidden * (1.0 + lax.erf(hidden * (0.5**0.5)))).astype(BF16)
            encoded = wide + jnp.dot(hidden, down[...], preferred_element_type=F32)
            encoded = encoded.astype(BF16).reshape(PART, CHAN, 16, D)
            for r in range(PART):
                for c in range(CHAN):
                    tiles[col, c, part + r] = encoded[r, c]
            span = pl.ds(part, PART)
            for c in (2, 3, 1, 0):
                to = lax.rem(chan + c, CHAN)
                for step in range(GROUP):
                    target = lax.rem(rank + step, GROUP)
                    i = place * COLS + col - target
                    slot = limit(i, HELD - 1)
                    inside = (i >= 0) & (i < HELD)
                    if c == 0 and step == 0:
                        copy = pltpu.make_async_copy(
                            tiles.at[col, chan, span],
                            home.at[slot, chan, span],
                            local.at[COLS + (col * ROWS + part) // PART],
                        )
                    else:
                        copy = remote(
                            tiles.at[col, to, span],
                            home.at[slot, chan, span],
                            home_send.at[len(returned)],
                            home_recv.at[(slot * CHAN + chan) * (ROWS // PART) + part // PART],
                            (base + target, to),
                        )
                    when(inside, copy.start)
                    returned.append((copy, inside, c == 0 and step == 0))

    departed(rims, rim_send, rim_recv)
    departed(table, halo_send, halo_recv)
    for copy, needed in sent:
        when(needed, copy.wait_send)
    for copy, inside, stays_here in returned:
        when(inside, copy.wait if stays_here else copy.wait_send)
    for i in range(HELD):
        worker = snake((rank + i) // COLS)
        for c in range(CHAN):
            at = lax.rem(chan + c, CHAN)
            for part in range(0, ROWS, PART):
                span = pl.ds(part, PART)
                arrival = remote(
                    tiles.at[0, 0, span],
                    home.at[i, at, span],
                    home_send.at[0],
                    home_recv.at[(i * CHAN + at) * (ROWS // PART) + part // PART],
                    (device, at),
                )
                when(None if c else worker != rank, arrival.wait_recv)


def settle_kernel(where, home, out, columns, blank, come, go):
    shift, count = where[0], where[1]

    def fetch(i):
        return pltpu.make_async_copy(home.at[jnp.minimum(i + shift, HELD - 1)], columns.at[i], come.at[i])

    for i in range(HELD):
        pl.when(i < count)(fetch(i).start)
    blank[...] = jnp.zeros_like(blank)
    for i in range(HELD):

        @pl.when(i < count)
        def _():
            fetch(i).wait()
            pltpu.make_async_copy(columns.at[i], out.at[i], go.at[i]).start()

        @pl.when(i >= count)
        def _():
            pltpu.make_async_copy(blank, out.at[i], go.at[i]).start()

    for i in range(HELD):
        pltpu.make_async_copy(blank, out.at[i], go.at[i]).wait()


def per_device(
    latents,
    owner,
    neighbours,
    rotations,
    cell_mask,
    gain_image,
    conv_weight,
    gain_attn,
    qkv_weight,
    out_weight,
    gain_mlp,
    up_weight,
    down_weight,
):
    weights = [conv_weight, qkv_weight, out_weight, up_weight, down_weight]
    vmem = pltpu.VMEM
    dma = pltpu.SemaphoreType.DMA
    moves = 8 + 2 * COLS
    home, where = pl.pallas_call(
        block_kernel,
        out_shape=(
            jax.ShapeDtypeStruct((HELD, CHAN, ROWS, 16, D), BF16),
            jax.ShapeDtypeStruct((2,), jnp.int32),
        ),
        in_specs=[HBM] + [VMEM] * 3 + [HBM] + [VMEM] * 3 + [HBM] * 5,
        out_specs=(HBM, SMEM),
        scratch_shapes=[
            pltpu.SMEM((FACE * BAND,), jnp.int32),
            vmem((32, 128), jnp.int32),
            vmem((HELD, FACE, 16, D), BF16),
            vmem((HELD, CHAN, PIECE, 16, 128), BF16),
            vmem((GROUP, CHAN, PIECE, 16, 128), BF16),
            vmem((GROUP, CHAN, PIECE, 16, 128), BF16),
            vmem((OWN * CELLS, D), BF16),
            vmem((OWN, CELLS, D), BF16),
            vmem((HELD, FACE, 128), BF16),
            vmem((SPOTS, RIM, D), BF16),
            vmem((OWN, 10, 24, D), F32),
            vmem((OWN * CELLS, 9 * D), BF16),
            vmem((OWN * CELLS, D), BF16),
            vmem((SPOTS, CELLS, D), BF16),
            vmem((SPOTS * CELLS, 2 * D), BF16),
            vmem((OWN * CELLS, D), BF16),
            vmem((PART * 9 * CELLS, 2 * D), BF16),
            vmem((OWN * CELLS, D), BF16),
            vmem((COLS, CHAN, ROWS, 16, D), BF16),
            *[vmem(w.shape, BF16) for w in weights],
            dma((7,)),
            dma((HELD * CHAN,)),
            dma((GROUP * CHAN * COLS,)),
            dma((moves,)),
            dma((moves,)),
            dma((moves,)),
            dma((moves,)),
            dma((GROUP * CHAN * OWN // PART,)),
            dma((HELD * CHAN * ROWS // PART,)),
            dma((COLS + OWN // PART,)),
        ],
        compiler_params=pltpu.CompilerParams(
            collective_id=0, has_side_effects=True, vmem_limit_bytes=60 << 20
        ),
        name="encoder_block",
    )(
        owner,
        cell_mask.T,
        neighbours.T,
        rotations.T,
        latents.reshape(HELD, FACE, 16, D),
        gain_image,
        gain_attn,
        gain_mlp,
        *weights,
    )
    out = pl.pallas_call(
        settle_kernel,
        out_shape=jax.ShapeDtypeStruct((HELD, FACE, 16, D), BF16),
        in_specs=[SMEM, HBM],
        out_specs=HBM,
        scratch_shapes=[
            vmem((HELD, FACE, 16, D), BF16),
            vmem((FACE, 16, D), BF16),
            dma((HELD,)),
            dma((HELD,)),
        ],
        name="settle",
    )(where, home.reshape(HELD, FACE, 16, D))
    return out.reshape(SLOTS, 16, D)


def solution(mesh):
    in_specs = (
        P("tiles", "chan", None),
        P(),
        P("tiles", None),
        P("tiles", None),
        P("tiles", "chan"),
        P(),
        P(),
        P(),
        P(),
        P(),
        P(),
        P(),
        P(),
    )
    return jax.shard_map(
        per_device,
        mesh=mesh,
        in_specs=in_specs,
        out_specs=P("tiles", "chan", None),
        check_vma=False,
    )
```

```python
import math

import jax
import jax.numpy as jnp
from jax import lax
from jax.experimental import pallas as pl
from jax.experimental.pallas import tpu as pltpu
from jax.sharding import PartitionSpec as P

MESH = pl.DeviceIdType.MESH
VMEM = pl.BlockSpec(memory_space=pltpu.VMEM)
SMEM = pl.BlockSpec(memory_space=pltpu.SMEM)
HBM = pl.BlockSpec(memory_space=pltpu.HBM)
F32, BF16 = jnp.float32, jnp.bfloat16

D = 384
FFN_UNITS = 1536
HEAD_DIM = 64
FACE = 16
BAND = 64
SIDE = 8
CELLS = 64
SLOTS = 80
HELD = 5
GROUP = 4
CHAN = 4
COLS = 2
ROWS = 4
OWN = COLS * ROWS
GRID_R, GRID_C = ROWS + 2, COLS + 2
SPOTS = GRID_R * GRID_C
HALF = ROWS * CELLS
PART = 2
RIM = 32
PIECE = ROWS * 3 + 1
epsilon = 1e-06


def rms(wide, gain):
    return wide * lax.rsqrt(jnp.mean(wide * wide, axis=-1, keepdims=True) + epsilon) * gain


def snake(q):
    return q // 2 * 2 + lax.rem(q + q // 2, 2)


def device_of(worker):
    base = worker // GROUP * GROUP
    return base + snake(worker - base)


def remote(src, dst, send, recv, device):
    return pltpu.make_async_remote_copy(
        src_ref=src, dst_ref=dst, send_sem=send, recv_sem=recv, device_id=device, device_id_type=MESH
    )


def neighbour_places(near, start, count):
    slot = lax.broadcasted_iota(jnp.int32, near.shape, 1)
    base = jnp.where(
        near < SLOTS,
        start,
        jnp.where(near < SLOTS + FACE, start - FACE - SLOTS, start + count - SLOTS - FACE),
    )
    tile = (near + base) & (FACE * BAND - 1)
    own_col = (start + slot) >> 4
    grid_row = (tile & 15) - (slot & 12) + 1
    grid_col = ((tile >> 4) - (own_col - (own_col & 1)) + 1) & (BAND - 1)
    grid_row = jnp.minimum(jnp.maximum(grid_row, 0), GRID_R - 1)
    grid_col = jnp.minimum(jnp.maximum(grid_col, 0), GRID_C - 1)
    return jnp.where(near < SLOTS + 2 * FACE, grid_col * GRID_R + grid_row, SPOTS)


def rim_wanted(near, turns):
    q = lax.broadcasted_iota(jnp.int32, (48, 128), 0)

    def pick(*values):
        found = values[7]
        for at, top in ((6, 35), (5, 34), (4, 33), (3, 32), (2, 24), (1, 16), (0, 8)):
            found = jnp.where(q < top, values[at], found)
        return found

    along = q & 7
    order = (1, 6, 3, 4, 0, 2, 5, 7)
    place = pick(*[near[n : n + 1] for n in order])
    turn = pick(*[turns[n : n + 1] for n in order])
    i = pick(7, 0, along, along, 7, 7, 0, 0)
    j = pick(along, along, 7, 0, 7, 0, 7, 0)

    def turned(a, b, c, d):
        return jnp.where(turn < 0.5, a, jnp.where(turn < 1.5, b, jnp.where(turn < 2.5, c, d)))

    from_row = turned(i, j, 7 - i, 7 - j)
    from_col = turned(j, 7 - i, 7 - j, i)
    rim = jnp.where(
        from_row == 0,
        from_col,
        jnp.where(from_row == 7, 8 + from_col, jnp.where(from_col == 0, 16 + from_row, 24 + from_row)),
    )
    return jnp.where(q < 36, place * RIM + rim.astype(F32), float(SPOTS * RIM))


def halo_moves(device, chan, base, rank):
    worker = base + snake(rank)
    total = lax.axis_size("tiles")
    left = device_of(lax.rem(worker + total - 1, total))
    right = device_of(lax.rem(worker + 1, total))
    up, down = chan > 0, chan < CHAN - 1
    above, below = lax.rem(chan + CHAN - 1, CHAN), lax.rem(chan + 1, CHAN)
    first, second, third = GRID_R, 2 * GRID_R, 3 * GRID_R
    last = ROWS - PART
    moves = [
        (first + 1, third + 1, PART, (0, 0), (left, chan), None, None),
        (second + 1, 1, PART, (1, 0), (right, chan), None, None),
        (first + 1 + last, third + 1 + last, PART, (0, last), (left, chan), None, None),
        (second + 1 + last, 1 + last, PART, (1, last), (right, chan), None, None),
        (first + 1, third + ROWS + 1, 1, (0, 0), (left, above), up, down),
        (first + ROWS, third, 1, (0, last), (left, below), down, up),
        (first + 1, first + ROWS + 1, 1, (0, 0), (device, above), up, down),
        (first + ROWS, first, 1, (0, last), (device, below), down, up),
        (second + 1, ROWS + 1, 1, (1, 0), (right, above), up, down),
        (second + ROWS, 0, 1, (1, last), (right, below), down, up),
        (second + 1, second + ROWS + 1, 1, (1, 0), (device, above), up, down),
        (second + ROWS, second, 1, (1, last), (device, below), down, up),
    ]
    return moves, (left, right, above, below)


def when(condition, action):
    if condition is None:
        action()
    else:
        pl.when(condition)(action)


def block_kernel(
    owner_hbm,
    mask_in,
    near_in,
    turn_in,
    latents,
    gain_image,
    gain_attn,
    gain_mlp,
    conv_hbm,
    qkv_hbm,
    proj_hbm,
    up_hbm,
    down_hbm,
    home,
    where,
    owner,
    raw,
    held,
    payload,
    got_first,
    got_second,
    own,
    normed,
    marks,
    rims,
    frame,
    patches,
    after,
    table,
    memory,
    queries,
    keys,
    mixed,
    tiles,
    conv,
    qkv,
    proj,
    up,
    down,
    load_sem,
    spread_send,
    spread_recv,
    rim_send,
    rim_recv,
    halo_send,
    halo_recv,
    home_send,
    home_recv,
    local,
):
    device, chan = lax.axis_index("tiles"), lax.axis_index("chan")
    rank = lax.rem(device, GROUP)
    base = device - rank
    place = snake(rank)
    moves, (left, right, above, below) = halo_moves(device, chan, base, rank)

    got = (got_first, got_second)
    owner_load = pltpu.make_async_copy(owner_hbm, owner, load_sem.at[6])
    owner_load.start()
    first_load = pltpu.make_async_copy(latents, held, load_sem.at[0])
    first_load.start()
    loads = []
    for at, (src, dst) in enumerate(
        [(conv_hbm, conv), (qkv_hbm, qkv), (proj_hbm, proj), (up_hbm, up), (down_hbm, down)]
    ):
        loads.append(pltpu.make_async_copy(src, dst, load_sem.at[1 + at]))

    barrier = pltpu.get_barrier_semaphore()
    partners = []
    for step in range(1, GROUP * CHAN):
        other = lax.rem(rank * CHAN + chan + step, GROUP * CHAN)
        partners.append((base + other // CHAN, lax.rem(other, CHAN)))
    for side in (left, right):
        partners += [(side, chan), (side, above), (side, below)]
    for partner in partners:
        pl.semaphore_signal(barrier, inc=1, device_id=partner, device_id_type=MESH)

    def count_columns(col, carry):
        start, count = carry
        holder = owner[col * FACE]
        return (
            start + jnp.where(holder < device, 1, 0),
            count + jnp.where(holder == device, 1, 0),
        )

    owner_load.wait()
    start, count = lax.fori_loop(0, BAND, count_columns, (jnp.int32(0), jnp.int32(0)))
    limit = lambda value, top: jnp.minimum(jnp.maximum(value, 0), top)
    shift = limit(start - base * COLS - rank, HELD - 1)
    where[0], where[1] = shift, count
    sources = [
        limit(owner[((base + place) * COLS + col) * FACE] - base, GROUP - 1) for col in range(COLS)
    ]

    raw[...] = jnp.zeros_like(raw)
    raw[0:16, 0:SLOTS] = mask_in[...]
    raw[16:24, 0:SLOTS] = near_in[...]
    raw[24:32, 0:SLOTS] = turn_in[...]
    lane = lax.broadcasted_iota(jnp.int32, (16, 128), 1)
    mask_rows = raw[0:16].astype(F32)
    near_rows = neighbour_places(raw[16:24], start * FACE, count * FACE).astype(F32)
    near_rows = jnp.concatenate([near_rows, raw[24:32].astype(F32)], axis=0)
    for i in range(HELD):
        cells = pltpu.roll(mask_rows, (128 - i * FACE) % 128, axis=1)
        near = pltpu.roll(near_rows, (128 + FACE - i * FACE) % 128, axis=1)
        marks[i] = jnp.where(lane < FACE, cells, near).astype(BF16)
    first_load.wait()

    def fill(i):
        col = lax.rem(i + HELD - shift, HELD)
        for c in range(CHAN):
            for r in range(ROWS):
                for part in range(3):
                    payload[i, c, r * 3 + part] = held[col, c * ROWS + r, :, part * 128 : (part + 1) * 128]
            payload[i, c, PIECE - 1] = marks[col]

    sent = []
    for step in range(HELD):
        i = lax.rem(2 * step + lax.rem(rank, 2), HELD)
        fill(i)
        if step == 0:
            pl.semaphore_wait(barrier, len(partners))
        target = snake((rank + i) // COLS)
        odd = lax.rem(rank, 2) == 1
        for c in (2, 3, 1, 0):
            to = lax.rem(chan + c, CHAN)
            away = None if c else target != rank
            for col in range(COLS):
                if step == 2:
                    needed = odd if col else jnp.logical_not(odd)
                    needed = needed if away is None else needed & away
                elif (step > 2) == (col == 1):
                    needed = away
                else:
                    continue
                copy = remote(
                    payload.at[i, to],
                    got[col].at[rank, chan],
                    spread_send.at[step * CHAN + c],
                    spread_recv.at[(rank * CHAN + chan) * COLS + col],
                    (base + target, to),
                )
                when(needed, copy.start)
                sent.append((copy, needed))
    stays = []
    for col in range(COLS):
        i = place * COLS + col - rank
        copy = pltpu.make_async_copy(
            payload.at[limit(i, HELD - 1), chan], got[col].at[rank, chan], local.at[col]
        )
        inside = (i >= 0) & (i < HELD)
        when(inside, copy.start)
        stays.append((copy, inside))
    for load in loads:
        load.start()
    beyond = jnp.zeros((RIM, D), BF16)
    for col in range(GRID_C):

        @pl.when(chan == 0)
        def _():
            rims[col * GRID_R] = beyond
            for part in range(2):
                table[col * GRID_R, part * RIM : (part + 1) * RIM] = beyond

        @pl.when(chan == CHAN - 1)
        def _():
            rims[(col + 1) * GRID_R - 1] = beyond
            for part in range(2):
                table[(col + 1) * GRID_R - 1, part * RIM : (part + 1) * RIM] = beyond

    def exchange(buffer, send, recv, kind, which):
        for at, (src, dst, many, ready, to, needed, _) in enumerate(moves):
            if ready[kind] == which:
                copy = remote(
                    buffer.at[pl.ds(src, many)], buffer.at[pl.ds(dst, many)], send.at[at], recv.at[at], to
                )
                when(needed, copy.start)

    def arrived(buffer, send, recv, first=0, end=SPOTS):
        for at, (src, dst, many, _, to, needed, coming) in enumerate(moves):
            if first <= dst < end:
                copy = remote(
                    buffer.at[pl.ds(src, many)], buffer.at[pl.ds(dst, many)], send.at[at], recv.at[at], to
                )
                when(coming, copy.wait_recv)

    def departed(buffer, send, recv):
        for at, (src, dst, many, _, to, needed, _) in enumerate(moves):
            copy = remote(
                buffer.at[pl.ds(src, many)], buffer.at[pl.ds(dst, many)], send.at[at], recv.at[at], to
            )
            when(needed, copy.wait_send)

    def pieces_in(col):
        for step in range(GROUP):
            source = lax.rem(rank + step, GROUP)
            far = place * COLS + col - source
            for c in range(CHAN):
                at = lax.rem(chan + c, CHAN)
                if step == 0 and c == 0:
                    when(stays[col][1], stays[col][0].wait)
                else:
                    arrival = remote(
                        payload.at[0, 0],
                        got[col].at[source, at],
                        spread_send.at[0],
                        spread_recv.at[(source * CHAN + at) * COLS + col],
                        (device, at),
                    )
                    when((far >= 0) & (far < HELD), arrival.wait_recv)

    row = lax.broadcasted_iota(jnp.int32, (RIM, CELLS), 0)
    cell = lax.broadcasted_iota(jnp.int32, (RIM, CELLS), 1)
    edge, along = row >> 3, row & 7
    at_rim = jnp.where(
        edge == 0, along, jnp.where(edge == 1, 56 + along, jnp.where(edge == 2, along * 8, along * 8 + 7))
    )
    at_rim = jnp.where(cell == at_rim, 1.0, 0.0).astype(BF16)
    gain_of = lambda gain: gain[...].reshape(1, D)
    wide_lane = lax.broadcasted_iota(jnp.int32, (48, 128), 1)
    masks = []
    wanted = []
    for col in range(COLS):
        pieces_in(col)
        blocks = [got[col][sources[col], c, PIECE - 1].astype(F32) for c in range(CHAN)]
        all_wanted = rim_wanted(blocks[0][0:8], blocks[0][8:16])
        for r in range(ROWS):
            slot = chan * ROWS + r
            wanted.append(
                jnp.sum(jnp.where(wide_lane == slot + FACE, all_wanted, 0.0), axis=1, keepdims=True)
            )
            pieces, column = [], []
            for c in range(CHAN):
                pieces.append(
                    jnp.concatenate([got[col][sources[col], c, r * 3 + part] for part in range(3)], axis=1)
                )
                column.append(jnp.sum(jnp.where(lane == slot, blocks[c], 0.0), axis=1, keepdims=True))
            values = jnp.concatenate(pieces, axis=0)
            mask = jnp.concatenate(column, axis=0)
            masks.append(mask)
            tile = col * ROWS + r
            own[tile * CELLS : (tile + 1) * CELLS] = values
            norm = (rms(values.astype(F32), gain_of(gain_image)) * mask).astype(BF16)
            normed[tile] = norm
            rims[(1 + col) * GRID_R + 1 + r] = jnp.dot(at_rim, norm, preferred_element_type=F32).astype(BF16)
        exchange(rims, rim_send, rim_recv, 0, col)
        for tile in range(col * ROWS, (col + 1) * ROWS):
            frame[tile, 1:9, 8:16, :] = normed[tile].astype(F32).reshape(SIDE, SIDE, D)

    loads[0].wait()
    arrived(rims, rim_send, rim_recv)

    rim_lane = lax.broadcasted_iota(jnp.int32, (48, SPOTS * RIM), 1).astype(F32)
    for part in range(0, ROWS, PART):
        for col in range(COLS):
            for r in range(part, part + PART):
                tile = col * ROWS + r
                at = part * COLS + col * PART + r - part
                chosen = jnp.where(rim_lane == wanted[tile], 1.0, 0.0).astype(BF16)
                rim = jnp.dot(chosen, rims[...].reshape(SPOTS * RIM, D), preferred_element_type=F32)
                frame[tile, 0, 8:16, :] = rim[0:8]
                frame[tile, 9, 8:16, :] = rim[8:16]
                for i in range(SIDE):
                    frame[tile, 1 + i, 7:8, :] = rim[16 + i : 17 + i]
                    frame[tile, 1 + i, 16:17, :] = rim[24 + i : 25 + i]
                frame[tile, 0, 7:8, :] = rim[32:33]
                frame[tile, 0, 16:17, :] = rim[33:34]
                frame[tile, 9, 7:8, :] = rim[34:35]
                frame[tile, 9, 16:17, :] = rim[35:36]
                for tap in range(9):
                    dr, dc = tap // 3, tap % 3
                    window = frame[tile, dr : dr + SIDE, 7 + dc : 7 + dc + SIDE, :]
                    patches[at * CELLS : (at + 1) * CELLS, tap * D : (tap + 1) * D] = window.reshape(
                        CELLS, D
                    ).astype(BF16)
        total = jnp.dot(
            patches[part * COLS * CELLS : (part + PART) * COLS * CELLS, :], conv[...], preferred_element_type=F32
        )
        for col in range(COLS):
            tile = col * ROWS + part
            rows = slice(tile * CELLS, (tile + PART) * CELLS)
            mine = total[col * PART * CELLS : (col + 1) * PART * CELLS]
            image = (own[rows, :].astype(F32) + mine).astype(BF16)
            after[rows, :] = image
            mask = jnp.concatenate(masks[tile : tile + PART], axis=0)
            attn = (rms(image.astype(F32), gain_of(gain_attn)) * mask).astype(BF16)
            spot = (1 + col) * GRID_R + 1 + part
            table[spot : spot + PART] = attn.reshape(PART, CELLS, D)
        exchange(table, halo_send, halo_recv, 1, part)

    def project(*spans):
        rows = jnp.concatenate(
            [table[spot : spot + many].reshape(many * CELLS, D) for spot, many in spans], axis=0
        )
        found = jnp.dot(rows, qkv[:, D:], preferred_element_type=F32).astype(BF16)
        at = 0
        for spot, many in spans:
            memory[spot * CELLS : (spot + many) * CELLS, :] = found[at : at + many * CELLS]
            at += many * CELLS

    loads[1].wait()
    scale = 1.0 / math.sqrt(HEAD_DIM)
    for col in range(COLS):
        spot = (1 + col) * GRID_R + 1
        found = jnp.dot(
            table[spot : spot + ROWS].reshape(HALF, D), qkv[:, :D], preferred_element_type=F32
        )
        queries[col * HALF : (col + 1) * HALF, :] = (found * scale).astype(BF16)
        project((spot, ROWS))
    for load in loads[2:]:
        load.wait()
    far = 3 * GRID_R
    arrived(table, halo_send, halo_recv, 0, far)
    project((0, GRID_R + 1), (GRID_R + ROWS + 1, 2), (2 * GRID_R + ROWS + 1, 1))

    def heads_step(rows, first, lanes, base):
        heads = lanes // HEAD_DIM
        head = lax.broadcasted_iota(jnp.int32, (CELLS, lanes), 1) >> 6
        query = queries[rows, first : first + lanes]
        nothing = jnp.zeros_like(query)
        blocks = jnp.concatenate([jnp.where(head == h, query, nothing) for h in range(heads)], axis=0)
        spots = slice(base, base + 9 * CELLS)
        scores = lax.dot_general(
            blocks, keys[spots, first : first + lanes], (((1,), (1,)), ((), ())), preferred_element_type=F32
        )
        weights = jnp.exp(scores - jnp.max(scores, axis=-1, keepdims=True))
        total = jnp.sum(weights, axis=-1, keepdims=True)
        value = jnp.dot(
            weights.astype(BF16), keys[spots, D + first : D + first + lanes], preferred_element_type=F32
        )
        value = value / total
        found = value[:CELLS]
        for h in range(1, heads):
            found = jnp.where(head == h, value[h * CELLS : (h + 1) * CELLS], found)
        mixed[rows, first : first + lanes] = found.astype(BF16)

    returned = []
    for col in range(COLS):

        def attend(r):
            base_key = r % PART * 9 * CELLS
            for n in range(3):
                spot = (col + n) * GRID_R + r
                keys[base_key + n * 3 * CELLS : base_key + (n + 1) * 3 * CELLS, :] = memory[
                    spot * CELLS : (spot + 3) * CELLS, :
                ]
            rows = slice((col * ROWS + r) * CELLS, (col * ROWS + r + 1) * CELLS)
            heads_step(rows, 0, 4 * HEAD_DIM, base_key)
            heads_step(rows, 4 * HEAD_DIM, 2 * HEAD_DIM, base_key)

        if col == 1:
            arrived(table, halo_send, halo_recv, far, SPOTS)
            project((far, GRID_R))
        for part in range(0, ROWS, PART):
            for r in range(part, part + PART):
                attend(r)
            rows = slice(col * HALF + part * CELLS, col * HALF + (part + PART) * CELLS)
            attended = jnp.dot(mixed[rows, :], proj[...], preferred_element_type=F32)
            attended = (after[rows, :].astype(F32) + attended).astype(BF16)
            wide = attended.astype(F32)
            hidden = jnp.dot(rms(wide, gain_of(gain_mlp)).astype(BF16), up[...], preferred_element_type=F32)
            hidden = (0.5 * hidden * (1.0 + lax.erf(hidden * (0.5**0.5)))).astype(BF16)
            encoded = wide + jnp.dot(hidden, down[...], preferred_element_type=F32)
            encoded = encoded.astype(BF16).reshape(PART, CHAN, 16, D)
            for r in range(PART):
                for c in range(CHAN):
                    tiles[col, c, part + r] = encoded[r, c]
            span = pl.ds(part, PART)
            for c in (2, 3, 1, 0):
                to = lax.rem(chan + c, CHAN)
                for step in range(GROUP):
                    target = lax.rem(rank + step, GROUP)
                    i = place * COLS + col - target
                    slot = limit(i, HELD - 1)
                    inside = (i >= 0) & (i < HELD)
                    if c == 0 and step == 0:
                        copy = pltpu.make_async_copy(
                            tiles.at[col, chan, span],
                            home.at[slot, chan, span],
                            local.at[COLS + (col * ROWS + part) // PART],
                        )
                    else:
                        copy = remote(
                            tiles.at[col, to, span],
                            home.at[slot, chan, span],
                            home_send.at[len(returned)],
                            home_recv.at[(slot * CHAN + chan) * (ROWS // PART) + part // PART],
                            (base + target, to),
                        )
                    when(inside, copy.start)
                    returned.append((copy, inside, c == 0 and step == 0))

    departed(rims, rim_send, rim_recv)
    departed(table, halo_send, halo_recv)
    for copy, needed in sent:
        when(needed, copy.wait_send)
    for copy, inside, stays_here in returned:
        when(inside, copy.wait if stays_here else copy.wait_send)
    for i in range(HELD):
        worker = snake((rank + i) // COLS)
        for c in range(CHAN):
            at = lax.rem(chan + c, CHAN)
            for part in range(0, ROWS, PART):
                span = pl.ds(part, PART)
                arrival = remote(
                    tiles.at[0, 0, span],
                    home.at[i, at, span],
                    home_send.at[0],
                    home_recv.at[(i * CHAN + at) * (ROWS // PART) + part // PART],
                    (device, at),
                )
                when(None if c else worker != rank, arrival.wait_recv)


def settle_kernel(where, home, out, columns, blank, come, go):
    shift, count = where[0], where[1]

    def fetch(i):
        return pltpu.make_async_copy(home.at[jnp.minimum(i + shift, HELD - 1)], columns.at[i], come.at[i])

    for i in range(HELD):
        pl.when(i < count)(fetch(i).start)
    blank[...] = jnp.zeros_like(blank)
    for i in range(HELD):

        @pl.when(i < count)
        def _():
            fetch(i).wait()
            pltpu.make_async_copy(columns.at[i], out.at[i], go.at[i]).start()

        @pl.when(i >= count)
        def _():
            pltpu.make_async_copy(blank, out.at[i], go.at[i]).start()

    for i in range(HELD):
        pltpu.make_async_copy(blank, out.at[i], go.at[i]).wait()


def per_device(
    latents,
    owner,
    neighbours,
    rotations,
    cell_mask,
    gain_image,
    conv_weight,
    gain_attn,
    qkv_weight,
    out_weight,
    gain_mlp,
    up_weight,
    down_weight,
):
    weights = [conv_weight, qkv_weight, out_weight, up_weight, down_weight]
    vmem = pltpu.VMEM
    dma = pltpu.SemaphoreType.DMA
    moves = 8 + 2 * COLS
    home, where = pl.pallas_call(
        block_kernel,
        out_shape=(
            jax.ShapeDtypeStruct((HELD, CHAN, ROWS, 16, D), BF16),
            jax.ShapeDtypeStruct((2,), jnp.int32),
        ),
        in_specs=[HBM] + [VMEM] * 3 + [HBM] + [VMEM] * 3 + [HBM] * 5,
        out_specs=(HBM, SMEM),
        scratch_shapes=[
            pltpu.SMEM((FACE * BAND,), jnp.int32),
            vmem((32, 128), jnp.int32),
            vmem((HELD, FACE, 16, D), BF16),
            vmem((HELD, CHAN, PIECE, 16, 128), BF16),
            vmem((GROUP, CHAN, PIECE, 16, 128), BF16),
            vmem((GROUP, CHAN, PIECE, 16, 128), BF16),
            vmem((OWN * CELLS, D), BF16),
            vmem((OWN, CELLS, D), BF16),
            vmem((HELD, FACE, 128), BF16),
            vmem((SPOTS, RIM, D), BF16),
            vmem((OWN, 10, 24, D), F32),
            vmem((OWN * CELLS, 9 * D), BF16),
            vmem((OWN * CELLS, D), BF16),
            vmem((SPOTS, CELLS, D), BF16),
            vmem((SPOTS * CELLS, 2 * D), BF16),
            vmem((OWN * CELLS, D), BF16),
            vmem((PART * 9 * CELLS, 2 * D), BF16),
            vmem((OWN * CELLS, D), BF16),
            vmem((COLS, CHAN, ROWS, 16, D), BF16),
            *[vmem(w.shape, BF16) for w in weights],
            dma((7,)),
            dma((HELD * CHAN,)),
            dma((GROUP * CHAN * COLS,)),
            dma((moves,)),
            dma((moves,)),
            dma((moves,)),
            dma((moves,)),
            dma((GROUP * CHAN * OWN // PART,)),
            dma((HELD * CHAN * ROWS // PART,)),
            dma((COLS + OWN // PART,)),
        ],
        compiler_params=pltpu.CompilerParams(
            collective_id=0, has_side_effects=True, vmem_limit_bytes=60 << 20
        ),
        name="encoder_block",
    )(
        owner,
        cell_mask.T,
        neighbours.T,
        rotations.T,
        latents.reshape(HELD, FACE, 16, D),
        gain_image,
        gain_attn,
        gain_mlp,
        *weights,
    )
    out = pl.pallas_call(
        settle_kernel,
        out_shape=jax.ShapeDtypeStruct((HELD, FACE, 16, D), BF16),
        in_specs=[SMEM, HBM],
        out_specs=HBM,
        scratch_shapes=[
            vmem((HELD, FACE, 16, D), BF16),
            vmem((FACE, 16, D), BF16),
            dma((HELD,)),
            dma((HELD,)),
        ],
        name="settle",
    )(where, home.reshape(HELD, FACE, 16, D))
    return out.reshape(SLOTS, 16, D)


def solution(mesh):
    in_specs = (
        P("tiles", "chan", None),
        P(),
        P("tiles", None),
        P("tiles", None),
        P("tiles", "chan"),
        P(),
        P(),
        P(),
        P(),
        P(),
        P(),
        P(),
        P(),
    )
    return jax.shard_map(
        per_device,
        mesh=mesh,
        in_specs=in_specs,
        out_specs=P("tiles", "chan", None),
        check_vma=False,
    )
```

```python
import math

import jax
import jax.numpy as jnp
from jax import lax
from jax.experimental import pallas as pl
from jax.experimental.pallas import tpu as pltpu
from jax.sharding import PartitionSpec as P

MESH = pl.DeviceIdType.MESH
VMEM = pl.BlockSpec(memory_space=pltpu.VMEM)
SMEM = pl.BlockSpec(memory_space=pltpu.SMEM)
HBM = pl.BlockSpec(memory_space=pltpu.HBM)
F32, BF16 = jnp.float32, jnp.bfloat16

D = 384
FFN_UNITS = 1536
HEAD_DIM = 64
FACE = 16
BAND = 64
SIDE = 8
CELLS = 64
SLOTS = 80
HELD = 5
GROUP = 4
CHAN = 4
COLS = 2
ROWS = 4
OWN = COLS * ROWS
GRID_R, GRID_C = ROWS + 2, COLS + 2
SPOTS = GRID_R * GRID_C
HALF = ROWS * CELLS
PART = 2
RIM = 32
PIECE = ROWS * 3 + 1
epsilon = 1e-06


def rms(wide, gain):
    return wide * lax.rsqrt(jnp.mean(wide * wide, axis=-1, keepdims=True) + epsilon) * gain


def snake(q):
    return q // 2 * 2 + lax.rem(q + q // 2, 2)


def device_of(worker):
    base = worker // GROUP * GROUP
    return base + snake(worker - base)


def remote(src, dst, send, recv, device):
    return pltpu.make_async_remote_copy(
        src_ref=src, dst_ref=dst, send_sem=send, recv_sem=recv, device_id=device, device_id_type=MESH
    )


def neighbour_places(near, start, count):
    slot = lax.broadcasted_iota(jnp.int32, near.shape, 1)
    base = jnp.where(
        near < SLOTS,
        start,
        jnp.where(near < SLOTS + FACE, start - FACE - SLOTS, start + count - SLOTS - FACE),
    )
    tile = (near + base) & (FACE * BAND - 1)
    own_col = (start + slot) >> 4
    grid_row = (tile & 15) - (slot & 12) + 1
    grid_col = ((tile >> 4) - (own_col - (own_col & 1)) + 1) & (BAND - 1)
    grid_row = jnp.minimum(jnp.maximum(grid_row, 0), GRID_R - 1)
    grid_col = jnp.minimum(jnp.maximum(grid_col, 0), GRID_C - 1)
    return jnp.where(near < SLOTS + 2 * FACE, grid_col * GRID_R + grid_row, SPOTS)


def rim_wanted(near, turns):
    q = lax.broadcasted_iota(jnp.int32, (48, 128), 0)

    def pick(*values):
        found = values[7]
        for at, top in ((6, 35), (5, 34), (4, 33), (3, 32), (2, 24), (1, 16), (0, 8)):
            found = jnp.where(q < top, values[at], found)
        return found

    along = q & 7
    order = (1, 6, 3, 4, 0, 2, 5, 7)
    place = pick(*[near[n : n + 1] for n in order])
    turn = pick(*[turns[n : n + 1] for n in order])
    i = pick(7, 0, along, along, 7, 7, 0, 0)
    j = pick(along, along, 7, 0, 7, 0, 7, 0)

    def turned(a, b, c, d):
        return jnp.where(turn < 0.5, a, jnp.where(turn < 1.5, b, jnp.where(turn < 2.5, c, d)))

    from_row = turned(i, j, 7 - i, 7 - j)
    from_col = turned(j, 7 - i, 7 - j, i)
    rim = jnp.where(
        from_row == 0,
        from_col,
        jnp.where(from_row == 7, 8 + from_col, jnp.where(from_col == 0, 16 + from_row, 24 + from_row)),
    )
    return jnp.where(q < 36, place * RIM + rim.astype(F32), float(SPOTS * RIM))


def halo_moves(device, chan, base, rank):
    worker = base + snake(rank)
    total = lax.axis_size("tiles")
    left = device_of(lax.rem(worker + total - 1, total))
    right = device_of(lax.rem(worker + 1, total))
    up, down = chan > 0, chan < CHAN - 1
    above, below = lax.rem(chan + CHAN - 1, CHAN), lax.rem(chan + 1, CHAN)
    first, second, third = GRID_R, 2 * GRID_R, 3 * GRID_R
    last = ROWS - PART
    moves = [
        (first + 1, third + 1, PART, (0, 0), (left, chan), None, None),
        (second + 1, 1, PART, (1, 0), (right, chan), None, None),
        (first + 1 + last, third + 1 + last, PART, (0, last), (left, chan), None, None),
        (second + 1 + last, 1 + last, PART, (1, last), (right, chan), None, None),
        (first + 1, third + ROWS + 1, 1, (0, 0), (left, above), up, down),
        (first + ROWS, third, 1, (0, last), (left, below), down, up),
        (first + 1, first + ROWS + 1, 1, (0, 0), (device, above), up, down),
        (first + ROWS, first, 1, (0, last), (device, below), down, up),
        (second + 1, ROWS + 1, 1, (1, 0), (right, above), up, down),
        (second + ROWS, 0, 1, (1, last), (right, below), down, up),
        (second + 1, second + ROWS + 1, 1, (1, 0), (device, above), up, down),
        (second + ROWS, second, 1, (1, last), (device, below), down, up),
    ]
    moves = moves[4:] + moves[:4]
    return moves, (left, right, above, below)


def when(condition, action):
    if condition is None:
        action()
    else:
        pl.when(condition)(action)


def block_kernel(
    owner_hbm,
    mask_in,
    near_in,
    turn_in,
    latents,
    gain_image,
    gain_attn,
    gain_mlp,
    conv_hbm,
    qkv_hbm,
    proj_hbm,
    up_hbm,
    down_hbm,
    home,
    where,
    owner,
    raw,
    held,
    payload,
    got_first,
    got_second,
    own,
    normed,
    marks,
    rims,
    frame,
    patches,
    after,
    table,
    memory,
    queries,
    keys,
    mixed,
    tiles,
    conv,
    qkv,
    proj,
    up,
    down,
    load_sem,
    spread_send,
    spread_recv,
    rim_send,
    rim_recv,
    halo_send,
    halo_recv,
    home_send,
    home_recv,
    local,
):
    device, chan = lax.axis_index("tiles"), lax.axis_index("chan")
    rank = lax.rem(device, GROUP)
    base = device - rank
    place = snake(rank)
    moves, (left, right, above, below) = halo_moves(device, chan, base, rank)

    got = (got_first, got_second)
    owner_load = pltpu.make_async_copy(owner_hbm, owner, load_sem.at[6])
    owner_load.start()
    first_load = pltpu.make_async_copy(latents, held, load_sem.at[0])
    first_load.start()
    loads = []
    for at, (src, dst) in enumerate(
        [(conv_hbm, conv), (qkv_hbm, qkv), (proj_hbm, proj), (up_hbm, up), (down_hbm, down)]
    ):
        loads.append(pltpu.make_async_copy(src, dst, load_sem.at[1 + at]))

    barrier = pltpu.get_barrier_semaphore()
    partners = []
    for step in range(1, GROUP * CHAN):
        other = lax.rem(rank * CHAN + chan + step, GROUP * CHAN)
        partners.append((base + other // CHAN, lax.rem(other, CHAN)))
    for side in (left, right):
        partners += [(side, chan), (side, above), (side, below)]
    for partner in partners:
        pl.semaphore_signal(barrier, inc=1, device_id=partner, device_id_type=MESH)

    def count_columns(col, carry):
        start, count = carry
        holder = owner[col * FACE]
        return (
            start + jnp.where(holder < device, 1, 0),
            count + jnp.where(holder == device, 1, 0),
        )

    owner_load.wait()
    start, count = lax.fori_loop(0, BAND, count_columns, (jnp.int32(0), jnp.int32(0)))
    limit = lambda value, top: jnp.minimum(jnp.maximum(value, 0), top)
    shift = limit(start - base * COLS - rank, HELD - 1)
    where[0], where[1] = shift, count
    sources = [
        limit(owner[((base + place) * COLS + col) * FACE] - base, GROUP - 1) for col in range(COLS)
    ]

    raw[...] = jnp.zeros_like(raw)
    raw[0:16, 0:SLOTS] = mask_in[...]
    raw[16:24, 0:SLOTS] = near_in[...]
    raw[24:32, 0:SLOTS] = turn_in[...]
    lane = lax.broadcasted_iota(jnp.int32, (16, 128), 1)
    mask_rows = raw[0:16].astype(F32)
    near_rows = neighbour_places(raw[16:24], start * FACE, count * FACE).astype(F32)
    near_rows = jnp.concatenate([near_rows, raw[24:32].astype(F32)], axis=0)
    for i in range(HELD):
        cells = pltpu.roll(mask_rows, (128 - i * FACE) % 128, axis=1)
        near = pltpu.roll(near_rows, (128 + FACE - i * FACE) % 128, axis=1)
        marks[i] = jnp.where(lane < FACE, cells, near).astype(BF16)
    first_load.wait()

    def fill(i):
        col = lax.rem(i + HELD - shift, HELD)
        for c in range(CHAN):
            for r in range(ROWS):
                for part in range(3):
                    payload[i, c, r * 3 + part] = held[col, c * ROWS + r, :, part * 128 : (part + 1) * 128]
            payload[i, c, PIECE - 1] = marks[col]

    sent = []
    for step in range(HELD):
        i = lax.rem(2 * step + lax.rem(rank, 2), HELD)
        fill(i)
        if step == 0:
            pl.semaphore_wait(barrier, len(partners))
        target = snake((rank + i) // COLS)
        odd = lax.rem(rank, 2) == 1
        for c in (2, 3, 1, 0):
            to = lax.rem(chan + c, CHAN)
            away = None if c else target != rank
            for col in range(COLS):
                if step == 2:
                    needed = odd if col else jnp.logical_not(odd)
                    needed = needed if away is None else needed & away
                elif (step > 2) == (col == 1):
                    needed = away
                else:
                    continue
                copy = remote(
                    payload.at[i, to],
                    got[col].at[rank, chan],
                    spread_send.at[step * CHAN + c],
                    spread_recv.at[(rank * CHAN + chan) * COLS + col],
                    (base + target, to),
                )
                when(needed, copy.start)
                sent.append((copy, needed))
    stays = []
    for col in range(COLS):
        i = place * COLS + col - rank
        copy = pltpu.make_async_copy(
            payload.at[limit(i, HELD - 1), chan], got[col].at[rank, chan], local.at[col]
        )
        inside = (i >= 0) & (i < HELD)
        when(inside, copy.start)
        stays.append((copy, inside))
    for load in loads:
        load.start()
    beyond = jnp.zeros((RIM, D), BF16)
    for col in range(GRID_C):

        @pl.when(chan == 0)
        def _():
            rims[col * GRID_R] = beyond
            for part in range(2):
                table[col * GRID_R, part * RIM : (part + 1) * RIM] = beyond

        @pl.when(chan == CHAN - 1)
        def _():
            rims[(col + 1) * GRID_R - 1] = beyond
            for part in range(2):
                table[(col + 1) * GRID_R - 1, part * RIM : (part + 1) * RIM] = beyond

    def exchange(buffer, send, recv, kind, which):
        for at, (src, dst, many, ready, to, needed, _) in enumerate(moves):
            if ready[kind] == which:
                copy = remote(
                    buffer.at[pl.ds(src, many)], buffer.at[pl.ds(dst, many)], send.at[at], recv.at[at], to
                )
                when(needed, copy.start)

    def arrived(buffer, send, recv, first=0, end=SPOTS):
        for at, (src, dst, many, _, to, needed, coming) in enumerate(moves):
            if first <= dst < end:
                copy = remote(
                    buffer.at[pl.ds(src, many)], buffer.at[pl.ds(dst, many)], send.at[at], recv.at[at], to
                )
                when(coming, copy.wait_recv)

    def departed(buffer, send, recv):
        for at, (src, dst, many, _, to, needed, _) in enumerate(moves):
            copy = remote(
                buffer.at[pl.ds(src, many)], buffer.at[pl.ds(dst, many)], send.at[at], recv.at[at], to
            )
            when(needed, copy.wait_send)

    def pieces_in(col):
        for step in range(GROUP):
            source = lax.rem(rank + step, GROUP)
            far = place * COLS + col - source
            for c in range(CHAN):
                at = lax.rem(chan + c, CHAN)
                if step == 0 and c == 0:
                    when(stays[col][1], stays[col][0].wait)
                else:
                    arrival = remote(
                        payload.at[0, 0],
                        got[col].at[source, at],
                        spread_send.at[0],
                        spread_recv.at[(source * CHAN + at) * COLS + col],
                        (device, at),
                    )
                    when((far >= 0) & (far < HELD), arrival.wait_recv)

    row = lax.broadcasted_iota(jnp.int32, (RIM, CELLS), 0)
    cell = lax.broadcasted_iota(jnp.int32, (RIM, CELLS), 1)
    edge, along = row >> 3, row & 7
    at_rim = jnp.where(
        edge == 0, along, jnp.where(edge == 1, 56 + along, jnp.where(edge == 2, along * 8, along * 8 + 7))
    )
    at_rim = jnp.where(cell == at_rim, 1.0, 0.0).astype(BF16)
    gain_of = lambda gain: gain[...].reshape(1, D)
    wide_lane = lax.broadcasted_iota(jnp.int32, (48, 128), 1)
    masks = []
    wanted = []
    for col in range(COLS):
        pieces_in(col)
        blocks = [got[col][sources[col], c, PIECE - 1].astype(F32) for c in range(CHAN)]
        all_wanted = rim_wanted(blocks[0][0:8], blocks[0][8:16])
        for r in range(ROWS):
            slot = chan * ROWS + r
            wanted.append(
                jnp.sum(jnp.where(wide_lane == slot + FACE, all_wanted, 0.0), axis=1, keepdims=True)
            )
            pieces, column = [], []
            for c in range(CHAN):
                pieces.append(
                    jnp.concatenate([got[col][sources[col], c, r * 3 + part] for part in range(3)], axis=1)
                )
                column.append(jnp.sum(jnp.where(lane == slot, blocks[c], 0.0), axis=1, keepdims=True))
            values = jnp.concatenate(pieces, axis=0)
            mask = jnp.concatenate(column, axis=0)
            masks.append(mask)
            tile = col * ROWS + r
            own[tile * CELLS : (tile + 1) * CELLS] = values
            norm = (rms(values.astype(F32), gain_of(gain_image)) * mask).astype(BF16)
            normed[tile] = norm
            rims[(1 + col) * GRID_R + 1 + r] = jnp.dot(at_rim, norm, preferred_element_type=F32).astype(BF16)
        exchange(rims, rim_send, rim_recv, 0, col)
        for tile in range(col * ROWS, (col + 1) * ROWS):
            frame[tile, 1:9, 8:16, :] = normed[tile].astype(F32).reshape(SIDE, SIDE, D)

    loads[0].wait()
    arrived(rims, rim_send, rim_recv)

    rim_lane = lax.broadcasted_iota(jnp.int32, (48, SPOTS * RIM), 1).astype(F32)
    for part in range(0, ROWS, PART):
        for col in range(COLS):
            for r in range(part, part + PART):
                tile = col * ROWS + r
                at = part * COLS + col * PART + r - part
                chosen = jnp.where(rim_lane == wanted[tile], 1.0, 0.0).astype(BF16)
                rim = jnp.dot(chosen, rims[...].reshape(SPOTS * RIM, D), preferred_element_type=F32)
                frame[tile, 0, 8:16, :] = rim[0:8]
                frame[tile, 9, 8:16, :] = rim[8:16]
                for i in range(SIDE):
                    frame[tile, 1 + i, 7:8, :] = rim[16 + i : 17 + i]
                    frame[tile, 1 + i, 16:17, :] = rim[24 + i : 25 + i]
                frame[tile, 0, 7:8, :] = rim[32:33]
                frame[tile, 0, 16:17, :] = rim[33:34]
                frame[tile, 9, 7:8, :] = rim[34:35]
                frame[tile, 9, 16:17, :] = rim[35:36]
                for tap in range(9):
                    dr, dc = tap // 3, tap % 3
                    window = frame[tile, dr : dr + SIDE, 7 + dc : 7 + dc + SIDE, :]
                    patches[at * CELLS : (at + 1) * CELLS, tap * D : (tap + 1) * D] = window.reshape(
                        CELLS, D
                    ).astype(BF16)
        total = jnp.dot(
            patches[part * COLS * CELLS : (part + PART) * COLS * CELLS, :], conv[...], preferred_element_type=F32
        )
        for col in range(COLS):
            tile = col * ROWS + part
            rows = slice(tile * CELLS, (tile + PART) * CELLS)
            mine = total[col * PART * CELLS : (col + 1) * PART * CELLS]
            image = (own[rows, :].astype(F32) + mine).astype(BF16)
            after[rows, :] = image
            mask = jnp.concatenate(masks[tile : tile + PART], axis=0)
            attn = (rms(image.astype(F32), gain_of(gain_attn)) * mask).astype(BF16)
            spot = (1 + col) * GRID_R + 1 + part
            table[spot : spot + PART] = attn.reshape(PART, CELLS, D)
        exchange(table, halo_send, halo_recv, 1, part)

    def project(*spans):
        rows = jnp.concatenate(
            [table[spot : spot + many].reshape(many * CELLS, D) for spot, many in spans], axis=0
        )
        found = jnp.dot(rows, qkv[:, D:], preferred_element_type=F32).astype(BF16)
        at = 0
        for spot, many in spans:
            memory[spot * CELLS : (spot + many) * CELLS, :] = found[at : at + many * CELLS]
            at += many * CELLS

    loads[1].wait()
    scale = 1.0 / math.sqrt(HEAD_DIM)
    for col in range(COLS):
        spot = (1 + col) * GRID_R + 1
        found = jnp.dot(
            table[spot : spot + ROWS].reshape(HALF, D), qkv[:, :D], preferred_element_type=F32
        )
        queries[col * HALF : (col + 1) * HALF, :] = (found * scale).astype(BF16)
        project((spot, ROWS))
    for load in loads[2:]:
        load.wait()
    far = 3 * GRID_R
    arrived(table, halo_send, halo_recv, 0, far)
    project((0, GRID_R + 1), (GRID_R + ROWS + 1, 2), (2 * GRID_R + ROWS + 1, 1))

    def heads_step(rows, first, lanes, base):
        heads = lanes // HEAD_DIM
        head = lax.broadcasted_iota(jnp.int32, (CELLS, lanes), 1) >> 6
        query = queries[rows, first : first + lanes]
        nothing = jnp.zeros_like(query)
        blocks = jnp.concatenate([jnp.where(head == h, query, nothing) for h in range(heads)], axis=0)
        spots = slice(base, base + 9 * CELLS)
        scores = lax.dot_general(
            blocks, keys[spots, first : first + lanes], (((1,), (1,)), ((), ())), preferred_element_type=F32
        )
        weights = jnp.exp(scores - jnp.max(scores, axis=-1, keepdims=True))
        total = jnp.sum(weights, axis=-1, keepdims=True)
        value = jnp.dot(
            weights.astype(BF16), keys[spots, D + first : D + first + lanes], preferred_element_type=F32
        )
        value = value / total
        found = value[:CELLS]
        for h in range(1, heads):
            found = jnp.where(head == h, value[h * CELLS : (h + 1) * CELLS], found)
        mixed[rows, first : first + lanes] = found.astype(BF16)

    returned = []
    for col in range(COLS):

        def attend(r):
            base_key = r % PART * 9 * CELLS
            for n in range(3):
                spot = (col + n) * GRID_R + r
                keys[base_key + n * 3 * CELLS : base_key + (n + 1) * 3 * CELLS, :] = memory[
                    spot * CELLS : (spot + 3) * CELLS, :
                ]
            rows = slice((col * ROWS + r) * CELLS, (col * ROWS + r + 1) * CELLS)
            heads_step(rows, 0, 4 * HEAD_DIM, base_key)
            heads_step(rows, 4 * HEAD_DIM, 2 * HEAD_DIM, base_key)

        if col == 1:
            arrived(table, halo_send, halo_recv, far, SPOTS)
            project((far, GRID_R))
        for part in range(0, ROWS, PART):
            for r in range(part, part + PART):
                attend(r)
            rows = slice(col * HALF + part * CELLS, col * HALF + (part + PART) * CELLS)
            attended = jnp.dot(mixed[rows, :], proj[...], preferred_element_type=F32)
            attended = (after[rows, :].astype(F32) + attended).astype(BF16)
            wide = attended.astype(F32)
            hidden = jnp.dot(rms(wide, gain_of(gain_mlp)).astype(BF16), up[...], preferred_element_type=F32)
            hidden = (0.5 * hidden * (1.0 + lax.erf(hidden * (0.5**0.5)))).astype(BF16)
            encoded = wide + jnp.dot(hidden, down[...], preferred_element_type=F32)
            encoded = encoded.astype(BF16).reshape(PART, CHAN, 16, D)
            for r in range(PART):
                for c in range(CHAN):
                    tiles[col, c, part + r] = encoded[r, c]
            span = pl.ds(part, PART)
            for c in (2, 3, 1, 0):
                to = lax.rem(chan + c, CHAN)
                for step in range(GROUP):
                    target = lax.rem(rank + step, GROUP)
                    i = place * COLS + col - target
                    slot = limit(i, HELD - 1)
                    inside = (i >= 0) & (i < HELD)
                    if c == 0 and step == 0:
                        copy = pltpu.make_async_copy(
                            tiles.at[col, chan, span],
                            home.at[slot, chan, span],
                            local.at[COLS + (col * ROWS + part) // PART],
                        )
                    else:
                        copy = remote(
                            tiles.at[col, to, span],
                            home.at[slot, chan, span],
                            home_send.at[len(returned)],
                            home_recv.at[(slot * CHAN + chan) * (ROWS // PART) + part // PART],
                            (base + target, to),
                        )
                    when(inside, copy.start)
                    returned.append((copy, inside, c == 0 and step == 0))

    departed(rims, rim_send, rim_recv)
    departed(table, halo_send, halo_recv)
    for copy, needed in sent:
        when(needed, copy.wait_send)
    for copy, inside, stays_here in returned:
        when(inside, copy.wait if stays_here else copy.wait_send)
    for i in range(HELD):
        worker = snake((rank + i) // COLS)
        for c in range(CHAN):
            at = lax.rem(chan + c, CHAN)
            for part in range(0, ROWS, PART):
                span = pl.ds(part, PART)
                arrival = remote(
                    tiles.at[0, 0, span],
                    home.at[i, at, span],
                    home_send.at[0],
                    home_recv.at[(i * CHAN + at) * (ROWS // PART) + part // PART],
                    (device, at),
                )
                when(None if c else worker != rank, arrival.wait_recv)


def settle_kernel(where, home, out, columns, blank, come, go):
    shift, count = where[0], where[1]

    def fetch(i):
        return pltpu.make_async_copy(home.at[jnp.minimum(i + shift, HELD - 1)], columns.at[i], come.at[i])

    for i in range(HELD):
        pl.when(i < count)(fetch(i).start)
    blank[...] = jnp.zeros_like(blank)
    for i in range(HELD):

        @pl.when(i < count)
        def _():
            fetch(i).wait()
            pltpu.make_async_copy(columns.at[i], out.at[i], go.at[i]).start()

        @pl.when(i >= count)
        def _():
            pltpu.make_async_copy(blank, out.at[i], go.at[i]).start()

    for i in range(HELD):
        pltpu.make_async_copy(blank, out.at[i], go.at[i]).wait()


def per_device(
    latents,
    owner,
    neighbours,
    rotations,
    cell_mask,
    gain_image,
    conv_weight,
    gain_attn,
    qkv_weight,
    out_weight,
    gain_mlp,
    up_weight,
    down_weight,
):
    weights = [conv_weight, qkv_weight, out_weight, up_weight, down_weight]
    vmem = pltpu.VMEM
    dma = pltpu.SemaphoreType.DMA
    moves = 8 + 2 * COLS
    home, where = pl.pallas_call(
        block_kernel,
        out_shape=(
            jax.ShapeDtypeStruct((HELD, CHAN, ROWS, 16, D), BF16),
            jax.ShapeDtypeStruct((2,), jnp.int32),
        ),
        in_specs=[HBM] + [VMEM] * 3 + [HBM] + [VMEM] * 3 + [HBM] * 5,
        out_specs=(HBM, SMEM),
        scratch_shapes=[
            pltpu.SMEM((FACE * BAND,), jnp.int32),
            vmem((32, 128), jnp.int32),
            vmem((HELD, FACE, 16, D), BF16),
            vmem((HELD, CHAN, PIECE, 16, 128), BF16),
            vmem((GROUP, CHAN, PIECE, 16, 128), BF16),
            vmem((GROUP, CHAN, PIECE, 16, 128), BF16),
            vmem((OWN * CELLS, D), BF16),
            vmem((OWN, CELLS, D), BF16),
            vmem((HELD, FACE, 128), BF16),
            vmem((SPOTS, RIM, D), BF16),
            vmem((OWN, 10, 24, D), F32),
            vmem((OWN * CELLS, 9 * D), BF16),
            vmem((OWN * CELLS, D), BF16),
            vmem((SPOTS, CELLS, D), BF16),
            vmem((SPOTS * CELLS, 2 * D), BF16),
            vmem((OWN * CELLS, D), BF16),
            vmem((PART * 9 * CELLS, 2 * D), BF16),
            vmem((OWN * CELLS, D), BF16),
            vmem((COLS, CHAN, ROWS, 16, D), BF16),
            *[vmem(w.shape, BF16) for w in weights],
            dma((7,)),
            dma((HELD * CHAN,)),
            dma((GROUP * CHAN * COLS,)),
            dma((moves,)),
            dma((moves,)),
            dma((moves,)),
            dma((moves,)),
            dma((GROUP * CHAN * OWN // PART,)),
            dma((HELD * CHAN * ROWS // PART,)),
            dma((COLS + OWN // PART,)),
        ],
        compiler_params=pltpu.CompilerParams(
            collective_id=0, has_side_effects=True, vmem_limit_bytes=60 << 20
        ),
        name="encoder_block",
    )(
        owner,
        cell_mask.T,
        neighbours.T,
        rotations.T,
        latents.reshape(HELD, FACE, 16, D),
        gain_image,
        gain_attn,
        gain_mlp,
        *weights,
    )
    out = pl.pallas_call(
        settle_kernel,
        out_shape=jax.ShapeDtypeStruct((HELD, FACE, 16, D), BF16),
        in_specs=[SMEM, HBM],
        out_specs=HBM,
        scratch_shapes=[
            vmem((HELD, FACE, 16, D), BF16),
            vmem((FACE, 16, D), BF16),
            dma((HELD,)),
            dma((HELD,)),
        ],
        name="settle",
    )(where, home.reshape(HELD, FACE, 16, D))
    return out.reshape(SLOTS, 16, D)


def solution(mesh):
    in_specs = (
        P("tiles", "chan", None),
        P(),
        P("tiles", None),
        P("tiles", None),
        P("tiles", "chan"),
        P(),
        P(),
        P(),
        P(),
        P(),
        P(),
        P(),
        P(),
    )
    return jax.shard_map(
        per_device,
        mesh=mesh,
        in_specs=in_specs,
        out_specs=P("tiles", "chan", None),
        check_vma=False,
    )
```
